32 devices in a mesh: dp: 8 (over y, x, core), tensor: 4 (over z).
Axes of the slice: x: 2, y: 2, z: 4, core: 2. Of those that a mesh axis runs over, the one named last changes fastest.
Arguments:
- layer_input: bfloat16 [8192, 768], P(('dp', 'tensor')), may hold values from -12 to 12
- attn_gain: float32 [768], replicated, may hold values from 0.5 to 1.5
- query_weight: bfloat16 [768, 768], P(None, 'tensor'), may hold values from -0.21875 to 0.21875
- key_weight: bfloat16 [768, 768], P(None, 'tensor'), may hold values from -0.21875 to 0.21875
- value_weight: bfloat16 [768, 768], P(None, 'tensor'), may hold values from -0.21875 to 0.21875
- out_weight: bfloat16 [768, 768], P('tensor'), may hold values from -3 to 3
- moe_gain: float32 [768], replicated, may hold values from 0.5 to 1.5
- router_weight: float32 [768, 12], replicated, may hold values from -0.109375 to 0.109375
- gate_residual: float32 [8192, 12], P('dp'), may hold values from -3 to 3
- const_gate: float32 [2, 768, 2], replicated, may hold values from -0.21875 to 0.21875
- const_value: float32 [2, 768], replicated, may hold values from -6 to 6
- gate_weight: bfloat16 [8, 768, 2048], P(None, None, 'tensor'), may hold values from -0.21875 to 0.21875
- up_weight: bfloat16 [8, 768, 2048], P(None, None, 'tensor'), may hold values from -0.21875 to 0.21875
- down_weight: bfloat16 [8, 2048, 768], P(None, 'tensor'), may hold values from -0.75 to 0.75
- routes: int32 [8192, 2], P('dp'), may hold values from 0 to 11, all different within a row; in each aligned block of 1024 rows (0 to 1023, 1024 to 2047, ...) at most 256 rows name the same one
- grad_out: bfloat16 [8192, 768], P(('dp', 'tensor')), may hold values from -12 to 12
Outputs:
- output: bfloat16 [8192, 768], P(('dp', 'tensor'))
- input_grad: bfloat16 [8192, 768], P(('dp', 'tensor'))
- attn_gain_grad: float32 [768], replicated
- query_grad: float32 [768, 768], P('dp', 'tensor')
- key_grad: float32 [768, 768], P('dp', 'tensor')
- value_grad: float32 [768, 768], P('dp', 'tensor')
- out_grad: float32 [768, 768], P('tensor', 'dp')
- moe_gain_grad: float32 [768], replicated
- router_grad: float32 [768, 12], replicated
- const_gate_grad: float32 [2, 768, 2], replicated
- const_value_grad: float32 [2, 768], replicated
- gate_grad: float32 [8, 768, 2048], P(None, 'dp', 'tensor')
- up_grad: float32 [8, 768, 2048], P(None, 'dp', 'tensor')
- down_grad: float32 [8, 2048, 768], P(None, 'tensor', 'dp')
The draws below stay inside these ranges and needn't reach their ends.
Inputs may be any that keep to these rules, and one draw needn't show every extreme that they name: `routes`: in each aligned block of 1024 rows (the tokens of one index of dp) every expert number is named by at most 256 rows, a bound that some block reaches; the two numbers of a row differ.
All inputs are finite; a program needn't handle non-finite values.
Results may differ from the reference program's by a relative error of at most 0.024.
Values may be sent and summed in bfloat16 or wider, within the bound.
A program may use at most 256 MiB of HBM per device.

```python
import math
import jax
import jax.numpy as jnp
import numpy as np
from jax import lax

D = 768
H = 12
HD = 64
HID = 2048
EXPERTS = 8
LENGTH = 1024
BLOCK = 256
NE = 12
GROUP = 1024
CAP = 256
TOKENS = 8192
N_DP = 8


def raised(drawn, rng, source, target, shards_of, factor):
    def block_of(axis_at):
        return (jnp.arange(drawn.shape[axis_at]) // (drawn.shape[axis_at] // shards_of)).reshape((-1,) + (1,) * (drawn.ndim - 1 - axis_at))

    one_side = jax.random.permutation(rng, shards_of)[block_of(target)]
    second = (block_of(target) + shards_of // 2) % shards_of
    return jnp.where((block_of(source) == one_side) | (block_of(source) == second), factor * drawn, drawn)


def levels(stream_key, dims, cuts, least, high):
    level = 1.0
    for dim, blocks in cuts:
        steps = jax.random.uniform(jax.random.fold_in(jax.random.fold_in(stream_key, 6), dim), (blocks,), jnp.float32, least / len(cuts), high / len(cuts))
        level = level * jnp.repeat(jnp.exp(steps), dims[dim] // blocks).reshape((-1,) + (1,) * (len(dims) - 1 - dim))
    return level


def shared_out(own_key, own, number, rows, count, top, bound, skew):
    sequence = jax.random.permutation(own_key, count)
    crowded, common = shares(count, rows * top, bound, skew, True), shares(count, rows * top, bound, skew, False)
    places = jnp.arange(count)

    def named(sizes, turn):
        used = int((sizes > 0).sum())
        fixed = max(1, used // 4)
        passed = fixed + (places - fixed + turn * (used - fixed)) % max(1, count - fixed)
        return jnp.zeros((count,), jnp.int32).at[sequence[jnp.where(places < fixed, places, passed)]].set(jnp.asarray(sizes, jnp.int32))

    sizes = jnp.where(number % 4 == 0, named(crowded, number // 4), named(common, number - number // 4 - 1))
    mixed = jax.random.permutation(jax.random.fold_in(own, 3), count)
    giver, taker = mixed[0:count // 2 * 2:2], mixed[1:count // 2 * 2:2]
    margin = jnp.minimum(sizes[giver] - 1, bound - sizes[taker]) // 2
    margin = jnp.where((giver == sequence[0]) | (taker == sequence[0]) | (sizes[taker] == 0), 0, jnp.maximum(margin, 0))
    passed = jax.random.randint(jax.random.fold_in(own, 4), (count // 2,), 0, 1 << 20) % (margin + 1)
    sizes = sizes.at[giver].add(-passed).at[taker].add(passed)
    labels = jnp.searchsorted(jnp.cumsum(sizes), jnp.arange(rows * top), side="right").astype(jnp.int32)
    listing = labels.reshape(top, rows).T
    listing = listing[jax.random.permutation(jax.random.fold_in(own, 1), rows)]
    turn = jax.random.randint(jax.random.fold_in(own, 2), (rows, 1), 0, top)
    return jnp.take_along_axis(listing, (jnp.arange(top)[None, :] + turn) % top, axis=1)


def shares(count, total, most, skew, full):
    weights = [(1 << 20) // math.isqrt(rank ** skew) + 1 for rank in range(1, count + 1)]
    largest = most if full else min(most, max(-(-total // count), total * weights[0] // sum(weights)))
    least = 1 if total - largest >= count - 1 else 0
    counts, spare = [largest] + [least] * (count - 1), total - largest - least * (count - 1)
    while spare > 0:
        movable = [i for i in range(1, count) if counts[i] < largest] or [i for i in range(1, count) if counts[i] < most]
        whole, left = sum([weights[i] for i in movable]), spare
        for i in movable:
            addition = min(most - counts[i], max(1, left * weights[i] // whole), spare)
            counts[i] = counts[i] + addition
            spare = spare - addition
    return np.array(counts)


def scatter_about(rng, shape, deviation, limit, split=(), kind=jnp.bfloat16):
    drawn = jax.random.normal(rng, shape, jnp.float32) * deviation
    if len(split) > 0:
        drawn = levels(rng, shape, split, -0.22, 0.18) * drawn
    return jnp.clip(drawn, min=-limit, max=limit).astype(kind)


def noise_with(key, dims, width, limit, pieces, heavy, kind=jnp.bfloat16):
    values = width * jax.random.normal(key, dims, jnp.float32)
    if pieces:
        values = values * levels(key, dims, pieces, -0.22, 0.18)
    return jnp.clip(raised(values, jax.random.fold_in(key, 3), *heavy), -limit, limit).astype(kind)


def setup_inputs(seed: int = 0) -> dict:
    splits = jax.random.split(jax.random.key(seed), 17)
    layer_input = noise_with(splits[0], (TOKENS, D), 1.0, 12.0, ((0, 32),), (0, 1, 32, 2.75))
    attn_gain = jnp.clip(1.0 + 0.1 * jax.random.normal(splits[1], (D,), jnp.float32), 0.5, 1.5)
    query_weight = scatter_about(splits[2], (D, H * HD), D ** -0.5, 0.21875, ((1, 4),))
    key_weight = scatter_about(splits[3], (D, H * HD), D ** -0.5, 0.21875, ((1, 4),))
    value_weight = scatter_about(splits[4], (D, H * HD), D ** -0.5, 0.21875, ((1, 4),))
    out_weight = scatter_about(splits[5], (H * HD, D), 4 ** -0.5, 3.0, ((0, 4),))
    moe_gain = jnp.clip(1.0 + 0.1 * jax.random.normal(splits[6], (D,), jnp.float32), 0.5, 1.5)
    router_weight = scatter_about(splits[7], (D, NE), (4 * D) ** -0.5, 0.109375, (), jnp.float32)
    gate_residual = scatter_about(splits[8], (TOKENS, NE), 0.5, 3.0, ((0, 8),), jnp.float32)
    const_gate = scatter_about(splits[9], (2, D, 2), D ** -0.5, 0.21875, (), jnp.float32)
    const_value = scatter_about(splits[10], (2, D), 1.0, 6.0, (), jnp.float32)
    gate_weight = scatter_about(splits[11], (EXPERTS, D, HID), D ** -0.5, 0.21875, ((2, 4),))
    up_weight = scatter_about(splits[12], (EXPERTS, D, HID), D ** -0.5, 0.21875, ((2, 4),))
    down_weight = scatter_about(splits[13], (EXPERTS, HID, D), (HID // 32) ** -0.5, 0.75, ((1, 4),))
    routes_keys = jax.random.split(jax.random.fold_in(splits[14], 1), TOKENS // GROUP)
    routes_turns = jax.random.permutation(jax.random.fold_in(splits[14], 3), TOKENS // GROUP)
    routes = jax.vmap(lambda own, number: shared_out(jax.random.fold_in(splits[14], 2), own, number, GROUP, NE, 2, CAP, 1))(routes_keys, routes_turns).reshape((TOKENS, 2))
    grad_out = noise_with(splits[15], (TOKENS, D), 1.0, 12.0, ((0, 32),), (0, 1, 32, 2.75))
    return dict(layer_input=layer_input, attn_gain=attn_gain, query_weight=query_weight, key_weight=key_weight, value_weight=value_weight, out_weight=out_weight, moe_gain=moe_gain, router_weight=router_weight, gate_residual=gate_residual, const_gate=const_gate, const_value=const_value, gate_weight=gate_weight, up_weight=up_weight, down_weight=down_weight, routes=routes, grad_out=grad_out)


EPSILON = 1e-06
MASKED = -1e+30

@jax.custom_vjp
def low(v):
    return lax.optimization_barrier(v.astype(jnp.bfloat16)).astype(jnp.float32)

@jax.custom_vjp
def low_back(v):
    return v

def low_keep(v):
    return (low(v), None)

def low_pass(kept, grad):
    return (grad,)

def back_keep(v):
    return (v, None)

def back_low(kept, grad):
    return (low(grad),)
low.defvjp(low_keep, low_pass)
low_back.defvjp(back_keep, back_low)

def rope_tables(length, head_width):
    position = jnp.arange(length, dtype=jnp.float32)[:, None]
    inverse = jnp.exp(jnp.arange(head_width // 2, dtype=jnp.float32) * (-2.0 * math.log(10000.0) / head_width))
    angle = position * inverse[None, :]
    return (jnp.cos(angle), jnp.sin(angle))

def rotate(values, cosine, sine):
    half_width = values.shape[-1] // 2
    first_half = values[..., :half_width]
    second_half = values[..., half_width:]
    cos_table = cosine[:, None, :]
    sin_table = sine[:, None, :]
    return jnp.concatenate([first_half * cos_table - second_half * sin_table, second_half * cos_table + first_half * sin_table], axis=-1)

def rms_norm(values, gain):
    scale = lax.rsqrt(lax.optimization_barrier(jnp.mean(values * values, axis=-1, keepdims=True)) + EPSILON)
    return values * scale * gain

def block_mask(query_start, query_rows, length):
    query_pos = query_start + jnp.arange(query_rows, dtype=jnp.int32)
    key_pos = jnp.arange(length, dtype=jnp.int32)
    return (key_pos // BLOCK)[None, :] <= (query_pos // BLOCK)[:, None]

def side_experts(norm_values, router_w, mix_weight, const_rows, residual_logits, picks, ffn_count):
    logits = jnp.dot(norm_values, router_w, precision=lax.Precision.HIGHEST) + residual_logits
    soft_probs = jax.nn.softmax(logits, axis=-1)
    chosen = jnp.take_along_axis(soft_probs, picks, axis=1)
    mixing = jax.nn.softmax(jnp.einsum('rd,cdj->rcj', norm_values, mix_weight, precision=lax.Precision.HIGHEST), axis=-1)
    constant = mixing[..., 0:1] * norm_values[:, None, :] + mixing[..., 1:2] * const_rows[None, :, :]
    special = (picks == ffn_count + 1).astype(jnp.float32)[..., None] * norm_values[:, None, :]
    special = special + (picks == ffn_count + 2).astype(jnp.float32)[..., None] * constant[:, 0][:, None, :]
    special = special + (picks == ffn_count + 3).astype(jnp.float32)[..., None] * constant[:, 1][:, None, :]
    return (chosen, lax.optimization_barrier(jnp.sum(chosen[..., None] * special, axis=1)))

def attend_sequence(operands):
    query, key, value = operands
    scores = low_back(jnp.einsum('qhd,khd->hqk', query, key, precision=lax.Precision.HIGHEST) * HD ** (-0.5))
    visible = block_mask(0, LENGTH, LENGTH)
    scores = jnp.where(visible[None], scores, MASKED)
    soft_probs = jax.nn.softmax(scores, axis=-1)
    return jnp.einsum('hqk,khd->qhd', low(soft_probs), value, precision=lax.Precision.HIGHEST)

def forward(layer_rows, attn_gain, query_weight, key_weight, value_weight, out_weight, moe_gain, router_weight, const_gate, const_value, gate_weight, up_weight, down_weight, residual_logits, picks):
    group_rows, model_width = layer_rows.shape
    seq_count = group_rows // LENGTH
    head_count = query_weight.shape[1] // HD
    ffn_count = gate_weight.shape[0]
    route_count = router_weight.shape[1]
    slot_count = ffn_count * CAP
    cosine, sine = rope_tables(LENGTH, HD)
    norm_attn = low(rms_norm(layer_rows, attn_gain))

    def project(weight):
        return low_back(jnp.dot(norm_attn, weight, precision=lax.Precision.HIGHEST)).reshape(seq_count, LENGTH, head_count, HD)
    query = low(rotate(project(query_weight), cosine, sine))
    key = low(rotate(project(key_weight), cosine, sine))
    value = low(project(value_weight))
    mixed = lax.map(jax.checkpoint(attend_sequence), (query, key, value))
    mixed = low(low_back(mixed.reshape(group_rows, head_count * HD)))
    hidden = layer_rows + low_back(jnp.dot(mixed, out_weight, precision=lax.Precision.HIGHEST))
    norm_moe = low(rms_norm(hidden, moe_gain))
    chosen, special_sum = side_experts(norm_moe, router_weight, const_gate, const_value, residual_logits, picks, ffn_count)
    flat_routes = picks.reshape(-1)
    onehot = (flat_routes[:, None] == jnp.arange(route_count, dtype=jnp.int32)[None, :]).astype(jnp.int32)
    earlier = (jnp.cumsum(onehot, axis=0) - onehot).astype(jnp.int32)
    slot_rank = lax.optimization_barrier(jnp.sum(onehot * earlier, axis=1)).astype(jnp.int32)
    is_ffn = flat_routes < ffn_count
    slot_index = jnp.where(is_ffn, flat_routes * CAP + slot_rank, slot_count).astype(jnp.int32)
    pair_rows = jnp.repeat(norm_moe, 2, axis=0) * is_ffn[:, None].astype(norm_moe.dtype)
    expert_in = jnp.zeros((slot_count + 1, model_width), norm_moe.dtype).at[slot_index].add(pair_rows)
    expert_in = expert_in[:slot_count].reshape(ffn_count, CAP, model_width)
    gate_pre = low_back(jnp.einsum('ecd,edf->ecf', expert_in, gate_weight, precision=lax.Precision.HIGHEST))
    up_pre = low_back(jnp.einsum('ecd,edf->ecf', expert_in, up_weight, precision=lax.Precision.HIGHEST))
    active = low(jax.nn.silu(gate_pre) * up_pre)
    expert_out = low_back(jnp.einsum('ecf,efd->ecd', active, down_weight, precision=lax.Precision.HIGHEST))
    padded = jnp.concatenate([expert_out.reshape(slot_count, model_width), jnp.zeros((1, model_width), expert_out.dtype)], axis=0)
    picked = padded[slot_index].reshape(group_rows, 2, model_width)
    return hidden + special_sum + lax.optimization_barrier(jnp.sum(chosen[..., None] * picked, axis=1))

def reference(layer_input, attn_gain, query_weight, key_weight, value_weight, out_weight, moe_gain, router_weight, gate_residual, const_gate, const_value, gate_weight, up_weight, down_weight, routes, grad_out):
    weights = (attn_gain, query_weight.astype(jnp.float32), key_weight.astype(jnp.float32), value_weight.astype(jnp.float32), out_weight.astype(jnp.float32), moe_gain, router_weight, const_gate, const_value, gate_weight.astype(jnp.float32), up_weight.astype(jnp.float32), down_weight.astype(jnp.float32))
    inputs = layer_input.astype(jnp.float32)
    cotangent = grad_out.astype(jnp.float32)

    def one_group(totals, group_index):
        begin = (group_index * GROUP).astype(jnp.int32)
        group_in = lax.dynamic_slice_in_dim(inputs, begin, GROUP, 0)
        group_res = lax.dynamic_slice_in_dim(gate_residual, begin, GROUP, 0)
        group_routes = lax.dynamic_slice_in_dim(routes, begin, GROUP, 0)
        group_cot = lax.dynamic_slice_in_dim(cotangent, begin, GROUP, 0)

        def run(values, *params):
            return forward(values, *params, group_res, group_routes)
        result, pull = jax.vjp(run, group_in, *weights)
        grads = pull(group_cot)
        totals = tuple((total + grad for total, grad in zip(totals, grads[1:])))
        return (totals, (result.astype(jnp.bfloat16), grads[0].astype(jnp.bfloat16)))
    initial = tuple((jnp.zeros_like(weight) for weight in weights))
    totals, (results, input_grads) = lax.scan(one_group, initial, jnp.arange(N_DP, dtype=jnp.int32))
    return (results.reshape(TOKENS, D), input_grads.reshape(TOKENS, D), totals[0], totals[1], totals[2], totals[3], totals[4], totals[5], totals[6], totals[7], totals[8], totals[9], totals[10], totals[11])
```

```python
import functools
import math

import jax
import jax.numpy as jnp
from jax import lax
from jax.experimental import pallas as pl
from jax.experimental.pallas import tpu as pltpu
from jax.sharding import PartitionSpec as P

HD = 64
LENGTH = 1024
BLOCK = 256
CAP = 256


EPSILON = 1e-06
MASKED = -1e30


def rope_tables(length, head_width):
    position = jnp.arange(length, dtype=jnp.float32)[:, None]
    inverse = jnp.exp(
        jnp.arange(head_width // 2, dtype=jnp.float32) * (-2.0 * math.log(10000.0) / head_width)
    )
    angle = position * inverse[None, :]
    return (jnp.cos(angle), jnp.sin(angle))


def rotate(values, cosine, sine):
    half_width = values.shape[-1] // 2
    first_half = values[..., :half_width]
    second_half = values[..., half_width:]
    cos_table = cosine[:, None, :]
    sin_table = sine[:, None, :]
    return jnp.concatenate(
        [
            first_half * cos_table - second_half * sin_table,
            second_half * cos_table + first_half * sin_table,
        ],
        axis=-1,
    )


def unrotate(values, cosine, sine):
    half_width = values.shape[-1] // 2
    first_half = values[..., :half_width]
    second_half = values[..., half_width:]
    cos_table = cosine[:, None, :]
    sin_table = sine[:, None, :]
    return jnp.concatenate(
        [
            first_half * cos_table + second_half * sin_table,
            second_half * cos_table - first_half * sin_table,
        ],
        axis=-1,
    )


def rms_norm(values, gain):
    scale = lax.rsqrt(jnp.mean(values * values, axis=-1, keepdims=True) + EPSILON)
    return values * scale * gain


def block_mask(query_start, query_rows, length):
    query_pos = query_start + jnp.arange(query_rows, dtype=jnp.int32)
    key_pos = jnp.arange(length, dtype=jnp.int32)
    return (key_pos // BLOCK)[None, :] <= (query_pos // BLOCK)[:, None]


def pad_router(router_weight, const_gate):
    gates = jnp.transpose(const_gate, (1, 0, 2)).reshape(const_gate.shape[1], -1)
    return jnp.concatenate([router_weight, gates], axis=1)


def side_experts(norm, named, weights, residual, const_value, ffn_count):
    route_count = named.shape[1]
    both = jnp.dot(norm, weights, precision=lax.Precision.HIGHEST)
    logits = both[:, :route_count] + residual
    probs = jax.nn.softmax(logits, axis=-1)
    mix = both[:, route_count:].reshape(norm.shape[0], 2, 2)
    share = jax.nn.sigmoid(mix[:, :, 0] - mix[:, :, 1])
    chosen = probs * named
    return probs, share, chosen


def side_sum(norm, share, chosen, const_value, ffn_count):
    c9 = chosen[:, ffn_count + 1 : ffn_count + 2]
    c10 = chosen[:, ffn_count + 2 : ffn_count + 4]
    keep = c9 + jnp.sum(c10 * share, axis=1, keepdims=True)
    mixed = keep * norm
    rest = c10 * (1.0 - share)
    mixed = mixed + rest[:, 0:1] * const_value[0:1] + rest[:, 1:2] * const_value[1:2]
    return mixed, keep, rest


def side_backward(norm, named, weights, const_value, probs, share, chosen, keep, rest, chosen_back, grad, ffn_count):
    self_dot = jnp.sum(grad * norm, axis=1, keepdims=True)
    value_dot = jnp.concatenate(
        [jnp.sum(grad * const_value[c : c + 1], axis=1, keepdims=True) for c in range(2)], axis=1
    )
    special = jnp.concatenate(
        [
            jnp.zeros_like(self_dot),
            self_dot,
            share * self_dot + (1.0 - share) * value_dot,
        ],
        axis=1,
    )
    d_probs = jnp.concatenate([chosen_back, special], axis=1) * named
    d_logits = probs * (d_probs - jnp.sum(probs * d_probs, axis=1, keepdims=True))
    c10 = chosen[:, ffn_count + 2 : ffn_count + 4]
    d_share = share * (1.0 - share) * c10 * (self_dot - value_dot)
    d_mix = jnp.stack([d_share, -d_share], axis=2).reshape(norm.shape[0], 4)
    d_both = jnp.concatenate([d_logits, d_mix], axis=1)
    back = (
        lax.dot_general(
            d_both, weights, (((1,), (1,)), ((), ())), precision=lax.Precision.HIGHEST
        )
        + keep * grad
    )
    weight_part = lax.dot_general(
        norm, d_both, (((0,), (0,)), ((), ())), precision=lax.Precision.HIGHEST
    )
    value_part = lax.dot_general(
        rest, grad, (((0,), (0,)), ((), ())), precision=lax.Precision.HIGHEST
    )
    return back, weight_part, value_part


EXP_PAD = 16


def dot(a, b):
    return jnp.dot(a, b, preferred_element_type=jnp.float32)


def dot_nt(a, b):
    return lax.dot_general(a, b, (((1,), (1,)), ((), ())), preferred_element_type=jnp.float32)


def dot_tn(a, b):
    return lax.dot_general(a, b, (((0,), (0,)), ((), ())), preferred_element_type=jnp.float32)


def three_parts(values):
    first = values.astype(jnp.bfloat16)
    rest = values - first.astype(jnp.float32)
    second = rest.astype(jnp.bfloat16)
    third = (rest - second.astype(jnp.float32)).astype(jnp.bfloat16)
    return (first, second, third)


def expert_kernel(
    n_dp,
    ffn_count,
    route_count,
    moe_ref,
    grad_ref,
    routes_ref,
    residual_ref,
    router_ref,
    gate_ref,
    up_ref,
    down_ref,
    part_ref,
    back_ref,
    chosen_ref,
    weight_ref,
    probs_s,
    rank_s,
    part_s,
    back_s,
):
    expert = pl.program_id(0)
    rows = moe_ref.shape[0]
    hidden = gate_ref.shape[2]
    step = moe_ref.shape[1] // n_dp

    @pl.when(expert == 0)
    def _():
        parts = three_parts(router_ref[...])
        logits = residual_ref[...]
        for part in parts:
            logits = logits + dot_nt(part, moe_ref[...])
        index = lax.broadcasted_iota(jnp.int32, (EXP_PAD, rows), 0)
        logits = jnp.where(index < route_count, logits, MASKED)
        top = jnp.max(logits, axis=0, keepdims=True)
        exps = jnp.exp(logits - top)
        probs_s[...] = exps / jnp.sum(exps, axis=0, keepdims=True)
        named = (routes_ref[0:1, :] == index) | (routes_ref[1:2, :] == index)
        named = jnp.where(named, 1.0, 0.0)
        width = 256
        before = lax.broadcasted_iota(jnp.int32, (width, width), 0)
        after = lax.broadcasted_iota(jnp.int32, (width, width), 1)
        earlier = jnp.where(before < after, 1.0, 0.0).astype(jnp.bfloat16)
        total = jnp.zeros((EXP_PAD, 1), jnp.float32)
        for start in range(0, rows, width):
            block = named[:, start : start + width]
            rank = dot(block.astype(jnp.bfloat16), earlier) + total
            rank_s[:, start : start + width] = jnp.where(block > 0.5, rank, -1.0)
            total = total + jnp.sum(block, axis=1, keepdims=True)
        part_s[...] = jnp.zeros_like(part_s)
        back_s[...] = jnp.zeros_like(back_s)

    slot = lax.broadcasted_iota(jnp.int32, (CAP, rows), 0).astype(jnp.float32)
    hit = rank_s[pl.ds(expert, 1), :] == slot
    dispatch = jnp.where(hit, 1.0, 0.0).astype(jnp.bfloat16)
    slot_weight = jnp.sum(
        jnp.where(hit, probs_s[pl.ds(expert, 1), :], 0.0), axis=1, keepdims=True
    )
    rows_in = dot(dispatch, moe_ref[...]).astype(jnp.bfloat16)
    rows_grad = dot(dispatch, grad_ref[...])
    gate_w = gate_ref[0]
    up_w = up_ref[0]
    down_w = down_ref[0]
    gate_pre = dot(rows_in, gate_w)
    up_pre = dot(rows_in, up_w)
    sigmoid = 1.0 / (1.0 + jnp.exp(-gate_pre))
    silu = gate_pre * sigmoid
    active = (silu * up_pre).astype(jnp.bfloat16)
    out = dot(active, down_w)
    inner = jnp.sum(rows_grad * out, axis=1, keepdims=True)
    chosen_ref[pl.ds(expert, 1), :] = jnp.sum(jnp.where(hit, inner, 0.0), axis=0, keepdims=True)
    part_s[...] += dot_tn(dispatch, (out * slot_weight).astype(jnp.bfloat16))
    grad_low = (rows_grad * slot_weight).astype(jnp.bfloat16)
    grad_active = dot_nt(grad_low, down_w)
    grad_gate = (grad_active * up_pre * sigmoid * (1.0 + gate_pre * (1.0 - sigmoid))).astype(
        jnp.bfloat16
    )
    grad_up = (grad_active * silu).astype(jnp.bfloat16)
    grad_in = dot_nt(grad_gate, gate_w) + dot_nt(grad_up, up_w)
    back_s[...] += dot_tn(dispatch, grad_in.astype(jnp.bfloat16))
    for n, (left, right) in enumerate(
        ((rows_in, grad_gate), (rows_in, grad_up), (grad_low, active))
    ):
        product = dot_tn(left, right).astype(jnp.bfloat16)
        for d in range(n_dp):
            weight_ref[0, d % 2, d // 2, :, n * hidden : (n + 1) * hidden] = product[
                d * step : (d + 1) * step
            ]

    @pl.when(expert == ffn_count - 1)
    def _():
        part_ref[...] = part_s[...].astype(jnp.bfloat16)
        back_ref[...] = back_s[...].astype(jnp.bfloat16)


def experts(n_dp, route_count, moe_rows, grad_rows, routes_t, residual_t, router_t, gate_w, up_w, down_w):
    rows, width = moe_rows.shape
    ffn_count, _, hidden = gate_w.shape
    step = width // n_dp

    def whole(shape):
        return pl.BlockSpec(shape, lambda e: (0,) * len(shape), pipeline_mode=pl.Buffered(1))

    return pl.pallas_call(
        functools.partial(expert_kernel, n_dp, ffn_count, route_count),
        grid=(ffn_count,),
        out_shape=(
            jax.ShapeDtypeStruct((rows, width), jnp.bfloat16),
            jax.ShapeDtypeStruct((rows, width), jnp.bfloat16),
            jax.ShapeDtypeStruct((ffn_count, rows), jnp.float32),
            jax.ShapeDtypeStruct((ffn_count, 2, n_dp // 2, step, 3 * hidden), jnp.bfloat16),
        ),
        in_specs=[
            whole((rows, width)),
            whole((rows, width)),
            whole((2, rows)),
            whole((EXP_PAD, rows)),
            whole((EXP_PAD, width)),
            pl.BlockSpec((1, width, hidden), lambda e: (e, 0, 0)),
            pl.BlockSpec((1, width, hidden), lambda e: (e, 0, 0)),
            pl.BlockSpec((1, hidden, width), lambda e: (e, 0, 0)),
        ],
        out_specs=(
            whole((rows, width)),
            whole((rows, width)),
            whole((ffn_count, rows)),
            pl.BlockSpec((1, 2, n_dp // 2, step, 3 * hidden), lambda e: (e, 0, 0, 0, 0)),
        ),
        scratch_shapes=[
            pltpu.VMEM((EXP_PAD, rows), jnp.float32),
            pltpu.VMEM((EXP_PAD, rows), jnp.float32),
            pltpu.VMEM((rows, width), jnp.float32),
            pltpu.VMEM((rows, width), jnp.float32),
        ],
        compiler_params=pltpu.CompilerParams(
            dimension_semantics=("arbitrary",), vmem_limit_bytes=48 << 20
        ),
        name="experts",
    )(moe_rows, grad_rows, routes_t, residual_t, router_t, gate_w, up_w, down_w)


def attention_forward(query, key, value):
    seq_count, length, head_count, head_width = query.shape
    query_rows = min(512, length)
    block_count = length // query_rows
    scale = head_width ** (-0.5)

    def one_block(block_index):
        seq_index = block_index // block_count
        query_start = block_index % block_count * query_rows
        query_seq = lax.dynamic_index_in_dim(query, seq_index, 0, keepdims=False)
        query_blk = lax.dynamic_slice_in_dim(query_seq, query_start, query_rows, 0)
        key_seq = lax.dynamic_index_in_dim(key, seq_index, 0, keepdims=False)
        value_seq = lax.dynamic_index_in_dim(value, seq_index, 0, keepdims=False)
        scores = (
            jnp.einsum("qhd,khd->hqk", query_blk, key_seq, preferred_element_type=jnp.float32)
            * scale
        )
        scores = jnp.where(block_mask(query_start, query_rows, length)[None], scores, MASKED)
        row_max = jnp.max(scores, axis=-1, keepdims=True)
        exp_scores = jnp.exp(scores - row_max)
        row_total = jnp.sum(exp_scores, axis=-1, keepdims=True)
        soft_probs = (exp_scores / row_total).astype(jnp.bfloat16)
        result = jnp.einsum(
            "hqk,khd->qhd", soft_probs, value_seq, preferred_element_type=jnp.float32
        )
        return (result, (row_max + jnp.log(row_total))[..., 0])

    return lax.map(one_block, jnp.arange(seq_count * block_count, dtype=jnp.int32))


def attention_backward(query, key, value, grad_mixed, log_totals):
    seq_count, length, head_count, head_width = query.shape
    query_rows = min(512, length)
    block_count = length // query_rows
    scale = head_width ** (-0.5)
    log_totals = log_totals.reshape(seq_count, block_count, head_count, query_rows)

    def per_sequence(operands):
        query_seq, key_seq, value_seq, grad_seq, total_seq = operands

        def block_step(carried, block_index):
            key_acc, value_acc = carried
            query_start = block_index * query_rows
            query_blk = lax.dynamic_slice_in_dim(query_seq, query_start, query_rows, 0)
            grad_blk = lax.dynamic_slice_in_dim(grad_seq, query_start, query_rows, 0)
            total_blk = lax.dynamic_index_in_dim(total_seq, block_index, 0, keepdims=False)
            scores = (
                jnp.einsum("qhd,khd->hqk", query_blk, key_seq, preferred_element_type=jnp.float32)
                * scale
            )
            scores = jnp.where(block_mask(query_start, query_rows, length)[None], scores, MASKED)
            soft_probs = jnp.exp(scores - total_blk[..., None])
            grad_probs = jnp.einsum(
                "qhd,khd->hqk", grad_blk, value_seq, preferred_element_type=jnp.float32
            )
            grad_scores = (
                soft_probs * (grad_probs - jnp.sum(soft_probs * grad_probs, axis=-1, keepdims=True))
            ).astype(jnp.bfloat16)
            query_part = (
                jnp.einsum("hqk,khd->qhd", grad_scores, key_seq, preferred_element_type=jnp.float32)
                * scale
            )
            key_acc = (
                key_acc
                + jnp.einsum(
                    "hqk,qhd->khd", grad_scores, query_blk, preferred_element_type=jnp.float32
                )
                * scale
            )
            value_acc = value_acc + jnp.einsum(
                "hqk,qhd->khd",
                soft_probs.astype(jnp.bfloat16),
                grad_blk,
                preferred_element_type=jnp.float32,
            )
            return ((key_acc, value_acc), query_part)

        zero_acc = jnp.zeros((length, head_count, head_width), jnp.float32)
        (key_acc, value_acc), query_parts = lax.scan(
            block_step, (zero_acc, zero_acc), jnp.arange(block_count, dtype=jnp.int32)
        )
        return (query_parts.reshape(length, head_count, head_width), key_acc, value_acc)

    return lax.map(per_sequence, (query, key, value, grad_mixed, log_totals))


def on_device(
    layer_input,
    attn_gain,
    query_weight,
    key_weight,
    value_weight,
    out_weight,
    moe_gain,
    router_weight,
    gate_residual,
    const_gate,
    const_value,
    gate_weight,
    up_weight,
    down_weight,
    routes,
    grad_out,
):
    local_rows, model_width = layer_input.shape
    tensor_size = lax.axis_size("tensor")
    group_rows = local_rows * tensor_size
    row_start = lax.axis_index("tensor") * local_rows
    seq_count = group_rows // LENGTH
    head_count = query_weight.shape[1] // HD
    ffn_count = gate_weight.shape[0]
    route_count = router_weight.shape[1]
    cosine, sine = rope_tables(LENGTH, HD)
    input_wide = layer_input.astype(jnp.float32)
    norm_attn, pull_attn_norm = jax.vjp(rms_norm, input_wide, attn_gain)
    norm_attn = norm_attn.astype(jnp.bfloat16)
    attn_rows = lax.all_gather(norm_attn, "tensor", axis=0, tiled=True)
    query_raw = jnp.dot(attn_rows, query_weight, preferred_element_type=jnp.float32).reshape(
        seq_count, LENGTH, head_count, HD
    )
    key_raw = jnp.dot(attn_rows, key_weight, preferred_element_type=jnp.float32).reshape(
        seq_count, LENGTH, head_count, HD
    )
    value_raw = jnp.dot(attn_rows, value_weight, preferred_element_type=jnp.float32).reshape(
        seq_count, LENGTH, head_count, HD
    )
    query = rotate(query_raw, cosine, sine).astype(jnp.bfloat16)
    key = rotate(key_raw, cosine, sine).astype(jnp.bfloat16)
    value = value_raw.astype(jnp.bfloat16)
    mixed, log_totals = attention_forward(query, key, value)
    mixed = mixed.reshape(group_rows, head_count * HD).astype(jnp.bfloat16)
    attn_part = jnp.dot(mixed, out_weight, preferred_element_type=jnp.float32)
    attn_sum = lax.psum_scatter(
        attn_part.astype(jnp.bfloat16), "tensor", scatter_dimension=0, tiled=True
    ).astype(jnp.float32)
    hidden = input_wide + attn_sum
    norm_moe, pull_moe_norm = jax.vjp(rms_norm, hidden, moe_gain)
    norm_moe = norm_moe.astype(jnp.bfloat16)
    moe_rows = lax.all_gather(norm_moe, "tensor", axis=0, tiled=True)
    both_weight = pad_router(router_weight, const_gate)
    n_dp = lax.axis_size("dp")
    grad_rows = lax.all_gather(grad_out, "tensor", axis=0, tiled=True)
    pad = ((0, EXP_PAD - route_count), (0, 0))
    ffn_part, ffn_back, chosen_t, expert_part = experts(
        n_dp,
        route_count,
        moe_rows,
        grad_rows,
        routes.T,
        jnp.pad(gate_residual.T, pad),
        jnp.pad(router_weight.T, pad),
        gate_weight,
        up_weight,
        down_weight,
    )
    ffn_sum = lax.psum_scatter(ffn_part, "tensor", scatter_dimension=0, tiled=True).astype(
        jnp.float32
    )
    moe_back = lax.psum_scatter(ffn_back, "tensor", scatter_dimension=0, tiled=True).astype(
        jnp.float32
    )
    chosen_back = lax.psum_scatter(chosen_t.T, "tensor", scatter_dimension=0, tiled=True)
    local_routes = lax.dynamic_slice_in_dim(routes, row_start, local_rows, 0)
    local_logits = lax.dynamic_slice_in_dim(gate_residual, row_start, local_rows, 0)
    kinds = jnp.arange(route_count, dtype=jnp.int32)[None, :]
    named = ((local_routes[:, 0:1] == kinds) | (local_routes[:, 1:2] == kinds)).astype(jnp.float32)
    norm_wide = norm_moe.astype(jnp.float32)
    probs, share, chosen = side_experts(
        norm_wide, named, both_weight, local_logits, const_value, ffn_count
    )
    special_sum, keep, rest = side_sum(norm_wide, share, chosen, const_value, ffn_count)
    output = (hidden + ffn_sum + special_sum).astype(jnp.bfloat16)
    grad_wide = grad_out.astype(jnp.float32)
    side_back, both_part, const_value_part = side_backward(
        norm_wide, named, both_weight, const_value, probs, share, chosen, keep, rest,
        chosen_back, grad_wide, ffn_count,
    )
    router_part = both_part[:, :route_count]
    const_gate_part = jnp.transpose(both_part[:, route_count:].reshape(model_width, 2, 2), (1, 0, 2))
    hidden_norm_back, moe_gain_part = pull_moe_norm(moe_back + side_back)
    hidden_grad = grad_wide + hidden_norm_back
    attn_grad_rows = lax.all_gather(hidden_grad.astype(jnp.bfloat16), "tensor", axis=0, tiled=True)
    out_part = jnp.einsum("gh,gd->hd", mixed, attn_grad_rows, preferred_element_type=jnp.float32)
    grad_mixed = (
        jnp.einsum("gd,hd->gh", attn_grad_rows, out_weight, preferred_element_type=jnp.float32)
        .astype(jnp.bfloat16)
        .reshape(seq_count, LENGTH, head_count, HD)
    )
    query_back, key_back, value_back = attention_backward(query, key, value, grad_mixed, log_totals)
    query_back = (
        unrotate(query_back, cosine, sine).astype(jnp.bfloat16).reshape(group_rows, head_count * HD)
    )
    key_back = (
        unrotate(key_back, cosine, sine).astype(jnp.bfloat16).reshape(group_rows, head_count * HD)
    )
    value_back = value_back.astype(jnp.bfloat16).reshape(group_rows, head_count * HD)
    query_part = jnp.einsum("gd,gh->dh", attn_rows, query_back, preferred_element_type=jnp.float32)
    key_part = jnp.einsum("gd,gh->dh", attn_rows, key_back, preferred_element_type=jnp.float32)
    value_part = jnp.einsum("gd,gh->dh", attn_rows, value_back, preferred_element_type=jnp.float32)
    attn_back = jnp.einsum(
        "gh,dh->gd", query_back, query_weight, preferred_element_type=jnp.float32
    )
    attn_back = attn_back + jnp.einsum(
        "gh,dh->gd", key_back, key_weight, preferred_element_type=jnp.float32
    )
    attn_back = attn_back + jnp.einsum(
        "gh,dh->gd", value_back, value_weight, preferred_element_type=jnp.float32
    )
    norm_back = lax.psum_scatter(
        attn_back.astype(jnp.bfloat16), "tensor", scatter_dimension=0, tiled=True
    ).astype(jnp.float32)
    input_norm_back, attn_gain_part = pull_attn_norm(norm_back)
    input_grad = (hidden_grad + input_norm_back).astype(jnp.bfloat16)
    small_sums = lax.psum(
        (attn_gain_part, moe_gain_part, router_part, const_gate_part, const_value_part),
        ("dp", "tensor"),
    )
    attn_parts = jnp.stack(
        [query_part, key_part, value_part, out_part.T], axis=1
    ).reshape(model_width, -1).astype(jnp.bfloat16)
    attn_sums = lax.psum_scatter(attn_parts, "dp", scatter_dimension=0, tiled=True).astype(
        jnp.float32
    ).reshape(model_width // n_dp, 4, -1)
    hidden_units = gate_weight.shape[2]
    expert_part = jnp.transpose(expert_part, (2, 1, 3, 0, 4)).reshape(
        model_width, -1
    )
    expert_sums = lax.psum_scatter(expert_part, "dp", scatter_dimension=0, tiled=True).astype(
        jnp.float32
    ).reshape(model_width // n_dp, ffn_count, 3 * hidden_units)
    expert_sums = jnp.transpose(expert_sums, (1, 0, 2))
    weight_sums = (
        attn_sums[:, 0],
        attn_sums[:, 1],
        attn_sums[:, 2],
        attn_sums[:, 3].T,
        expert_sums[:, :, :hidden_units],
        expert_sums[:, :, hidden_units : 2 * hidden_units],
        jnp.transpose(expert_sums[:, :, 2 * hidden_units :], (0, 2, 1)),
    )
    return (
        output,
        input_grad,
        small_sums[0],
        weight_sums[0],
        weight_sums[1],
        weight_sums[2],
        weight_sums[3],
        small_sums[1],
        small_sums[2],
        small_sums[3],
        small_sums[4],
        weight_sums[4],
        weight_sums[5],
        weight_sums[6],
    )


def solution(mesh):
    in_specs = (
        P(("dp", "tensor"), None),
        P(),
        P(None, "tensor"),
        P(None, "tensor"),
        P(None, "tensor"),
        P("tensor", None),
        P(),
        P(),
        P("dp", None),
        P(),
        P(),
        P(None, None, "tensor"),
        P(None, None, "tensor"),
        P(None, "tensor", None),
        P("dp", None),
        P(("dp", "tensor"), None),
    )
    out_specs = (
        P(("dp", "tensor"), None),
        P(("dp", "tensor"), None),
        P(),
        P("dp", "tensor"),
        P("dp", "tensor"),
        P("dp", "tensor"),
        P("tensor", "dp"),
        P(),
        P(),
        P(),
        P(),
        P(None, "dp", "tensor"),
        P(None, "dp", "tensor"),
        P(None, "tensor", "dp"),
    )
    return jax.shard_map(
        on_device, mesh=mesh, in_specs=in_specs, out_specs=out_specs, check_vma=False
    )
```

```python
import functools
import math

import jax
import jax.numpy as jnp
import numpy as np
from jax import lax
from jax.experimental import pallas as pl
from jax.experimental.pallas import tpu as pltpu
from jax.sharding import PartitionSpec as P

HD = 64
LENGTH = 1024
BLOCK = 256
CAP = 256


EPSILON = 1e-06
MASKED = -1e30


def rope_tables(length, head_width):
    position = jnp.arange(length, dtype=jnp.float32)[:, None]
    inverse = jnp.exp(
        jnp.arange(head_width // 2, dtype=jnp.float32) * (-2.0 * math.log(10000.0) / head_width)
    )
    angle = position * inverse[None, :]
    return (jnp.cos(angle), jnp.sin(angle))


def rotate(values, cosine, sine):
    half_width = values.shape[-1] // 2
    first_half = values[..., :half_width]
    second_half = values[..., half_width:]
    cos_table = cosine[:, None, :]
    sin_table = sine[:, None, :]
    return jnp.concatenate(
        [
            first_half * cos_table - second_half * sin_table,
            second_half * cos_table + first_half * sin_table,
        ],
        axis=-1,
    )


def unrotate(values, cosine, sine):
    half_width = values.shape[-1] // 2
    first_half = values[..., :half_width]
    second_half = values[..., half_width:]
    cos_table = cosine[:, None, :]
    sin_table = sine[:, None, :]
    return jnp.concatenate(
        [
            first_half * cos_table + second_half * sin_table,
            second_half * cos_table - first_half * sin_table,
        ],
        axis=-1,
    )


def rms_norm(values, gain):
    scale = lax.rsqrt(jnp.mean(values * values, axis=-1, keepdims=True) + EPSILON)
    return values * scale * gain


def block_mask(query_start, query_rows, length):
    query_pos = query_start + jnp.arange(query_rows, dtype=jnp.int32)
    key_pos = jnp.arange(length, dtype=jnp.int32)
    return (key_pos // BLOCK)[None, :] <= (query_pos // BLOCK)[:, None]


def attention_forward(query, key, value):
    seq_count, length, head_count, head_width = query.shape
    query_rows = min(512, length)
    block_count = length // query_rows
    scale = head_width ** (-0.5)

    def one_block(block_index):
        seq_index = block_index // block_count
        query_start = block_index % block_count * query_rows
        query_seq = lax.dynamic_index_in_dim(query, seq_index, 0, keepdims=False)
        query_blk = lax.dynamic_slice_in_dim(query_seq, query_start, query_rows, 0)
        key_seq = lax.dynamic_index_in_dim(key, seq_index, 0, keepdims=False)
        value_seq = lax.dynamic_index_in_dim(value, seq_index, 0, keepdims=False)
        scores = (
            jnp.einsum("qhd,khd->hqk", query_blk, key_seq, preferred_element_type=jnp.float32)
            * scale
        )
        scores = jnp.where(block_mask(query_start, query_rows, length)[None], scores, MASKED)
        row_max = jnp.max(scores, axis=-1, keepdims=True)
        exp_scores = jnp.exp(scores - row_max)
        row_total = jnp.sum(exp_scores, axis=-1, keepdims=True)
        soft_probs = (exp_scores / row_total).astype(jnp.bfloat16)
        result = jnp.einsum(
            "hqk,khd->qhd", soft_probs, value_seq, preferred_element_type=jnp.float32
        )
        return (result, (row_max + jnp.log(row_total))[..., 0])

    return lax.map(one_block, jnp.arange(seq_count * block_count, dtype=jnp.int32))


EXP_PAD = 16


def dot(a, b):
    return jnp.dot(a, b, preferred_element_type=jnp.float32)


def dot_nt(a, b):
    return lax.dot_general(a, b, (((1,), (1,)), ((), ())), preferred_element_type=jnp.float32)


def dot_tn(a, b):
    return lax.dot_general(a, b, (((0,), (0,)), ((), ())), preferred_element_type=jnp.float32)


def three_parts(values):
    first = values.astype(jnp.bfloat16)
    rest = values - first.astype(jnp.float32)
    second = rest.astype(jnp.bfloat16)
    third = (rest - second.astype(jnp.float32)).astype(jnp.bfloat16)
    return (first, second, third)


def expert_kernel(
    n_dp,
    ffn_count,
    route_count,
    moe_ref,
    grad_ref,
    routes_ref,
    residual_ref,
    router_ref,
    gate_ref,
    up_ref,
    down_ref,
    part_ref,
    back_ref,
    chosen_ref,
    weight_ref,
    probs_s,
    rank_s,
    part_s,
    back_s,
):
    expert = pl.program_id(0)
    rows = moe_ref.shape[0]
    hidden = gate_ref.shape[2]
    step = moe_ref.shape[1] // n_dp

    @pl.when(expert == 0)
    def _():
        parts = three_parts(router_ref[...])
        logits = residual_ref[...]
        for part in parts:
            logits = logits + dot_nt(part, moe_ref[...])
        index = lax.broadcasted_iota(jnp.int32, (EXP_PAD, rows), 0)
        logits = jnp.where(index < route_count, logits, MASKED)
        top = jnp.max(logits, axis=0, keepdims=True)
        exps = jnp.exp(logits - top)
        probs_s[...] = exps / jnp.sum(exps, axis=0, keepdims=True)
        named = (routes_ref[0:1, :] == index) | (routes_ref[1:2, :] == index)
        named = jnp.where(named, 1.0, 0.0)
        width = 256
        before = lax.broadcasted_iota(jnp.int32, (width, width), 0)
        after = lax.broadcasted_iota(jnp.int32, (width, width), 1)
        earlier = jnp.where(before < after, 1.0, 0.0).astype(jnp.bfloat16)
        total = jnp.zeros((EXP_PAD, 1), jnp.float32)
        for start in range(0, rows, width):
            block = named[:, start : start + width]
            rank = dot(block.astype(jnp.bfloat16), earlier) + total
            rank_s[:, start : start + width] = jnp.where(block > 0.5, rank, -1.0)
            total = total + jnp.sum(block, axis=1, keepdims=True)
        part_s[...] = jnp.zeros_like(part_s)
        back_s[...] = jnp.zeros_like(back_s)

    slot = lax.broadcasted_iota(jnp.int32, (CAP, rows), 0).astype(jnp.float32)
    hit = rank_s[pl.ds(expert, 1), :] == slot
    dispatch = jnp.where(hit, 1.0, 0.0).astype(jnp.bfloat16)
    slot_weight = jnp.sum(
        jnp.where(hit, probs_s[pl.ds(expert, 1), :], 0.0), axis=1, keepdims=True
    )
    rows_in = dot(dispatch, moe_ref[...]).astype(jnp.bfloat16)
    rows_grad = dot(dispatch, grad_ref[...])
    gate_w = gate_ref[0]
    up_w = up_ref[0]
    down_w = down_ref[0]
    gate_pre = dot(rows_in, gate_w)
    up_pre = dot(rows_in, up_w)
    sigmoid = 1.0 / (1.0 + jnp.exp(-gate_pre))
    silu = gate_pre * sigmoid
    active = (silu * up_pre).astype(jnp.bfloat16)
    out = dot(active, down_w)
    inner = jnp.sum(rows_grad * out, axis=1, keepdims=True)
    chosen_row = jnp.sum(jnp.where(hit, inner, 0.0), axis=0, keepdims=True)
    for n in range(chosen_ref.shape[0]):
        chosen_ref[n, pl.ds(expert, 1), :] = chosen_row[
            :, n * chosen_ref.shape[2] : (n + 1) * chosen_ref.shape[2]
        ]
    part_s[...] += dot_tn(dispatch, (out * slot_weight).astype(jnp.bfloat16))
    grad_low = (rows_grad * slot_weight).astype(jnp.bfloat16)
    grad_active = dot_nt(grad_low, down_w)
    grad_gate = (grad_active * up_pre * sigmoid * (1.0 + gate_pre * (1.0 - sigmoid))).astype(
        jnp.bfloat16
    )
    grad_up = (grad_active * silu).astype(jnp.bfloat16)
    grad_in = dot_nt(grad_gate, gate_w) + dot_nt(grad_up, up_w)
    back_s[...] += dot_tn(dispatch, grad_in.astype(jnp.bfloat16))
    for n, (left, right) in enumerate(
        ((rows_in, grad_gate), (rows_in, grad_up), (grad_low, active))
    ):
        product = dot_tn(left, right).astype(jnp.bfloat16)
        for d in range(n_dp):
            weight_ref[0, d % 2, d // 2, :, n * hidden : (n + 1) * hidden] = product[
                d * step : (d + 1) * step
            ]

    @pl.when(expert == ffn_count - 1)
    def _():
        part_ref[...] = part_s[...].astype(jnp.bfloat16)
        back_ref[...] = back_s[...].astype(jnp.bfloat16)


def experts(n_dp, n_t, route_count, moe_rows, grad_rows, routes_t, residual_t, router_t, gate_w, up_w, down_w):
    rows, width = moe_rows.shape
    ffn_count, _, hidden = gate_w.shape
    step = width // n_dp

    def whole(shape):
        return pl.BlockSpec(shape, lambda e: (0,) * len(shape), pipeline_mode=pl.Buffered(1))

    return pl.pallas_call(
        functools.partial(expert_kernel, n_dp, ffn_count, route_count),
        grid=(ffn_count,),
        out_shape=(
            jax.ShapeDtypeStruct((rows, width), jnp.bfloat16),
            jax.ShapeDtypeStruct((rows, width), jnp.bfloat16),
            jax.ShapeDtypeStruct((n_t, ffn_count, rows // n_t), jnp.float32),
            jax.ShapeDtypeStruct((ffn_count, 2, n_dp // 2, step, 3 * hidden), jnp.bfloat16),
        ),
        in_specs=[
            whole((rows, width)),
            whole((rows, width)),
            whole((2, rows)),
            whole((EXP_PAD, rows)),
            whole((EXP_PAD, width)),
            pl.BlockSpec((1, width, hidden), lambda e: (e, 0, 0)),
            pl.BlockSpec((1, width, hidden), lambda e: (e, 0, 0)),
            pl.BlockSpec((1, hidden, width), lambda e: (e, 0, 0)),
        ],
        out_specs=(
            whole((rows, width)),
            whole((rows, width)),
            whole((n_t, ffn_count, rows // n_t)),
            pl.BlockSpec((1, 2, n_dp // 2, step, 3 * hidden), lambda e: (e, 0, 0, 0, 0)),
        ),
        scratch_shapes=[
            pltpu.VMEM((EXP_PAD, rows), jnp.float32),
            pltpu.VMEM((EXP_PAD, rows), jnp.float32),
            pltpu.VMEM((rows, width), jnp.float32),
            pltpu.VMEM((rows, width), jnp.float32),
        ],
        compiler_params=pltpu.CompilerParams(
            dimension_semantics=("arbitrary",), vmem_limit_bytes=48 << 20
        ),
        name="experts",
    )(moe_rows, grad_rows, routes_t, residual_t, router_t, gate_w, up_w, down_w)


MESH = pl.DeviceIdType.MESH


def bit_of(index, position):
    return index // (1 << position) % 2


def flipped(index, position):
    return index + (1 << position) * (1 - 2 * bit_of(index, position))


def log2_of(count):
    return count.bit_length() - 1


def greet(dp, place, dp_bits, tensor_count):
    barrier = pltpu.get_barrier_semaphore()
    for position in range(dp_bits):
        pl.semaphore_signal(
            barrier, inc=1, device_id={"dp": flipped(dp, position)}, device_id_type=MESH
        )
    for step in range(1, tensor_count):
        pl.semaphore_signal(
            barrier,
            inc=1,
            device_id={"tensor": (place + step) % tensor_count},
            device_id_type=MESH,
        )
    pl.semaphore_wait(barrier, dp_bits + tensor_count - 1)


class LineGather:
    def __init__(self, blocks, send, recv, place):
        self.blocks, self.send, self.recv, self.place = blocks, send, recv, place
        self.count = blocks.shape[0]

    def copy(self, block, way):
        return pltpu.make_async_remote_copy(
            src_ref=self.blocks.at[block],
            dst_ref=self.blocks.at[block],
            send_sem=self.send.at[way, block],
            recv_sem=self.recv.at[block],
            device_id={"tensor": self.place + 1 - 2 * way},
            device_id_type=MESH,
        )

    def start(self):
        self.pass_on(self.place)

    def pass_on(self, block, ways=(0, 1)):
        if 0 in ways:

            @pl.when(self.place < self.count - 1)
            def _():
                self.copy(block, 0).start()

        if 1 in ways:

            @pl.when(self.place > 0)
            def _():
                self.copy(block, 1).start()

    def step(self, distance):
        below, above = self.place - distance, self.place + distance

        @pl.when(below >= 0)
        def _():
            self.copy(below, 0).wait_recv()
            self.pass_on(below, (0,))

        @pl.when(above < self.count)
        def _():
            self.copy(above, 1).wait_recv()
            self.pass_on(above, (1,))

    def finish(self):
        for distance in range(self.count):
            below, above = self.place - distance, self.place + distance

            @pl.when((below >= 0) & (self.place < self.count - 1))
            def _(below=below):
                self.copy(below, 0).wait_send()

            @pl.when((above < self.count) & (self.place > 0))
            def _(above=above):
                self.copy(above, 1).wait_send()


class LineScatter:
    def __init__(self, parts, arrived, send, recv, place, pieces):
        self.parts, self.arrived, self.send, self.recv = parts, arrived, send, recv
        self.place, self.count, self.pieces = place, parts.shape[0], pieces
        self.rows = parts.shape[1] // pieces

    def piece(self, ref, block, n):
        return ref.at[block, pl.ds(n * self.rows, self.rows)]

    def copy(self, block, n, way, own=False):
        there = self.piece(self.arrived, block + 1 - way, n)
        return pltpu.make_async_remote_copy(
            src_ref=self.piece(self.parts, block, n) if own else there,
            dst_ref=there,
            send_sem=self.send.at[way, block, n],
            recv_sem=self.recv.at[way, block, n],
            device_id={"tensor": self.place + 1 - 2 * way},
            device_id_type=MESH,
        )

    def originate(self, block):
        for way, first in ((0, 0), (1, self.count - 1)):
            if block != first:

                @pl.when(self.place == first)
                def _(way=way):
                    for n in range(self.pieces):
                        self.copy(block, n, way, own=True).start()

    def forward(self, block):
        for way in (0, 1):
            inside = (
                (self.place > 0) & (self.place < block)
                if way == 0
                else (self.place > block) & (self.place < self.count - 1)
            )

            @pl.when(inside)
            def _(way=way):
                for n in range(self.pieces):
                    self.copy(block, n, way).wait_recv()
                    there = self.piece(self.arrived, block + 1 - way, n)
                    mine = self.piece(self.parts, block, n)
                    there[...] = (
                        there[...].astype(jnp.float32) + mine[...].astype(jnp.float32)
                    ).astype(there.dtype)
                    self.copy(block, n, way).start()

    def collect(self, total):
        place = self.place
        total[...] = self.parts[place].astype(jnp.float32)
        for way in (0, 1):

            @pl.when(place > 0 if way == 0 else place < self.count - 1)
            def _(way=way):
                for n in range(self.pieces):
                    self.copy(place, n, way).wait_recv()
                    rows = pl.ds(n * self.rows, self.rows)
                    total[rows, :] += self.arrived[place + 1 - way, rows, :].astype(jnp.float32)

    def finish(self):
        for block in range(self.count):
            for way in (0, 1):

                @pl.when(self.place < block if way == 0 else self.place > block)
                def _(block=block, way=way):
                    for n in range(self.pieces):
                        self.copy(block, n, way).wait_send()


class Halving:
    def __init__(self, source, kept, first, stages, sems, dp, dp_bits, splits):
        self.source, self.kept, self.first, self.stages = source, kept, first, stages
        self.first_send, self.first_recv, self.local, self.send, self.recv = sems
        self.dp, self.bits, self.splits = dp, dp_bits, splits
        self.core = bit_of(dp, 0)
        upper = list(range(dp_bits - 1))
        self.orders = (upper, upper[1:] + upper[:1])

    def first_copy(self, e):
        return pltpu.make_async_remote_copy(
            src_ref=self.source.at[e, 1 - self.core],
            dst_ref=self.first.at[e],
            send_sem=self.first_send.at[e],
            recv_sem=self.first_recv.at[e],
            device_id={"dp": flipped(self.dp, 0)},
            device_id_type=MESH,
        )

    def local_copy(self, e):
        return pltpu.make_async_copy(
            self.source.at[e, self.core], self.kept.at[e], self.local.at[e]
        )

    def blocks(self, part, stage, k, mine):
        order = self.orders[part]
        index = 0
        for done in order[:stage]:
            index = index + (1 << done) * bit_of(self.dp, done + 1)
        here = bit_of(self.dp, order[stage] + 1)
        index = index + (1 << order[stage]) * (here if mine else 1 - here)
        for n, free in enumerate(order[stage + 1 :]):
            index = index + (1 << free) * (k // (1 << n) % 2)
        return index

    def width(self, part):
        return pl.ds(*self.splits[part])

    def stage_copy(self, e, part, stage, k):
        start, size = self.splits[part]
        return pltpu.make_async_remote_copy(
            src_ref=self.kept.at[e, self.blocks(part, stage, k, False), :, pl.ds(start, size)],
            dst_ref=self.stages[stage].at[e, k, :, pl.ds(start, size)],
            send_sem=self.send[stage].at[e, part, k],
            recv_sem=self.recv[stage].at[e, part, k],
            device_id={"dp": flipped(self.dp, self.orders[part][stage] + 1)},
            device_id_type=MESH,
        )

    def number(self, stage):
        return 1 << (self.bits - 2 - stage)

    def start(self, e):
        self.first_copy(e).start()
        self.local_copy(e).start()

    def send_stage(self, e, stage):
        for k in range(self.number(stage)):
            for part in (0, 1):
                self.stage_copy(e, part, stage, k).start()

    def add_rows(self, target, addend):
        rows = target.shape[0]
        step = 32 if rows % 32 == 0 else rows

        def body(n, _):
            at = pl.ds(pl.multiple_of(n * step, step), step)
            target[at, :] = (
                target[at, :].astype(jnp.float32) + addend[at, :].astype(jnp.float32)
            ).astype(target.dtype)
            return 0

        lax.fori_loop(0, rows // step, body, 0)

    def open(self, e, remote_only=False):
        self.first_copy(e).wait_recv()
        if not remote_only:
            self.local_copy(e).wait()
        for block in range(self.kept.shape[1]):
            self.add_rows(self.kept.at[e, block], self.first.at[e, block])
        self.send_stage(e, 0)

    def advance(self, e, stage):
        for k in range(self.number(stage)):
            for part in (0, 1):
                self.stage_copy(e, part, stage, k).wait_recv()
                block = self.blocks(part, stage, k, True)
                self.add_rows(
                    self.kept.at[e, block, :, self.width(part)],
                    self.stages[stage].at[e, k, :, self.width(part)],
                )
        self.send_stage(e, stage + 1)

    def close(self, e, out):
        stage = self.bits - 2
        for part in (0, 1):
            self.stage_copy(e, part, stage, 0).wait_recv()
            block = self.blocks(part, stage, 0, True)
            columns = self.width(part)
            out[:, columns] = self.kept[e, block, :, columns].astype(jnp.float32) + self.stages[
                stage
            ][e, 0, :, columns].astype(jnp.float32)

    def finish(self, e):
        self.first_copy(e).wait_send()
        for stage in range(self.bits - 1):
            for k in range(self.number(stage)):
                for part in (0, 1):
                    self.stage_copy(e, part, stage, k).wait_send()


class Butterfly:
    def __init__(self, total, arrived, send, recv, dp, place, dp_bits, tensor_bits):
        self.total, self.arrived, self.send, self.recv = total, arrived, send, recv
        self.partners = [{"dp": flipped(dp, b)} for b in range(dp_bits)]
        self.partners += [{"tensor": flipped(place, b)} for b in range(tensor_bits)]

    def copy(self, n):
        return pltpu.make_async_remote_copy(
            src_ref=self.total,
            dst_ref=self.arrived.at[n],
            send_sem=self.send.at[n],
            recv_sem=self.recv.at[n],
            device_id=self.partners[n],
            device_id_type=MESH,
        )

    def start(self, n):
        self.copy(n).start()

    def take(self, n):
        self.copy(n).wait()
        self.total[...] += self.arrived[n]


def side_forward(norm, named, residual, weight_parts, const_value, route_count, ffn_count):
    lane = lax.broadcasted_iota(jnp.int32, named.shape, 1)
    low = norm.astype(jnp.bfloat16)
    both = dot(low, weight_parts[0]) + dot(low, weight_parts[1]) + dot(low, weight_parts[2])
    logits = jnp.where(lane < route_count, both + residual, MASKED)
    exps = jnp.exp(logits - jnp.max(logits, axis=1, keepdims=True))
    probs = exps / jnp.sum(exps, axis=1, keepdims=True)
    chosen = probs * named
    shares, keeps, rests = [], chosen[:, ffn_count + 1 : ffn_count + 2], []
    for c in range(2):
        at = route_count + 2 * c
        share = 1.0 / (1.0 + jnp.exp(both[:, at + 1 : at + 2] - both[:, at : at + 1]))
        weight = chosen[:, ffn_count + 2 + c : ffn_count + 3 + c]
        shares.append(share)
        keeps = keeps + weight * share
        rests.append(weight * (1.0 - share))
    special = keeps * norm + rests[0] * const_value[0:1] + rests[1] * const_value[1:2]
    return probs, chosen, shares, keeps, rests, special


def side_backward(
    norm, grad, named, forward, chosen_back, weight_parts, const_value, route_count, ffn_count
):
    probs, chosen, shares, keeps, rests, _ = forward
    lane = lax.broadcasted_iota(jnp.int32, named.shape, 1)
    self_dot = jnp.sum(grad * norm, axis=1, keepdims=True)
    value_dots = [
        jnp.sum(grad * const_value[c : c + 1], axis=1, keepdims=True) for c in range(2)
    ]
    d_probs = jnp.where(lane < ffn_count, chosen_back, 0.0)
    d_probs = jnp.where(lane == ffn_count + 1, self_dot, d_probs)
    for c in range(2):
        mixed = shares[c] * self_dot + (1.0 - shares[c]) * value_dots[c]
        d_probs = jnp.where(lane == ffn_count + 2 + c, mixed, d_probs)
    d_probs = d_probs * named
    d_both = probs * (d_probs - jnp.sum(probs * d_probs, axis=1, keepdims=True))
    d_both = jnp.where(lane < route_count, d_both, 0.0)
    for c in range(2):
        weight = chosen[:, ffn_count + 2 + c : ffn_count + 3 + c]
        d_share = shares[c] * (1.0 - shares[c]) * weight * (self_dot - value_dots[c])
        d_both = jnp.where(lane == route_count + 2 * c, d_share, d_both)
        d_both = jnp.where(lane == route_count + 2 * c + 1, -d_share, d_both)
    d_parts = three_parts(d_both)
    back = keeps * grad
    for m, n in ((0, 0), (0, 1), (1, 0), (1, 1)):
        back = back + dot_nt(d_parts[m], weight_parts[n])
    low = norm.astype(jnp.bfloat16)
    weight_part = dot_tn(d_parts[0], low) + dot_tn(d_parts[1], low) + dot_tn(d_parts[2], low)
    value_part = [jnp.sum(rests[c] * grad, axis=0, keepdims=True) for c in range(2)]
    return back, weight_part, value_part


class Nothing:
    def __getattr__(self, name):
        return lambda *arguments: None


def reduced_inside(step):
    return step % 32 == 0


def backward_kernel(
    sizes,
    part_ref,
    back_ref,
    chosen_ref,
    expert_ref,
    hidden_ref,
    moe_ref,
    grad_ref,
    input_ref,
    routes_ref,
    residual_ref,
    both_ref,
    value_ref,
    moe_gain_ref,
    attn_gain_ref,
    q_ref,
    k_ref,
    v_ref,
    o_ref,
    lse_ref,
    rows_ref,
    qkv_ref,
    out_w_ref,
    table_ref,
    output_ref,
    input_grad_ref,
    expert_out,
    attn_out,
    small_out,
    gain_out,
    chosen_in,
    pair_buf,
    line_back,
    line_part,
    staged,
    grad_rows,
    attn_part,
    acc,
    hidden_grad,
    double_grad,
    delta,
    dq,
    dk,
    dv,
    packed,
    *rest,
):
    dp_bits, n_t, ffn_count, route_count, attn_split, inside = sizes
    stage_count = dp_bits - 1 if inside else 0
    if inside:
        attn_pairs, kept, first = rest[:3]
        stages = rest[3 : 3 + stage_count]
        rest = rest[3 + stage_count :]
        a_kept, a_first = rest[:2]
        a_stages = rest[2 : 2 + stage_count]
        rest = rest[2 + stage_count :]
    else:
        attn_pairs = attn_out
    small_in, gain_acc, gain_in = rest[:3]
    rest = list(rest[3:])

    def sems(count):
        taken = rest[:count]
        del rest[:count]
        return taken

    (chosen_send, chosen_recv, gather_send, gather_recv) = sems(4)
    line_sems = [sems(2) for _ in range(3)]
    if inside:
        e_sems = sems(3) + [sems(stage_count), sems(stage_count)]
        a_sems = sems(3) + [sems(stage_count), sems(stage_count)]
    small_sems = sems(2)
    gain_sems = sems(2)
    (staged_sem,) = sems(1)

    dp = lax.axis_index("dp")
    place = lax.axis_index("tensor")
    local = hidden_ref.shape[0]
    width = hidden_ref.shape[1]
    hidden_units = expert_ref.shape[-1]
    heads = q_ref.shape[0]
    tensor_bits = log2_of(n_t)
    greet(dp, place, dp_bits, n_t)

    back_line = LineScatter(back_ref, line_back, *line_sems[0], place, 2)
    part_line = LineScatter(part_ref, line_part, *line_sems[1], place, 2)
    attn_line = LineScatter(attn_part, line_back, *line_sems[2], place, 4)
    gather = LineGather(grad_rows, gather_send, gather_recv, place)
    half = hidden_units // 2
    attn_width = attn_pairs.shape[-1]
    expert = attn = Nothing()
    if inside:
        splits = ((0, half), (half, half))
        expert = Halving(expert_ref, kept, first, stages, e_sems, dp, dp_bits, splits)
        splits = ((0, attn_split), (attn_split, attn_width - attn_split))
        attn = Halving(attn_pairs, a_kept, a_first, a_stages, a_sems, dp, dp_bits, splits)
    small = Butterfly(small_out, small_in, *small_sems, dp, place, dp_bits, tensor_bits)
    gain = Butterfly(gain_acc, gain_in, *gain_sems, dp, place, dp_bits, tensor_bits)

    def chosen_copy(step):
        there = (place + step) % n_t
        return pltpu.make_async_remote_copy(
            src_ref=chosen_ref.at[there],
            dst_ref=chosen_in.at[step - 1],
            send_sem=chosen_send.at[step - 1],
            recv_sem=chosen_recv.at[step - 1],
            device_id={"tensor": there},
            device_id_type=MESH,
        )

    for block in (n_t - 1, 0, *range(n_t - 2, 0, -1)):
        back_line.originate(block)
    for step in range(1, n_t):
        chosen_copy(step).start()

    def begin(e, _):
        expert.start(e)
        return 0

    lax.fori_loop(0, ffn_count, begin, 0)

    norm = moe_ref[place].astype(jnp.float32)
    lane = lax.broadcasted_iota(jnp.int32, (local, 128), 1)
    routes = routes_ref[...]
    named = (routes[:, 0:1] == lane) | (routes[:, 1:2] == lane)
    named = jnp.where(named, 1.0, 0.0)
    residual = jnp.concatenate(
        [residual_ref[...], jnp.zeros((local, 128 - route_count), jnp.float32)], axis=1
    )
    weight_parts = three_parts(both_ref[...])
    const_value = value_ref[...]
    grad = grad_ref[...].astype(jnp.float32)
    forward = side_forward(
        norm, named, residual, weight_parts, const_value, route_count, ffn_count
    )
    hidden = hidden_ref[...]
    pair_buf[...] = hidden + forward[-1]

    for block in (n_t - 1, 0, *range(n_t - 2, 0, -1)):
        back_line.forward(block)
    for block in (n_t - 1, 0, *range(n_t - 2, 0, -1)):
        part_line.originate(block)

    def opened(e, _):
        expert.open(e)
        return 0

    lax.fori_loop(0, ffn_count, opened, 0)

    back_line.collect(acc)
    chosen_total = chosen_ref[place]
    for step in range(1, n_t):
        chosen_copy(step).wait_recv()
        chosen_total = chosen_total + chosen_in[step - 1]
    chosen_back = jnp.concatenate(
        [chosen_total, jnp.zeros((128 - ffn_count, local), jnp.float32)], axis=0
    ).T
    back, weight_part, value_part = side_backward(
        norm, grad, named, forward, chosen_back, weight_parts, const_value, route_count, ffn_count
    )
    norm_grad = acc[...] + back
    scale = lax.rsqrt(jnp.mean(hidden * hidden, axis=1, keepdims=True) + EPSILON)
    u = norm_grad * moe_gain_ref[...]
    small_out[0:1, :] = jnp.sum(norm_grad * hidden * scale, axis=0, keepdims=True)
    small_out[1:2, :] = value_part[0]
    small_out[2:3, :] = value_part[1]
    small_out[3:8, :] = jnp.zeros((5, width), jnp.float32)
    small_out[8:24, :] = weight_part[0:16]
    hidden_grad[...] = (
        grad + scale * u - hidden * (scale * scale * scale) * jnp.mean(u * hidden, axis=1, keepdims=True)
    )
    grad_rows[place] = hidden_grad[...].astype(jnp.bfloat16)
    back_line.finish()
    gather.start()
    small.start(0)
    for block in (n_t - 1, 0, *range(n_t - 2, 0, -1)):
        part_line.forward(block)
    for step in range(1, n_t):
        gather.step(step)
        if step < small_in.shape[0]:
            small.take(step - 1)
            small.start(step)

    rows = local

    def row_block(n):
        return pl.ds(pl.multiple_of(n * rows, rows), rows)

    count = n_t
    head_lane = lax.broadcasted_iota(jnp.int32, (rows, 128), 1)
    low_half = head_lane < 64
    for block in range(count):
        at = pl.ds(block * rows, rows)
        product = dot_nt(grad_rows[block], out_w_ref[...])
        for h in range(heads):
            piece = product[:, h * 128 : (h + 1) * 128].astype(jnp.bfloat16)
            double_grad[h, at, :] = piece
            both = piece.astype(jnp.float32) * o_ref[h, at, :].astype(jnp.float32)
            delta[h : h + 1, at] = 0.5 * jnp.sum(both.T, axis=0, keepdims=True)
    out_pack = []
    for h in range(0, heads, 2):
        o_a = o_ref[h]
        o_b = o_ref[h + 1] if h + 1 < heads else jnp.zeros_like(o_a)
        lanes = lax.broadcasted_iota(jnp.int32, o_a.shape, 1)
        out_pack.append(jnp.where(lanes < 64, o_a, o_b))
    n_half = attn_pairs.shape[2]
    step_rows = attn_pairs.shape[3]
    qkv_width = packed.shape[1]

    def spread(product, start, stop):
        low = product.astype(jnp.bfloat16)
        for d in range(2 * n_half):
            attn_pairs[0, d % 2, d // 2, :, start:stop] = low[d * step_rows : (d + 1) * step_rows]

    for n, pack in enumerate(out_pack):
        total = jnp.zeros((width, 128), jnp.float32)
        for block in range(count):
            total = total + dot_tn(grad_rows[block], pack[block * rows : (block + 1) * rows])
        spread(total, qkv_width + n * 128, qkv_width + (n + 1) * 128)

    def advance_all(stage):
        def body(e, _):
            expert.advance(e, stage)
            return 0

        lax.fori_loop(0, ffn_count, body, 0)

    dq[...] = jnp.zeros_like(dq)
    factor = 64 ** (-0.5)
    gain_total = jnp.zeros((1, width), jnp.float32)
    for key_block in range(count):
        keys = pl.ds(key_block * rows, rows)
        dk[...] = jnp.zeros_like(dk)
        dv[...] = jnp.zeros_like(dv)

        def query_step(query_block, _, keys=keys):
            at = row_block(query_block)
            for h in range(heads):
                q, g = q_ref[h, at, :], double_grad[h, at, :]
                k, v = k_ref[h, keys, :], v_ref[h, keys, :]
                scores = dot_nt(k, q) * (0.5 * factor)
                probs = jnp.exp(scores - lse_ref[h : h + 1, at])
                d_probs = dot_nt(v, g) * 0.5
                d_scores = (probs * (d_probs - delta[h : h + 1, at])).astype(jnp.bfloat16)
                dk[h] += dot(d_scores, q)
                dv[h] += dot(probs.astype(jnp.bfloat16), g)
                dq[h, at, :] += dot_tn(d_scores, k)
            return 0

        lax.fori_loop(key_block, count, query_step, 0)
        table = table_ref[keys, :]
        pieces = []
        for source in (dq.at[:, keys, :], dk):
            for h in range(heads):
                turned = source[h] * (table * factor)
                pieces.append(turned + pltpu.roll(turned, 64, 1))
        for h in range(heads):
            pieces.append(dv[h])
        if len(pieces) % 2:
            pieces.append(jnp.zeros((rows, 128), jnp.float32))
        for n in range(0, len(pieces), 2):
            packed[keys, n * 64 : n * 64 + 128] = jnp.where(
                low_half, pieces[n], pieces[n + 1]
            ).astype(jnp.bfloat16)
        back_rows = dot_nt(packed[keys, :], qkv_ref[...])
        gain_total = gain_total + jnp.sum(
            back_rows * rows_ref[key_block].astype(jnp.float32), axis=0, keepdims=True
        )
        attn_part[key_block] = back_rows.astype(jnp.bfloat16)
        attn_line.originate(key_block)
        if key_block > 0:
            attn_line.forward(key_block - 1)
        if key_block == 0:
            part_line.collect(acc)
            output_ref[...] = (pair_buf[...] + acc[...]).astype(output_ref.dtype)

    gain_acc[...] = jnp.broadcast_to(gain_total / attn_gain_ref[...], gain_acc.shape)
    gain.start(0)
    for n in range(qkv_width // 128):
        total = jnp.zeros((width, 128), jnp.float32)
        for block in range(count):
            total = total + dot_tn(
                rows_ref[block], packed[pl.ds(block * rows, rows), n * 128 : (n + 1) * 128]
            )
        spread(total, n * 128, (n + 1) * 128)
    attn.start(0)
    attn_line.forward(count - 1)
    gain.take(0)
    gain.start(1)
    attn.open(0)
    for stage in range(stage_count - 1):
        advance_all(stage)
        attn.advance(0, stage)
    for n in range(1, gain_in.shape[0]):
        gain.take(n)
        if n + 1 < gain_in.shape[0]:
            gain.start(n + 1)
    for n in range(n_t - 1, small_in.shape[0]):
        small.take(n)
        if n + 1 < small_in.shape[0]:
            small.start(n + 1)
    gain_out[...] = gain_acc[...]
    attn_line.collect(acc)
    wide = input_ref[...].astype(jnp.float32)
    scale = lax.rsqrt(jnp.mean(wide * wide, axis=1, keepdims=True) + EPSILON)
    w = acc[...] * attn_gain_ref[...]
    input_grad_ref[...] = (
        hidden_grad[...]
        + scale * w
        - wide * (scale * scale * scale) * jnp.mean(w * wide, axis=1, keepdims=True)
    ).astype(input_grad_ref.dtype)
    def stored(e):
        return pltpu.make_async_copy(staged.at[e % 2], expert_out.at[e], staged_sem.at[e])

    for e in range(ffn_count if inside else 0):
        if e > 1:
            stored(e - 2).wait()
        expert.close(e, staged.at[e % 2])
        stored(e).start()
    attn.close(0, attn_out)

    for line in (part_line, attn_line):
        line.finish()
    for step in range(1, n_t):
        chosen_copy(step).wait_send()
    gather.finish()

    def ended(e, _):
        expert.finish(e)
        return 0

    lax.fori_loop(0, ffn_count, ended, 0)
    attn.finish(0)
    for e in range(ffn_count - 2, ffn_count if inside else 0):
        stored(e).wait()


def backward(dp_count, n_t, ffn_part, ffn_back, chosen, expert_part, hidden, moe_rows, grad_out,
             layer_input, routes, residual, both_weight, const_value, moe_gain, attn_gain,
             q2, k2, v2, o2, lse, attn_rows, qkv_weight, out_double, table):
    local, width = hidden.shape
    group = local * n_t
    ffn_count = expert_part.shape[0]
    units = expert_part.shape[-1]
    step = width // dp_count
    half = dp_count // 2
    dp_bits = log2_of(dp_count)
    inside = reduced_inside(step)
    stage_count = dp_bits - 1 if inside else 0
    tensor_bits = log2_of(n_t)
    heads = q2.shape[0]
    qkv_width = qkv_weight.shape[1]
    attn_width = qkv_width + -(-heads // 2) * 128
    attn_split = attn_width // 2 // 128 * 128
    bf, f32 = jnp.bfloat16, jnp.float32
    dma = pltpu.SemaphoreType.DMA
    rounds = dp_bits + tensor_bits

    def numbers(stage):
        return half >> (stage + 1)

    def line(rows_shape):
        return pltpu.VMEM((n_t + 1, *rows_shape[1:]), bf)

    block_shape = (n_t, local, width)
    reduction = []
    if inside:
        reduction = [
            pltpu.VMEM((1, 2, half, step, attn_width), bf),
            pltpu.VMEM((ffn_count, half, step, units), bf),
            pltpu.VMEM((ffn_count, half, step, units), bf),
            *[pltpu.VMEM((ffn_count, numbers(s), step, units), bf) for s in range(stage_count)],
            pltpu.VMEM((1, half, step, attn_width), bf),
            pltpu.VMEM((1, half, step, attn_width), bf),
            *[pltpu.VMEM((1, numbers(s), step, attn_width), bf) for s in range(stage_count)],
        ]
    scratch = [
        pltpu.VMEM((n_t - 1, ffn_count, local), f32),
        pltpu.VMEM((local, width), f32),
        line(block_shape),
        line(block_shape),
        pltpu.VMEM((2, step, units), f32),
        pltpu.VMEM(block_shape, bf),
        pltpu.VMEM(block_shape, bf),
        pltpu.VMEM((local, width), f32),
        pltpu.VMEM((local, width), f32),
        pltpu.VMEM((heads, group, 128), bf),
        pltpu.VMEM((8, group), f32),
        pltpu.VMEM((heads, group, 128), f32),
        pltpu.VMEM((heads, local, 128), f32),
        pltpu.VMEM((heads, local, 128), f32),
        pltpu.VMEM((group, qkv_width), bf),
        *reduction,
        pltpu.VMEM((rounds, 24, width), f32),
        pltpu.VMEM((8, width), f32),
        pltpu.VMEM((rounds, 8, width), f32),
        dma((n_t - 1,)),
        dma((n_t - 1,)),
        dma((2, n_t)),
        dma((n_t,)),
        dma((2, n_t, 2)),
        dma((2, n_t, 2)),
        dma((2, n_t, 2)),
        dma((2, n_t, 2)),
        dma((2, n_t, 4)),
        dma((2, n_t, 4)),
        *[
            s
            for n in ((ffn_count, 1) if inside else ())
            for s in (
                dma((n,)),
                dma((n,)),
                dma((n,)),
                *[dma((n, 2, numbers(s))) for s in range(stage_count)],
                *[dma((n, 2, numbers(s))) for s in range(stage_count)],
            )
        ],
        dma((rounds,)),
        dma((rounds,)),
        dma((rounds,)),
        dma((rounds,)),
        dma((ffn_count,)),
    ]
    vmem = pl.BlockSpec(memory_space=pltpu.VMEM)
    operands = (ffn_part, ffn_back, chosen, expert_part, hidden, moe_rows, grad_out, layer_input,
                routes, residual, both_weight, const_value, moe_gain, attn_gain, q2, k2, v2, o2,
                lse, attn_rows, qkv_weight, out_double, table)
    specs = [vmem] * len(operands)
    specs[3] = pl.BlockSpec(memory_space=pl.ANY)
    return pl.pallas_call(
        functools.partial(
            backward_kernel, (dp_bits, n_t, ffn_count, residual.shape[1], attn_split, inside)
        ),
        out_shape=(
            jax.ShapeDtypeStruct((local, width), bf),
            jax.ShapeDtypeStruct((local, width), bf),
            jax.ShapeDtypeStruct((ffn_count, step, units) if inside else (8, 128), f32),
            jax.ShapeDtypeStruct((step, attn_width), f32)
            if inside
            else jax.ShapeDtypeStruct((1, 2, half, step, attn_width), bf),
            jax.ShapeDtypeStruct((24, width), f32),
            jax.ShapeDtypeStruct((8, width), f32),
        ),
        in_specs=specs,
        out_specs=(vmem, vmem, pl.BlockSpec(memory_space=pl.ANY), vmem, vmem, vmem),
        scratch_shapes=scratch,
        compiler_params=pltpu.CompilerParams(
            collective_id=1, has_side_effects=True, vmem_limit_bytes=62 << 20
        ),
        name="backward",
    )(*operands)


def rope_lanes(length, head_width):
    position = np.arange(length, dtype=np.float64)[:, None]
    inverse = np.exp(np.arange(head_width // 2) * (-2.0 * math.log(10000.0) / head_width))
    angle = position * inverse[None, :]
    c, s = np.cos(angle), np.sin(angle)
    cosine = np.concatenate([c, c, c, c], axis=1).astype(np.float32)
    sine = np.concatenate([-s, s, s, -s], axis=1).astype(np.float32)
    return cosine, sine


def tidy_kernel(route_count, expert_ref, gate_out, up_out, down_out):
    units = gate_out.shape[2]
    gate_out[...] = expert_ref[:, :, 0:units]
    up_out[...] = expert_ref[:, :, units : 2 * units]
    down_out[0] = expert_ref[0, :, 2 * units :].T


def tidy(expert_sum):
    count, step, width = expert_sum.shape
    units = width // 3
    shape = jax.ShapeDtypeStruct((count, step, units), jnp.float32)
    spec = pl.BlockSpec((1, step, units), lambda e: (e, 0, 0))
    return pl.pallas_call(
        functools.partial(tidy_kernel, 0),
        grid=(count,),
        out_shape=(shape, shape, jax.ShapeDtypeStruct((count, units, step), jnp.float32)),
        in_specs=[pl.BlockSpec((1, step, width), lambda e: (e, 0, 0))],
        out_specs=(spec, spec, pl.BlockSpec((1, units, step), lambda e: (e, 0, 0))),
        compiler_params=pltpu.CompilerParams(dimension_semantics=("arbitrary",)),
        name="tidy",
    )(expert_sum)


def on_device(
    layer_input,
    attn_gain,
    query_weight,
    key_weight,
    value_weight,
    out_weight,
    moe_gain,
    router_weight,
    gate_residual,
    const_gate,
    const_value,
    gate_weight,
    up_weight,
    down_weight,
    routes,
    grad_out,
):
    local_rows, model_width = layer_input.shape
    tensor_size = lax.axis_size("tensor")
    group_rows = local_rows * tensor_size
    seq_count = group_rows // LENGTH
    head_count = query_weight.shape[1] // HD
    ffn_count = gate_weight.shape[0]
    route_count = router_weight.shape[1]
    cosine, sine = rope_tables(LENGTH, HD)
    input_wide = layer_input.astype(jnp.float32)
    norm_attn = rms_norm(input_wide, attn_gain)
    norm_attn = norm_attn.astype(jnp.bfloat16)
    attn_rows = lax.all_gather(norm_attn, "tensor", axis=0, tiled=True)
    query_raw = jnp.dot(attn_rows, query_weight, preferred_element_type=jnp.float32).reshape(
        seq_count, LENGTH, head_count, HD
    )
    key_raw = jnp.dot(attn_rows, key_weight, preferred_element_type=jnp.float32).reshape(
        seq_count, LENGTH, head_count, HD
    )
    value_raw = jnp.dot(attn_rows, value_weight, preferred_element_type=jnp.float32).reshape(
        seq_count, LENGTH, head_count, HD
    )
    query = rotate(query_raw, cosine, sine).astype(jnp.bfloat16)
    key = rotate(key_raw, cosine, sine).astype(jnp.bfloat16)
    value = value_raw.astype(jnp.bfloat16)
    mixed, log_totals = attention_forward(query, key, value)
    mixed_wide = mixed
    mixed = mixed.reshape(group_rows, head_count * HD).astype(jnp.bfloat16)
    attn_part = jnp.dot(mixed, out_weight, preferred_element_type=jnp.float32)
    attn_sum = lax.psum_scatter(
        attn_part.astype(jnp.bfloat16), "tensor", scatter_dimension=0, tiled=True
    ).astype(jnp.float32)
    hidden = input_wide + attn_sum
    norm_moe = rms_norm(hidden, moe_gain)
    norm_moe = norm_moe.astype(jnp.bfloat16)
    moe_rows = lax.all_gather(norm_moe, "tensor", axis=0, tiled=True)
    n_dp = lax.axis_size("dp")
    grad_rows = lax.all_gather(grad_out, "tensor", axis=0, tiled=True)
    pad = ((0, EXP_PAD - route_count), (0, 0))
    ffn_part, ffn_back, chosen_t, expert_part = experts(
        n_dp,
        tensor_size,
        route_count,
        moe_rows,
        grad_rows,
        routes.T,
        jnp.pad(gate_residual.T, pad),
        jnp.pad(router_weight.T, pad),
        gate_weight,
        up_weight,
        down_weight,
    )
    gates = jnp.transpose(const_gate, (1, 0, 2)).reshape(model_width, -1)
    both_weight = jnp.concatenate(
        [router_weight, gates, jnp.zeros((model_width, 128 - 4 - route_count), jnp.float32)], axis=1
    )

    def swap(values):
        return jnp.concatenate([values[..., 32:], values[..., :32]], axis=-1)

    def by_head(values, other):
        values = values.reshape(group_rows, head_count, HD)
        return jnp.transpose(jnp.concatenate([values, other(values)], axis=-1), (1, 0, 2))

    q2 = by_head(query, swap)
    k2 = by_head(key, swap)
    v2 = by_head(value, lambda x: x)
    o2 = by_head(mixed, lambda x: x)
    lse = jnp.transpose(log_totals, (1, 0, 2)).reshape(head_count, group_rows)
    lse = jnp.pad(lse, ((0, 8 - head_count), (0, 0)))
    qkv_weight = jnp.concatenate([query_weight, key_weight, value_weight], axis=1)
    qkv_weight = jnp.pad(qkv_weight, ((0, 0), (0, -qkv_weight.shape[1] % 128)))
    out_double = out_weight.reshape(head_count, 1, HD, model_width)
    out_double = jnp.broadcast_to(out_double, (head_count, 2, HD, model_width)).reshape(
        head_count * 2 * HD, model_width
    )
    cosine, sine = rope_lanes(LENGTH, HD)
    blocks = (tensor_size, local_rows, model_width)
    row_start = lax.axis_index("tensor") * local_rows
    local_routes = lax.dynamic_slice_in_dim(routes, row_start, local_rows, 0)
    local_residual = lax.dynamic_slice_in_dim(gate_residual, row_start, local_rows, 0)
    output, input_grad, expert_sum, attn_sum_rows, small, gain = backward(
        n_dp,
        tensor_size,
        ffn_part.reshape(blocks),
        ffn_back.reshape(blocks),
        chosen_t,
        expert_part,
        hidden,
        moe_rows.reshape(blocks),
        grad_out,
        layer_input,
        local_routes,
        local_residual,
        both_weight,
        const_value,
        moe_gain.reshape(1, model_width),
        attn_gain.reshape(1, model_width),
        q2,
        k2,
        v2,
        o2,
        lse,
        attn_rows.reshape(blocks),
        qkv_weight,
        out_double,
        jnp.asarray(np.concatenate([cosine[:, :HD], sine[:, HD:]], axis=1)),
    )
    if not reduced_inside(model_width // n_dp):

        def scattered(pairs):
            pairs = jnp.transpose(pairs, (2, 1, 3, 0, 4)).reshape(model_width, -1)
            return lax.psum_scatter(pairs, "dp", scatter_dimension=0, tiled=True).astype(
                jnp.float32
            )

        attn_sum_rows = scattered(attn_sum_rows)
        expert_sum = scattered(expert_part).reshape(
            model_width // n_dp, ffn_count, expert_part.shape[-1]
        )
        expert_sum = jnp.transpose(expert_sum, (1, 0, 2))
    gate_sum, up_sum, down_sum = tidy(expert_sum)
    wide = head_count * HD
    out_at = qkv_weight.shape[1]
    both_grad = small[8:24].T
    return (
        output,
        input_grad,
        gain[0],
        attn_sum_rows[:, :wide],
        attn_sum_rows[:, wide : 2 * wide],
        attn_sum_rows[:, 2 * wide : 3 * wide],
        attn_sum_rows[:, out_at : out_at + wide].T,
        small[0],
        both_grad[:, :route_count],
        jnp.transpose(both_grad[:, route_count : route_count + 4].reshape(model_width, 2, 2), (1, 0, 2)),
        small[1:3],
        gate_sum,
        up_sum,
        down_sum,
    )


def solution(mesh):
    in_specs = (
        P(("dp", "tensor"), None),
        P(),
        P(None, "tensor"),
        P(None, "tensor"),
        P(None, "tensor"),
        P("tensor", None),
        P(),
        P(),
        P("dp", None),
        P(),
        P(),
        P(None, None, "tensor"),
        P(None, None, "tensor"),
        P(None, "tensor", None),
        P("dp", None),
        P(("dp", "tensor"), None),
    )
    out_specs = (
        P(("dp", "tensor"), None),
        P(("dp", "tensor"), None),
        P(),
        P("dp", "tensor"),
        P("dp", "tensor"),
        P("dp", "tensor"),
        P("tensor", "dp"),
        P(),
        P(),
        P(),
        P(),
        P(None, "dp", "tensor"),
        P(None, "dp", "tensor"),
        P(None, "tensor", "dp"),
    )
    return jax.shard_map(
        on_device, mesh=mesh, in_specs=in_specs, out_specs=out_specs, check_vma=False
    )
```

```python
import functools
import math

import jax
import jax.numpy as jnp
import numpy as np
from jax import lax
from jax.experimental import pallas as pl
from jax.experimental.pallas import tpu as pltpu
from jax.sharding import PartitionSpec as P

HD = 64
LENGTH = 1024
BLOCK = 256
CAP = 256


EPSILON = 1e-06
MASKED = -1e30


EXP_PAD = 16


def dot(a, b):
    return jnp.dot(a, b, preferred_element_type=jnp.float32)


def dot_nt(a, b):
    return lax.dot_general(a, b, (((1,), (1,)), ((), ())), preferred_element_type=jnp.float32)


def dot_tn(a, b):
    return lax.dot_general(a, b, (((0,), (0,)), ((), ())), preferred_element_type=jnp.float32)


def three_parts(values):
    first = values.astype(jnp.bfloat16)
    rest = values - first.astype(jnp.float32)
    second = rest.astype(jnp.bfloat16)
    third = (rest - second.astype(jnp.float32)).astype(jnp.bfloat16)
    return (first, second, third)


def expert_kernel(
    n_dp,
    ffn_count,
    route_count,
    moe_ref,
    grad_ref,
    routes_ref,
    residual_ref,
    router_ref,
    gate_ref,
    up_ref,
    down_ref,
    part_ref,
    back_ref,
    chosen_ref,
    weight_ref,
    probs_s,
    rank_s,
    part_s,
    back_s,
):
    expert = pl.program_id(0)
    rows = moe_ref.shape[0]
    hidden = gate_ref.shape[2]
    step = moe_ref.shape[1] // n_dp

    @pl.when(expert == 0)
    def _():
        parts = three_parts(router_ref[...])
        logits = residual_ref[...]
        for part in parts:
            logits = logits + dot_nt(part, moe_ref[...])
        index = lax.broadcasted_iota(jnp.int32, (EXP_PAD, rows), 0)
        logits = jnp.where(index < route_count, logits, MASKED)
        top = jnp.max(logits, axis=0, keepdims=True)
        exps = jnp.exp(logits - top)
        probs_s[...] = exps / jnp.sum(exps, axis=0, keepdims=True)
        named = (routes_ref[0:1, :] == index) | (routes_ref[1:2, :] == index)
        named = jnp.where(named, 1.0, 0.0)
        width = 256
        before = lax.broadcasted_iota(jnp.int32, (width, width), 0)
        after = lax.broadcasted_iota(jnp.int32, (width, width), 1)
        earlier = jnp.where(before < after, 1.0, 0.0).astype(jnp.bfloat16)
        total = jnp.zeros((EXP_PAD, 1), jnp.float32)
        for start in range(0, rows, width):
            block = named[:, start : start + width]
            rank = dot(block.astype(jnp.bfloat16), earlier) + total
            rank_s[:, start : start + width] = jnp.where(block > 0.5, rank, -1.0)
            total = total + jnp.sum(block, axis=1, keepdims=True)
        part_s[...] = jnp.zeros_like(part_s)
        back_s[...] = jnp.zeros_like(back_s)

    slot = lax.broadcasted_iota(jnp.int32, (CAP, rows), 0).astype(jnp.float32)
    hit = rank_s[pl.ds(expert, 1), :] == slot
    dispatch = jnp.where(hit, 1.0, 0.0).astype(jnp.bfloat16)
    slot_weight = jnp.sum(
        jnp.where(hit, probs_s[pl.ds(expert, 1), :], 0.0), axis=1, keepdims=True
    )
    rows_in = dot(dispatch, moe_ref[...]).astype(jnp.bfloat16)
    rows_grad = dot(dispatch, grad_ref[...])
    gate_w = gate_ref[0]
    up_w = up_ref[0]
    down_w = down_ref[0]
    gate_pre = dot(rows_in, gate_w)
    up_pre = dot(rows_in, up_w)
    sigmoid = 1.0 / (1.0 + jnp.exp(-gate_pre))
    silu = gate_pre * sigmoid
    active = (silu * up_pre).astype(jnp.bfloat16)
    out = dot(active, down_w)
    inner = jnp.sum(rows_grad * out, axis=1, keepdims=True)
    chosen_row = jnp.sum(jnp.where(hit, inner, 0.0), axis=0, keepdims=True)
    for n in range(chosen_ref.shape[0]):
        chosen_ref[n, pl.ds(expert, 1), :] = chosen_row[
            :, n * chosen_ref.shape[2] : (n + 1) * chosen_ref.shape[2]
        ]
    part_s[...] += dot_tn(dispatch, (out * slot_weight).astype(jnp.bfloat16))
    grad_low = (rows_grad * slot_weight).astype(jnp.bfloat16)
    grad_active = dot_nt(grad_low, down_w)
    grad_gate = (grad_active * up_pre * sigmoid * (1.0 + gate_pre * (1.0 - sigmoid))).astype(
        jnp.bfloat16
    )
    grad_up = (grad_active * silu).astype(jnp.bfloat16)
    grad_in = dot_nt(grad_gate, gate_w) + dot_nt(grad_up, up_w)
    back_s[...] += dot_tn(dispatch, grad_in.astype(jnp.bfloat16))
    for n, (left, right) in enumerate(
        ((rows_in, grad_gate), (rows_in, grad_up), (grad_low, active))
    ):
        product = dot_tn(left, right).astype(jnp.bfloat16)
        for d in range(n_dp):
            weight_ref[0, d % 2, d // 2, :, n * hidden : (n + 1) * hidden] = product[
                d * step : (d + 1) * step
            ]

    @pl.when(expert == ffn_count - 1)
    def _():
        part_ref[...] = part_s[...].astype(jnp.bfloat16)
        back_ref[...] = back_s[...].astype(jnp.bfloat16)


def experts(n_dp, n_t, route_count, moe_rows, grad_rows, routes_t, residual_t, router_t, gate_w, up_w, down_w):
    rows, width = moe_rows.shape
    ffn_count, _, hidden = gate_w.shape
    step = width // n_dp

    def whole(shape):
        return pl.BlockSpec(shape, lambda e: (0,) * len(shape), pipeline_mode=pl.Buffered(1))

    return pl.pallas_call(
        functools.partial(expert_kernel, n_dp, ffn_count, route_count),
        grid=(ffn_count,),
        out_shape=(
            jax.ShapeDtypeStruct((rows, width), jnp.bfloat16),
            jax.ShapeDtypeStruct((rows, width), jnp.bfloat16),
            jax.ShapeDtypeStruct((n_t, ffn_count, rows // n_t), jnp.float32),
            jax.ShapeDtypeStruct((ffn_count, 2, n_dp // 2, step, 3 * hidden), jnp.bfloat16),
        ),
        in_specs=[
            whole((rows, width)),
            whole((rows, width)),
            whole((2, rows)),
            whole((EXP_PAD, rows)),
            whole((EXP_PAD, width)),
            pl.BlockSpec((1, width, hidden), lambda e: (e, 0, 0)),
            pl.BlockSpec((1, width, hidden), lambda e: (e, 0, 0)),
            pl.BlockSpec((1, hidden, width), lambda e: (e, 0, 0)),
        ],
        out_specs=(
            whole((rows, width)),
            whole((rows, width)),
            whole((n_t, ffn_count, rows // n_t)),
            pl.BlockSpec((1, 2, n_dp // 2, step, 3 * hidden), lambda e: (e, 0, 0, 0, 0)),
        ),
        scratch_shapes=[
            pltpu.VMEM((EXP_PAD, rows), jnp.float32),
            pltpu.VMEM((EXP_PAD, rows), jnp.float32),
            pltpu.VMEM((rows, width), jnp.float32),
            pltpu.VMEM((rows, width), jnp.float32),
        ],
        compiler_params=pltpu.CompilerParams(
            dimension_semantics=("arbitrary",), vmem_limit_bytes=48 << 20
        ),
        name="experts",
    )(moe_rows, grad_rows, routes_t, residual_t, router_t, gate_w, up_w, down_w)


MESH = pl.DeviceIdType.MESH


def bit_of(index, position):
    return index // (1 << position) % 2


def flipped(index, position):
    return index + (1 << position) * (1 - 2 * bit_of(index, position))


def log2_of(count):
    return count.bit_length() - 1


def greet(dp, place, dp_bits, tensor_count):
    barrier = pltpu.get_barrier_semaphore()
    for position in range(dp_bits):
        pl.semaphore_signal(
            barrier, inc=1, device_id={"dp": flipped(dp, position)}, device_id_type=MESH
        )
    for step in range(1, tensor_count):
        pl.semaphore_signal(
            barrier,
            inc=1,
            device_id={"tensor": (place + step) % tensor_count},
            device_id_type=MESH,
        )
    pl.semaphore_wait(barrier, dp_bits + tensor_count - 1)


class LineGather:
    def __init__(self, blocks, send, recv, place):
        self.blocks, self.send, self.recv, self.place = blocks, send, recv, place
        self.count = blocks.shape[0]

    def copy(self, block, way):
        return pltpu.make_async_remote_copy(
            src_ref=self.blocks.at[block],
            dst_ref=self.blocks.at[block],
            send_sem=self.send.at[way, block],
            recv_sem=self.recv.at[block],
            device_id={"tensor": self.place + 1 - 2 * way},
            device_id_type=MESH,
        )

    def start(self):
        self.pass_on(self.place)

    def pass_on(self, block, ways=(0, 1)):
        if 0 in ways:

            @pl.when(self.place < self.count - 1)
            def _():
                self.copy(block, 0).start()

        if 1 in ways:

            @pl.when(self.place > 0)
            def _():
                self.copy(block, 1).start()

    def step(self, distance):
        below, above = self.place - distance, self.place + distance

        @pl.when(below >= 0)
        def _():
            self.copy(below, 0).wait_recv()
            self.pass_on(below, (0,))

        @pl.when(above < self.count)
        def _():
            self.copy(above, 1).wait_recv()
            self.pass_on(above, (1,))

    def finish(self):
        for distance in range(self.count):
            below, above = self.place - distance, self.place + distance

            @pl.when((below >= 0) & (self.place < self.count - 1))
            def _(below=below):
                self.copy(below, 0).wait_send()

            @pl.when((above < self.count) & (self.place > 0))
            def _(above=above):
                self.copy(above, 1).wait_send()


class LineScatter:
    def __init__(self, parts, arrived, send, recv, place, pieces):
        self.parts, self.arrived, self.send, self.recv = parts, arrived, send, recv
        self.place, self.count, self.pieces = place, parts.shape[0], pieces
        self.rows = parts.shape[1] // pieces

    def piece(self, ref, block, n):
        return ref.at[block, pl.ds(n * self.rows, self.rows)]

    def copy(self, block, n, way, own=False):
        there = self.piece(self.arrived, block + 1 - way, n)
        return pltpu.make_async_remote_copy(
            src_ref=self.piece(self.parts, block, n) if own else there,
            dst_ref=there,
            send_sem=self.send.at[way, block, n],
            recv_sem=self.recv.at[way, block, n],
            device_id={"tensor": self.place + 1 - 2 * way},
            device_id_type=MESH,
        )

    def originate(self, block):
        for way, first in ((0, 0), (1, self.count - 1)):
            if block != first:

                @pl.when(self.place == first)
                def _(way=way):
                    for n in range(self.pieces):
                        self.copy(block, n, way, own=True).start()

    def forward(self, block):
        for way in (0, 1):
            inside = (
                (self.place > 0) & (self.place < block)
                if way == 0
                else (self.place > block) & (self.place < self.count - 1)
            )

            @pl.when(inside)
            def _(way=way):
                for n in range(self.pieces):
                    self.copy(block, n, way).wait_recv()
                    there = self.piece(self.arrived, block + 1 - way, n)
                    mine = self.piece(self.parts, block, n)
                    there[...] = (
                        there[...].astype(jnp.float32) + mine[...].astype(jnp.float32)
                    ).astype(there.dtype)
                    self.copy(block, n, way).start()

    def collect(self, total):
        place = self.place
        total[...] = self.parts[place].astype(jnp.float32)
        for way in (0, 1):

            @pl.when(place > 0 if way == 0 else place < self.count - 1)
            def _(way=way):
                for n in range(self.pieces):
                    self.copy(place, n, way).wait_recv()
                    rows = pl.ds(n * self.rows, self.rows)
                    total[rows, :] += self.arrived[place + 1 - way, rows, :].astype(jnp.float32)

    def finish(self):
        for block in range(self.count):
            for way in (0, 1):

                @pl.when(self.place < block if way == 0 else self.place > block)
                def _(block=block, way=way):
                    for n in range(self.pieces):
                        self.copy(block, n, way).wait_send()


class Halving:
    def __init__(self, source, kept, first, stages, sems, dp, dp_bits, splits):
        self.source, self.kept, self.first, self.stages = source, kept, first, stages
        self.first_send, self.first_recv, self.local, self.send, self.recv = sems
        self.dp, self.bits, self.splits = dp, dp_bits, splits
        self.core = bit_of(dp, 0)
        upper = list(range(dp_bits - 1))
        self.orders = (upper, upper[1:] + upper[:1])

    def first_copy(self, e):
        return pltpu.make_async_remote_copy(
            src_ref=self.source.at[e, 1 - self.core],
            dst_ref=self.first.at[e],
            send_sem=self.first_send.at[e],
            recv_sem=self.first_recv.at[e],
            device_id={"dp": flipped(self.dp, 0)},
            device_id_type=MESH,
        )

    def local_copy(self, e):
        return pltpu.make_async_copy(
            self.source.at[e, self.core], self.kept.at[e], self.local.at[e]
        )

    def blocks(self, part, stage, k, mine):
        order = self.orders[part]
        index = 0
        for done in order[:stage]:
            index = index + (1 << done) * bit_of(self.dp, done + 1)
        here = bit_of(self.dp, order[stage] + 1)
        index = index + (1 << order[stage]) * (here if mine else 1 - here)
        for n, free in enumerate(order[stage + 1 :]):
            index = index + (1 << free) * (k // (1 << n) % 2)
        return index

    def width(self, part):
        return pl.ds(*self.splits[part])

    def stage_copy(self, e, part, stage, k):
        start, size = self.splits[part]
        return pltpu.make_async_remote_copy(
            src_ref=self.kept.at[e, self.blocks(part, stage, k, False), :, pl.ds(start, size)],
            dst_ref=self.stages[stage].at[e, k, :, pl.ds(start, size)],
            send_sem=self.send[stage].at[e, part, k],
            recv_sem=self.recv[stage].at[e, part, k],
            device_id={"dp": flipped(self.dp, self.orders[part][stage] + 1)},
            device_id_type=MESH,
        )

    def number(self, stage):
        return 1 << (self.bits - 2 - stage)

    def start(self, e):
        self.first_copy(e).start()
        self.local_copy(e).start()

    def send_stage(self, e, stage):
        for k in range(self.number(stage)):
            for part in (0, 1):
                self.stage_copy(e, part, stage, k).start()

    def add_rows(self, target, addend):
        rows = target.shape[0]
        step = 32 if rows % 32 == 0 else rows

        def body(n, _):
            at = pl.ds(pl.multiple_of(n * step, step), step)
            target[at, :] = (
                target[at, :].astype(jnp.float32) + addend[at, :].astype(jnp.float32)
            ).astype(target.dtype)
            return 0

        lax.fori_loop(0, rows // step, body, 0)

    def open(self, e, remote_only=False):
        self.first_copy(e).wait_recv()
        if not remote_only:
            self.local_copy(e).wait()
        for block in range(self.kept.shape[1]):
            self.add_rows(self.kept.at[e, block], self.first.at[e, block])
        self.send_stage(e, 0)

    def advance(self, e, stage):
        for k in range(self.number(stage)):
            for part in (0, 1):
                self.stage_copy(e, part, stage, k).wait_recv()
                block = self.blocks(part, stage, k, True)
                self.add_rows(
                    self.kept.at[e, block, :, self.width(part)],
                    self.stages[stage].at[e, k, :, self.width(part)],
                )
        self.send_stage(e, stage + 1)

    def close(self, e, out):
        stage = self.bits - 2
        for part in (0, 1):
            self.stage_copy(e, part, stage, 0).wait_recv()
            block = self.blocks(part, stage, 0, True)
            columns = self.width(part)
            out[:, columns] = self.kept[e, block, :, columns].astype(jnp.float32) + self.stages[
                stage
            ][e, 0, :, columns].astype(jnp.float32)

    def finish(self, e):
        self.first_copy(e).wait_send()
        for stage in range(self.bits - 1):
            for k in range(self.number(stage)):
                for part in (0, 1):
                    self.stage_copy(e, part, stage, k).wait_send()


class Butterfly:
    def __init__(self, total, arrived, send, recv, dp, place, dp_bits, tensor_bits):
        self.total, self.arrived, self.send, self.recv = total, arrived, send, recv
        self.partners = [{"dp": flipped(dp, b)} for b in range(dp_bits)]
        self.partners += [{"tensor": flipped(place, b)} for b in range(tensor_bits)]

    def copy(self, n):
        return pltpu.make_async_remote_copy(
            src_ref=self.total,
            dst_ref=self.arrived.at[n],
            send_sem=self.send.at[n],
            recv_sem=self.recv.at[n],
            device_id=self.partners[n],
            device_id_type=MESH,
        )

    def start(self, n):
        self.copy(n).start()

    def take(self, n):
        self.copy(n).wait()
        self.total[...] += self.arrived[n]


def select_lanes(rows, columns, source):
    row = lax.broadcasted_iota(jnp.int32, (rows, columns), 0)
    column = lax.broadcasted_iota(jnp.int32, (rows, columns), 1)
    return jnp.where(row == source(column), 1.0, 0.0).astype(jnp.bfloat16)


def forward_kernel(
    n_t,
    input_ref,
    attn_gain_ref,
    moe_gain_ref,
    q_w_ref,
    k_w_ref,
    v_w_ref,
    out_w_ref,
    grad_ref,
    cos_ref,
    sin_ref,
    q_out,
    k_out,
    v_out,
    o_out,
    lse_out,
    rows_out,
    moe_out,
    grad_out,
    hidden_out,
    qkv_out,
    double_out,
    weights,
    part,
    arrived,
    acc,
    rows_send,
    rows_recv,
    grad_send,
    grad_recv,
    moe_send,
    moe_recv,
    line_send,
    line_recv,
):
    place = lax.axis_index("tensor")
    heads = q_out.shape[0]
    local, width = input_ref.shape
    barrier = pltpu.get_barrier_semaphore()
    for step in range(1, n_t):
        pl.semaphore_signal(
            barrier,
            inc=1,
            device_id={"tensor": (place + step) % n_t},
            device_id_type=MESH,
        )
    wide = input_ref[...].astype(jnp.float32)
    scale = lax.rsqrt(jnp.mean(wide * wide, axis=1, keepdims=True) + EPSILON)
    rows_out[place] = (wide * scale * attn_gain_ref[...]).astype(jnp.bfloat16)
    grad_out[place] = grad_ref[...]
    pl.semaphore_wait(barrier, n_t - 1)

    rows_gather = LineGather(rows_out, rows_send, rows_recv, place)
    grad_gather = LineGather(grad_out, grad_send, grad_recv, place)
    moe_gather = LineGather(moe_out, moe_send, moe_recv, place)
    line = LineScatter(part, arrived, line_send, line_recv, place, 4)
    rows_gather.start()

    columns = heads * HD
    twice = select_lanes(columns, heads * 128, lambda c: c // 128 * HD + c % HD)
    swapped = select_lanes(
        columns,
        heads * 128,
        lambda c: c // 128 * HD + (c % HD + c % 128 // HD * (HD // 2)) % HD,
    )
    for n, (ref, lanes) in enumerate(
        ((q_w_ref, swapped), (k_w_ref, swapped), (v_w_ref, twice))
    ):
        weights[:, n * heads * 128 : (n + 1) * heads * 128] = dot(ref[...], lanes).astype(
            jnp.bfloat16
        )
    joined = jnp.zeros(qkv_out.shape, jnp.float32)
    for n, ref in enumerate((q_w_ref, k_w_ref, v_w_ref)):
        lanes = select_lanes(columns, qkv_out.shape[1], lambda c, n=n: c - n * columns)
        joined = joined + dot(ref[...], lanes)
    qkv_out[...] = joined.astype(jnp.bfloat16)
    double_out[...] = dot_tn(twice, out_w_ref[...]).astype(jnp.bfloat16)

    def project(block):
        at = pl.ds(pl.multiple_of(block * local, local), local)
        product = dot(rows_out[block], weights[...])
        cosine, sine = cos_ref[at, :], sin_ref[at, :]
        for n, target in enumerate((q_out, k_out, v_out)):
            for h in range(heads):
                start = (n * heads + h) * 128
                piece = product[:, start : start + 128]
                if n < 2:
                    piece = piece * cosine + pltpu.roll(piece, 64, 1) * sine
                target[h, at, :] = piece.astype(jnp.bfloat16)

    def arrive(distance, _):
        @pl.when(distance > 0)
        def _():
            rows_gather.step(distance)

        def side(way, _):
            block = place + (2 * way - 1) * distance

            @pl.when((block >= 0) & (block < n_t) & ((distance > 0) | (way == 0)))
            def _():
                project(block)

            return 0

        lax.fori_loop(0, 2, side, 0)
        return 0

    lax.fori_loop(0, n_t, arrive, 0)
    grad_gather.start()

    factor = 0.5 * HD ** (-0.5)

    lse_out[...] = jnp.zeros_like(lse_out)

    def attend(block):
        at = slice(block * local, (block + 1) * local)
        seen = (block + 1) * local
        mixed = []
        for h in range(heads):
            scores = dot_nt(q_out[h, at, :], k_out[h, 0:seen, :]) * factor
            top = jnp.max(scores, axis=1, keepdims=True)
            exps = jnp.exp(scores - top)
            total = jnp.sum(exps, axis=1, keepdims=True)
            probs = (exps / total).astype(jnp.bfloat16)
            out = dot(probs, v_out[h, 0:seen, :]).astype(jnp.bfloat16)
            o_out[h, at, :] = out
            mixed.append(out)
            log_total = jnp.broadcast_to(top + jnp.log(total), (local, 128))
            lse_out[h : h + 1, at] = log_total.T[0:1, :]
        mixed = jnp.concatenate(mixed, axis=1)
        part[block] = (0.5 * dot(mixed, double_out[...])).astype(jnp.bfloat16)

    order = (*range(1, n_t), 0)
    for n, block in enumerate(order):
        attend(block)
        line.originate(block)
        if n > 0:
            grad_gather.step(n)
            line.forward(order[n - 1])
    line.forward(order[-1])
    line.collect(acc)
    hidden = input_ref[...].astype(jnp.float32) + acc[...]
    hidden_out[...] = hidden
    scale = lax.rsqrt(jnp.mean(hidden * hidden, axis=1, keepdims=True) + EPSILON)
    moe_out[place] = (hidden * scale * moe_gain_ref[...]).astype(jnp.bfloat16)
    moe_gather.start()
    for step in range(1, n_t):
        moe_gather.step(step)
    for exchange in (rows_gather, grad_gather, moe_gather, line):
        exchange.finish()


def forward(n_t, layer_input, attn_gain, moe_gain, q_w, k_w, v_w, out_w, grad_out, cosine, sine):
    local, width = layer_input.shape
    group = local * n_t
    heads = q_w.shape[1] // HD
    bf, f32 = jnp.bfloat16, jnp.float32
    dma = pltpu.SemaphoreType.DMA
    vmem = pl.BlockSpec(memory_space=pltpu.VMEM)
    blocks = (n_t, local, width)
    qkv_width = -(-3 * heads * HD // 128) * 128
    outs = (
        *[jax.ShapeDtypeStruct((heads, group, 128), bf)] * 4,
        jax.ShapeDtypeStruct((8, group), f32),
        *[jax.ShapeDtypeStruct(blocks, bf)] * 3,
        jax.ShapeDtypeStruct((local, width), f32),
        jax.ShapeDtypeStruct((width, qkv_width), bf),
        jax.ShapeDtypeStruct((heads * 128, width), bf),
    )
    return pl.pallas_call(
        functools.partial(forward_kernel, n_t),
        out_shape=outs,
        in_specs=[vmem] * 10,
        out_specs=(vmem,) * len(outs),
        scratch_shapes=[
            pltpu.VMEM((width, 3 * heads * 128), bf),
            pltpu.VMEM(blocks, bf),
            pltpu.VMEM((n_t + 1, local, width), bf),
            pltpu.VMEM((local, width), f32),
            *[s for _ in range(3) for s in (dma((2, n_t)), dma((n_t,)))],
            dma((2, n_t, 4)),
            dma((2, n_t, 4)),
        ],
        compiler_params=pltpu.CompilerParams(
            collective_id=2, has_side_effects=True, vmem_limit_bytes=56 << 20
        ),
        name="forward",
    )(layer_input, attn_gain, moe_gain, q_w, k_w, v_w, out_w, grad_out, cosine, sine)


def side_forward(norm, named, residual, weight_parts, const_value, route_count, ffn_count):
    lane = lax.broadcasted_iota(jnp.int32, named.shape, 1)
    low = norm.astype(jnp.bfloat16)
    both = dot(low, weight_parts[0]) + dot(low, weight_parts[1]) + dot(low, weight_parts[2])
    logits = jnp.where(lane < route_count, both + residual, MASKED)
    exps = jnp.exp(logits - jnp.max(logits, axis=1, keepdims=True))
    probs = exps / jnp.sum(exps, axis=1, keepdims=True)
    chosen = probs * named
    shares, keeps, rests = [], chosen[:, ffn_count + 1 : ffn_count + 2], []
    for c in range(2):
        at = route_count + 2 * c
        share = 1.0 / (1.0 + jnp.exp(both[:, at + 1 : at + 2] - both[:, at : at + 1]))
        weight = chosen[:, ffn_count + 2 + c : ffn_count + 3 + c]
        shares.append(share)
        keeps = keeps + weight * share
        rests.append(weight * (1.0 - share))
    special = keeps * norm + rests[0] * const_value[0:1] + rests[1] * const_value[1:2]
    return probs, chosen, shares, keeps, rests, special


def side_backward(
    norm, grad, named, forward, chosen_back, weight_parts, const_value, route_count, ffn_count
):
    probs, chosen, shares, keeps, rests, _ = forward
    lane = lax.broadcasted_iota(jnp.int32, named.shape, 1)
    self_dot = jnp.sum(grad * norm, axis=1, keepdims=True)
    value_dots = [
        jnp.sum(grad * const_value[c : c + 1], axis=1, keepdims=True) for c in range(2)
    ]
    d_probs = jnp.where(lane < ffn_count, chosen_back, 0.0)
    d_probs = jnp.where(lane == ffn_count + 1, self_dot, d_probs)
    for c in range(2):
        mixed = shares[c] * self_dot + (1.0 - shares[c]) * value_dots[c]
        d_probs = jnp.where(lane == ffn_count + 2 + c, mixed, d_probs)
    d_probs = d_probs * named
    d_both = probs * (d_probs - jnp.sum(probs * d_probs, axis=1, keepdims=True))
    d_both = jnp.where(lane < route_count, d_both, 0.0)
    for c in range(2):
        weight = chosen[:, ffn_count + 2 + c : ffn_count + 3 + c]
        d_share = shares[c] * (1.0 - shares[c]) * weight * (self_dot - value_dots[c])
        d_both = jnp.where(lane == route_count + 2 * c, d_share, d_both)
        d_both = jnp.where(lane == route_count + 2 * c + 1, -d_share, d_both)
    d_parts = three_parts(d_both)
    back = keeps * grad
    for m, n in ((0, 0), (0, 1), (1, 0), (1, 1)):
        back = back + dot_nt(d_parts[m], weight_parts[n])
    low = norm.astype(jnp.bfloat16)
    weight_part = dot_tn(d_parts[0], low) + dot_tn(d_parts[1], low) + dot_tn(d_parts[2], low)
    value_part = [jnp.sum(rests[c] * grad, axis=0, keepdims=True) for c in range(2)]
    return back, weight_part, value_part


class Nothing:
    def __getattr__(self, name):
        return lambda *arguments: None


def reduced_inside(step):
    return step % 32 == 0


def backward_kernel(
    sizes,
    part_ref,
    back_ref,
    chosen_ref,
    expert_ref,
    hidden_ref,
    moe_ref,
    grad_ref,
    input_ref,
    routes_ref,
    residual_ref,
    both_ref,
    value_ref,
    moe_gain_ref,
    attn_gain_ref,
    q_ref,
    k_ref,
    v_ref,
    o_ref,
    lse_ref,
    rows_ref,
    qkv_ref,
    out_w_ref,
    table_ref,
    output_ref,
    input_grad_ref,
    expert_out,
    attn_out,
    small_out,
    gain_out,
    chosen_in,
    pair_buf,
    line_back,
    line_part,
    staged,
    grad_rows,
    attn_part,
    acc,
    hidden_grad,
    double_grad,
    delta,
    dq,
    dk,
    dv,
    packed,
    *rest,
):
    dp_bits, n_t, ffn_count, route_count, attn_split, inside = sizes
    stage_count = dp_bits - 1 if inside else 0
    if inside:
        attn_pairs, kept, first = rest[:3]
        stages = rest[3 : 3 + stage_count]
        rest = rest[3 + stage_count :]
        a_kept, a_first = rest[:2]
        a_stages = rest[2 : 2 + stage_count]
        rest = rest[2 + stage_count :]
    else:
        attn_pairs = attn_out
    small_in, gain_acc, gain_in = rest[:3]
    rest = list(rest[3:])

    def sems(count):
        taken = rest[:count]
        del rest[:count]
        return taken

    (chosen_send, chosen_recv, gather_send, gather_recv) = sems(4)
    line_sems = [sems(2) for _ in range(3)]
    if inside:
        e_sems = sems(3) + [sems(stage_count), sems(stage_count)]
        a_sems = sems(3) + [sems(stage_count), sems(stage_count)]
    small_sems = sems(2)
    gain_sems = sems(2)
    (staged_sem,) = sems(1)

    dp = lax.axis_index("dp")
    place = lax.axis_index("tensor")
    local = hidden_ref.shape[0]
    width = hidden_ref.shape[1]
    hidden_units = expert_ref.shape[-1]
    heads = q_ref.shape[0]
    tensor_bits = log2_of(n_t)
    greet(dp, place, dp_bits, n_t)

    back_line = LineScatter(back_ref, line_back, *line_sems[0], place, 2)
    part_line = LineScatter(part_ref, line_part, *line_sems[1], place, 2)
    attn_line = LineScatter(attn_part, line_back, *line_sems[2], place, 4)
    gather = LineGather(grad_rows, gather_send, gather_recv, place)
    half = hidden_units // 2
    attn_width = attn_pairs.shape[-1]
    expert = attn = Nothing()
    if inside:
        splits = ((0, half), (half, half))
        expert = Halving(expert_ref, kept, first, stages, e_sems, dp, dp_bits, splits)
        splits = ((0, attn_split), (attn_split, attn_width - attn_split))
        attn = Halving(attn_pairs, a_kept, a_first, a_stages, a_sems, dp, dp_bits, splits)
    small = Butterfly(small_out, small_in, *small_sems, dp, place, dp_bits, tensor_bits)
    gain = Butterfly(gain_acc, gain_in, *gain_sems, dp, place, dp_bits, tensor_bits)

    def chosen_copy(step):
        there = (place + step) % n_t
        return pltpu.make_async_remote_copy(
            src_ref=chosen_ref.at[there],
            dst_ref=chosen_in.at[step - 1],
            send_sem=chosen_send.at[step - 1],
            recv_sem=chosen_recv.at[step - 1],
            device_id={"tensor": there},
            device_id_type=MESH,
        )

    for block in (n_t - 1, 0, *range(n_t - 2, 0, -1)):
        back_line.originate(block)
    for step in range(1, n_t):
        chosen_copy(step).start()

    def begin(e, _):
        expert.start(e)
        return 0

    lax.fori_loop(0, ffn_count, begin, 0)

    norm = moe_ref[place].astype(jnp.float32)
    lane = lax.broadcasted_iota(jnp.int32, (local, 128), 1)
    routes = routes_ref[...]
    named = (routes[:, 0:1] == lane) | (routes[:, 1:2] == lane)
    named = jnp.where(named, 1.0, 0.0)
    residual = jnp.concatenate(
        [residual_ref[...], jnp.zeros((local, 128 - route_count), jnp.float32)], axis=1
    )
    weight_parts = three_parts(both_ref[...])
    const_value = value_ref[...]
    grad = grad_ref[...].astype(jnp.float32)
    forward = side_forward(
        norm, named, residual, weight_parts, const_value, route_count, ffn_count
    )
    hidden = hidden_ref[...]
    pair_buf[...] = hidden + forward[-1]

    for block in (n_t - 1, 0, *range(n_t - 2, 0, -1)):
        back_line.forward(block)
    for block in (n_t - 1, 0, *range(n_t - 2, 0, -1)):
        part_line.originate(block)

    def opened(e, _):
        expert.open(e)
        return 0

    lax.fori_loop(0, ffn_count, opened, 0)

    back_line.collect(acc)
    chosen_total = chosen_ref[place]
    for step in range(1, n_t):
        chosen_copy(step).wait_recv()
        chosen_total = chosen_total + chosen_in[step - 1]
    chosen_back = jnp.concatenate(
        [chosen_total, jnp.zeros((128 - ffn_count, local), jnp.float32)], axis=0
    ).T
    back, weight_part, value_part = side_backward(
        norm, grad, named, forward, chosen_back, weight_parts, const_value, route_count, ffn_count
    )
    norm_grad = acc[...] + back
    scale = lax.rsqrt(jnp.mean(hidden * hidden, axis=1, keepdims=True) + EPSILON)
    u = norm_grad * moe_gain_ref[...]
    small_out[0:1, :] = jnp.sum(norm_grad * hidden * scale, axis=0, keepdims=True)
    small_out[1:2, :] = value_part[0]
    small_out[2:3, :] = value_part[1]
    small_out[3:8, :] = jnp.zeros((5, width), jnp.float32)
    small_out[8:24, :] = weight_part[0:16]
    hidden_grad[...] = (
        grad + scale * u - hidden * (scale * scale * scale) * jnp.mean(u * hidden, axis=1, keepdims=True)
    )
    grad_rows[place] = hidden_grad[...].astype(jnp.bfloat16)
    back_line.finish()
    gather.start()
    small.start(0)
    for block in (n_t - 1, 0, *range(n_t - 2, 0, -1)):
        part_line.forward(block)
    for step in range(1, n_t):
        gather.step(step)
        if step < small_in.shape[0]:
            small.take(step - 1)
            small.start(step)

    rows = local

    def row_block(n):
        return pl.ds(pl.multiple_of(n * rows, rows), rows)

    count = n_t
    head_lane = lax.broadcasted_iota(jnp.int32, (rows, 128), 1)
    low_half = head_lane < 64
    for block in range(count):
        at = pl.ds(block * rows, rows)
        product = dot_nt(grad_rows[block], out_w_ref[...])
        for h in range(heads):
            piece = product[:, h * 128 : (h + 1) * 128].astype(jnp.bfloat16)
            double_grad[h, at, :] = piece
            both = piece.astype(jnp.float32) * o_ref[h, at, :].astype(jnp.float32)
            delta[h : h + 1, at] = 0.5 * jnp.sum(both.T, axis=0, keepdims=True)
    out_pack = []
    for h in range(0, heads, 2):
        o_a = o_ref[h]
        o_b = o_ref[h + 1] if h + 1 < heads else jnp.zeros_like(o_a)
        lanes = lax.broadcasted_iota(jnp.int32, o_a.shape, 1)
        out_pack.append(jnp.where(lanes < 64, o_a, o_b))
    n_half = attn_pairs.shape[2]
    step_rows = attn_pairs.shape[3]
    qkv_width = packed.shape[1]

    def spread(product, start, stop):
        low = product.astype(jnp.bfloat16)
        for d in range(2 * n_half):
            attn_pairs[0, d % 2, d // 2, :, start:stop] = low[d * step_rows : (d + 1) * step_rows]

    for n, pack in enumerate(out_pack):
        total = jnp.zeros((width, 128), jnp.float32)
        for block in range(count):
            total = total + dot_tn(grad_rows[block], pack[block * rows : (block + 1) * rows])
        spread(total, qkv_width + n * 128, qkv_width + (n + 1) * 128)

    def advance_all(stage):
        def body(e, _):
            expert.advance(e, stage)
            return 0

        lax.fori_loop(0, ffn_count, body, 0)

    dq[...] = jnp.zeros_like(dq)
    factor = 64 ** (-0.5)
    gain_total = jnp.zeros((1, width), jnp.float32)
    for key_block in range(count):
        keys = pl.ds(key_block * rows, rows)
        dk[...] = jnp.zeros_like(dk)
        dv[...] = jnp.zeros_like(dv)

        def query_step(query_block, _, keys=keys):
            at = row_block(query_block)
            for h in range(heads):
                q, g = q_ref[h, at, :], double_grad[h, at, :]
                k, v = k_ref[h, keys, :], v_ref[h, keys, :]
                scores = dot_nt(k, q) * (0.5 * factor)
                probs = jnp.exp(scores - lse_ref[h : h + 1, at])
                d_probs = dot_nt(v, g) * 0.5
                d_scores = (probs * (d_probs - delta[h : h + 1, at])).astype(jnp.bfloat16)
                dk[h] += dot(d_scores, q)
                dv[h] += dot(probs.astype(jnp.bfloat16), g)
                dq[h, at, :] += dot_tn(d_scores, k)
            return 0

        lax.fori_loop(key_block, count, query_step, 0)
        table = table_ref[keys, :]
        pieces = []
        for source in (dq.at[:, keys, :], dk):
            for h in range(heads):
                turned = source[h] * (table * factor)
                pieces.append(turned + pltpu.roll(turned, 64, 1))
        for h in range(heads):
            pieces.append(dv[h])
        if len(pieces) % 2:
            pieces.append(jnp.zeros((rows, 128), jnp.float32))
        for n in range(0, len(pieces), 2):
            packed[keys, n * 64 : n * 64 + 128] = jnp.where(
                low_half, pieces[n], pieces[n + 1]
            ).astype(jnp.bfloat16)
        back_rows = dot_nt(packed[keys, :], qkv_ref[...])
        gain_total = gain_total + jnp.sum(
            back_rows * rows_ref[key_block].astype(jnp.float32), axis=0, keepdims=True
        )
        attn_part[key_block] = back_rows.astype(jnp.bfloat16)
        attn_line.originate(key_block)
        if key_block > 0:
            attn_line.forward(key_block - 1)
        if key_block == 0:
            part_line.collect(acc)
            output_ref[...] = (pair_buf[...] + acc[...]).astype(output_ref.dtype)

    gain_acc[...] = jnp.broadcast_to(gain_total / attn_gain_ref[...], gain_acc.shape)
    gain.start(0)
    for n in range(qkv_width // 128):
        total = jnp.zeros((width, 128), jnp.float32)
        for block in range(count):
            total = total + dot_tn(
                rows_ref[block], packed[pl.ds(block * rows, rows), n * 128 : (n + 1) * 128]
            )
        spread(total, n * 128, (n + 1) * 128)
    attn.start(0)
    attn_line.forward(count - 1)
    gain.take(0)
    gain.start(1)
    attn.open(0)
    for stage in range(stage_count - 1):
        advance_all(stage)
        attn.advance(0, stage)
    for n in range(1, gain_in.shape[0]):
        gain.take(n)
        if n + 1 < gain_in.shape[0]:
            gain.start(n + 1)
    for n in range(n_t - 1, small_in.shape[0]):
        small.take(n)
        if n + 1 < small_in.shape[0]:
            small.start(n + 1)
    gain_out[...] = gain_acc[...]
    attn_line.collect(acc)
    wide = input_ref[...].astype(jnp.float32)
    scale = lax.rsqrt(jnp.mean(wide * wide, axis=1, keepdims=True) + EPSILON)
    w = acc[...] * attn_gain_ref[...]
    input_grad_ref[...] = (
        hidden_grad[...]
        + scale * w
        - wide * (scale * scale * scale) * jnp.mean(w * wide, axis=1, keepdims=True)
    ).astype(input_grad_ref.dtype)
    def stored(e):
        return pltpu.make_async_copy(staged.at[e % 2], expert_out.at[e], staged_sem.at[e])

    for e in range(ffn_count if inside else 0):
        if e > 1:
            stored(e - 2).wait()
        expert.close(e, staged.at[e % 2])
        stored(e).start()
    attn.close(0, attn_out)

    for line in (part_line, attn_line):
        line.finish()
    for step in range(1, n_t):
        chosen_copy(step).wait_send()
    gather.finish()

    def ended(e, _):
        expert.finish(e)
        return 0

    lax.fori_loop(0, ffn_count, ended, 0)
    attn.finish(0)
    for e in range(ffn_count - 2, ffn_count if inside else 0):
        stored(e).wait()


def backward(dp_count, n_t, ffn_part, ffn_back, chosen, expert_part, hidden, moe_rows, grad_out,
             layer_input, routes, residual, both_weight, const_value, moe_gain, attn_gain,
             q2, k2, v2, o2, lse, attn_rows, qkv_weight, out_double, table):
    local, width = hidden.shape
    group = local * n_t
    ffn_count = expert_part.shape[0]
    units = expert_part.shape[-1]
    step = width // dp_count
    half = dp_count // 2
    dp_bits = log2_of(dp_count)
    inside = reduced_inside(step)
    stage_count = dp_bits - 1 if inside else 0
    tensor_bits = log2_of(n_t)
    heads = q2.shape[0]
    qkv_width = qkv_weight.shape[1]
    attn_width = qkv_width + -(-heads // 2) * 128
    attn_split = attn_width // 2 // 128 * 128
    bf, f32 = jnp.bfloat16, jnp.float32
    dma = pltpu.SemaphoreType.DMA
    rounds = dp_bits + tensor_bits

    def numbers(stage):
        return half >> (stage + 1)

    def line(rows_shape):
        return pltpu.VMEM((n_t + 1, *rows_shape[1:]), bf)

    block_shape = (n_t, local, width)
    reduction = []
    if inside:
        reduction = [
            pltpu.VMEM((1, 2, half, step, attn_width), bf),
            pltpu.VMEM((ffn_count, half, step, units), bf),
            pltpu.VMEM((ffn_count, half, step, units), bf),
            *[pltpu.VMEM((ffn_count, numbers(s), step, units), bf) for s in range(stage_count)],
            pltpu.VMEM((1, half, step, attn_width), bf),
            pltpu.VMEM((1, half, step, attn_width), bf),
            *[pltpu.VMEM((1, numbers(s), step, attn_width), bf) for s in range(stage_count)],
        ]
    scratch = [
        pltpu.VMEM((n_t - 1, ffn_count, local), f32),
        pltpu.VMEM((local, width), f32),
        line(block_shape),
        line(block_shape),
        pltpu.VMEM((2, step, units), f32),
        pltpu.VMEM(block_shape, bf),
        pltpu.VMEM(block_shape, bf),
        pltpu.VMEM((local, width), f32),
        pltpu.VMEM((local, width), f32),
        pltpu.VMEM((heads, group, 128), bf),
        pltpu.VMEM((8, group), f32),
        pltpu.VMEM((heads, group, 128), f32),
        pltpu.VMEM((heads, local, 128), f32),
        pltpu.VMEM((heads, local, 128), f32),
        pltpu.VMEM((group, qkv_width), bf),
        *reduction,
        pltpu.VMEM((rounds, 24, width), f32),
        pltpu.VMEM((8, width), f32),
        pltpu.VMEM((rounds, 8, width), f32),
        dma((n_t - 1,)),
        dma((n_t - 1,)),
        dma((2, n_t)),
        dma((n_t,)),
        dma((2, n_t, 2)),
        dma((2, n_t, 2)),
        dma((2, n_t, 2)),
        dma((2, n_t, 2)),
        dma((2, n_t, 4)),
        dma((2, n_t, 4)),
        *[
            s
            for n in ((ffn_count, 1) if inside else ())
            for s in (
                dma((n,)),
                dma((n,)),
                dma((n,)),
                *[dma((n, 2, numbers(s))) for s in range(stage_count)],
                *[dma((n, 2, numbers(s))) for s in range(stage_count)],
            )
        ],
        dma((rounds,)),
        dma((rounds,)),
        dma((rounds,)),
        dma((rounds,)),
        dma((ffn_count,)),
    ]
    vmem = pl.BlockSpec(memory_space=pltpu.VMEM)
    operands = (ffn_part, ffn_back, chosen, expert_part, hidden, moe_rows, grad_out, layer_input,
                routes, residual, both_weight, const_value, moe_gain, attn_gain, q2, k2, v2, o2,
                lse, attn_rows, qkv_weight, out_double, table)
    specs = [vmem] * len(operands)
    specs[3] = pl.BlockSpec(memory_space=pl.ANY)
    return pl.pallas_call(
        functools.partial(
            backward_kernel, (dp_bits, n_t, ffn_count, residual.shape[1], attn_split, inside)
        ),
        out_shape=(
            jax.ShapeDtypeStruct((local, width), bf),
            jax.ShapeDtypeStruct((local, width), bf),
            jax.ShapeDtypeStruct((ffn_count, step, units) if inside else (8, 128), f32),
            jax.ShapeDtypeStruct((step, attn_width), f32)
            if inside
            else jax.ShapeDtypeStruct((1, 2, half, step, attn_width), bf),
            jax.ShapeDtypeStruct((24, width), f32),
            jax.ShapeDtypeStruct((8, width), f32),
        ),
        in_specs=specs,
        out_specs=(vmem, vmem, pl.BlockSpec(memory_space=pl.ANY), vmem, vmem, vmem),
        scratch_shapes=scratch,
        compiler_params=pltpu.CompilerParams(
            collective_id=1, has_side_effects=True, vmem_limit_bytes=62 << 20
        ),
        name="backward",
    )(*operands)


def rope_lanes(length, head_width):
    position = np.arange(length, dtype=np.float64)[:, None]
    inverse = np.exp(np.arange(head_width // 2) * (-2.0 * math.log(10000.0) / head_width))
    angle = position * inverse[None, :]
    c, s = np.cos(angle), np.sin(angle)
    cosine = np.concatenate([c, c, c, c], axis=1).astype(np.float32)
    sine = np.concatenate([-s, s, s, -s], axis=1).astype(np.float32)
    return cosine, sine


def tidy_kernel(route_count, expert_ref, gate_out, up_out, down_out):
    units = gate_out.shape[2]
    gate_out[...] = expert_ref[:, :, 0:units]
    up_out[...] = expert_ref[:, :, units : 2 * units]
    down_out[0] = expert_ref[0, :, 2 * units :].T


def tidy(expert_sum):
    count, step, width = expert_sum.shape
    units = width // 3
    shape = jax.ShapeDtypeStruct((count, step, units), jnp.float32)
    spec = pl.BlockSpec((1, step, units), lambda e: (e, 0, 0))
    return pl.pallas_call(
        functools.partial(tidy_kernel, 0),
        grid=(count,),
        out_shape=(shape, shape, jax.ShapeDtypeStruct((count, units, step), jnp.float32)),
        in_specs=[pl.BlockSpec((1, step, width), lambda e: (e, 0, 0))],
        out_specs=(spec, spec, pl.BlockSpec((1, units, step), lambda e: (e, 0, 0))),
        compiler_params=pltpu.CompilerParams(dimension_semantics=("arbitrary",)),
        name="tidy",
    )(expert_sum)


def on_device(
    layer_input,
    attn_gain,
    query_weight,
    key_weight,
    value_weight,
    out_weight,
    moe_gain,
    router_weight,
    gate_residual,
    const_gate,
    const_value,
    gate_weight,
    up_weight,
    down_weight,
    routes,
    grad_out,
):
    local_rows, model_width = layer_input.shape
    tensor_size = lax.axis_size("tensor")
    group_rows = local_rows * tensor_size
    head_count = query_weight.shape[1] // HD
    ffn_count = gate_weight.shape[0]
    route_count = router_weight.shape[1]
    attn_gain_row = attn_gain.reshape(1, model_width)
    moe_gain_row = moe_gain.reshape(1, model_width)
    cosine, sine = rope_lanes(LENGTH, HD)
    q2, k2, v2, o2, lse, attn_rows, moe_rows, grad_rows, hidden, qkv_weight, out_double = forward(
        tensor_size,
        layer_input,
        attn_gain_row,
        moe_gain_row,
        query_weight,
        key_weight,
        value_weight,
        out_weight,
        grad_out,
        jnp.asarray(cosine),
        jnp.asarray(sine),
    )
    n_dp = lax.axis_size("dp")
    pad = ((0, EXP_PAD - route_count), (0, 0))
    ffn_part, ffn_back, chosen_t, expert_part = experts(
        n_dp,
        tensor_size,
        route_count,
        moe_rows.reshape(group_rows, model_width),
        grad_rows.reshape(group_rows, model_width),
        routes.T,
        jnp.pad(gate_residual.T, pad),
        jnp.pad(router_weight.T, pad),
        gate_weight,
        up_weight,
        down_weight,
    )
    gates = jnp.transpose(const_gate, (1, 0, 2)).reshape(model_width, -1)
    both_weight = jnp.concatenate(
        [router_weight, gates, jnp.zeros((model_width, 128 - 4 - route_count), jnp.float32)], axis=1
    )

    blocks = (tensor_size, local_rows, model_width)
    row_start = lax.axis_index("tensor") * local_rows
    local_routes = lax.dynamic_slice_in_dim(routes, row_start, local_rows, 0)
    local_residual = lax.dynamic_slice_in_dim(gate_residual, row_start, local_rows, 0)
    output, input_grad, expert_sum, attn_sum_rows, small, gain = backward(
        n_dp,
        tensor_size,
        ffn_part.reshape(blocks),
        ffn_back.reshape(blocks),
        chosen_t,
        expert_part,
        hidden,
        moe_rows,
        grad_out,
        layer_input,
        local_routes,
        local_residual,
        both_weight,
        const_value,
        moe_gain_row,
        attn_gain_row,
        q2,
        k2,
        v2,
        o2,
        lse,
        attn_rows,
        qkv_weight,
        out_double,
        jnp.asarray(np.concatenate([cosine[:, :HD], sine[:, HD:]], axis=1)),
    )
    if not reduced_inside(model_width // n_dp):

        def scattered(pairs):
            pairs = jnp.transpose(pairs, (2, 1, 3, 0, 4)).reshape(model_width, -1)
            return lax.psum_scatter(pairs, "dp", scatter_dimension=0, tiled=True).astype(
                jnp.float32
            )

        attn_sum_rows = scattered(attn_sum_rows)
        expert_sum = scattered(expert_part).reshape(
            model_width // n_dp, ffn_count, expert_part.shape[-1]
        )
        expert_sum = jnp.transpose(expert_sum, (1, 0, 2))
    gate_sum, up_sum, down_sum = tidy(expert_sum)
    wide = head_count * HD
    out_at = qkv_weight.shape[1]
    both_grad = small[8:24].T
    return (
        output,
        input_grad,
        gain[0],
        attn_sum_rows[:, :wide],
        attn_sum_rows[:, wide : 2 * wide],
        attn_sum_rows[:, 2 * wide : 3 * wide],
        attn_sum_rows[:, out_at : out_at + wide].T,
        small[0],
        both_grad[:, :route_count],
        jnp.transpose(both_grad[:, route_count : route_count + 4].reshape(model_width, 2, 2), (1, 0, 2)),
        small[1:3],
        gate_sum,
        up_sum,
        down_sum,
    )


def solution(mesh):
    in_specs = (
        P(("dp", "tensor"), None),
        P(),
        P(None, "tensor"),
        P(None, "tensor"),
        P(None, "tensor"),
        P("tensor", None),
        P(),
        P(),
        P("dp", None),
        P(),
        P(),
        P(None, None, "tensor"),
        P(None, None, "tensor"),
        P(None, "tensor", None),
        P("dp", None),
        P(("dp", "tensor"), None),
    )
    out_specs = (
        P(("dp", "tensor"), None),
        P(("dp", "tensor"), None),
        P(),
        P("dp", "tensor"),
        P("dp", "tensor"),
        P("dp", "tensor"),
        P("tensor", "dp"),
        P(),
        P(),
        P(),
        P(),
        P(None, "dp", "tensor"),
        P(None, "dp", "tensor"),
        P(None, "tensor", "dp"),
    )
    return jax.shard_map(
        on_device, mesh=mesh, in_specs=in_specs, out_specs=out_specs, check_vma=False
    )
```

```python
import functools
import math

import jax
import jax.numpy as jnp
import numpy as np
from jax import lax
from jax.experimental import pallas as pl
from jax.experimental.pallas import tpu as pltpu
from jax.sharding import PartitionSpec as P

HD = 64
LENGTH = 1024
BLOCK = 256
CAP = 256


EPSILON = 1e-06
MASKED = -1e30


EXP_PAD = 16


def dot(a, b):
    return jnp.dot(a, b, preferred_element_type=jnp.float32)


def dot_nt(a, b):
    return lax.dot_general(a, b, (((1,), (1,)), ((), ())), preferred_element_type=jnp.float32)


def dot_tn(a, b):
    return lax.dot_general(a, b, (((0,), (0,)), ((), ())), preferred_element_type=jnp.float32)


def three_parts(values):
    first = values.astype(jnp.bfloat16)
    rest = values - first.astype(jnp.float32)
    second = rest.astype(jnp.bfloat16)
    third = (rest - second.astype(jnp.float32)).astype(jnp.bfloat16)
    return (first, second, third)


MESH = pl.DeviceIdType.MESH
PIECES = 8
GRAD_PIECES = 2
SUM_PIECES = 4
LINE_TURNS = (2, 5, 7)


def bit_of(index, position):
    return index // (1 << position) % 2


def flipped(index, position):
    return index + (1 << position) * (1 - 2 * bit_of(index, position))


def log2_of(count):
    return count.bit_length() - 1


def greet(axes):
    barrier = pltpu.get_barrier_semaphore()
    for axis, index, count in axes:

        def body(step, _, axis=axis, index=index, count=count):
            pl.semaphore_signal(
                barrier, inc=1, device_id={axis: (index + step) % count}, device_id_type=MESH
            )
            return 0

        lax.fori_loop(1, count, body, 0)
    pl.semaphore_wait(barrier, sum(count - 1 for _, _, count in axes))


class LineGather:
    def __init__(self, blocks, send, recv, place, pieces=1):
        self.blocks, self.send, self.recv, self.place = blocks, send, recv, place
        self.count, self.pieces = blocks.shape[0], pieces
        self.rows = blocks.shape[1] // pieces

    def copy(self, block, n, way):
        piece = self.blocks.at[block, pl.ds(n * self.rows, self.rows)]
        return pltpu.make_async_remote_copy(
            src_ref=piece,
            dst_ref=piece,
            send_sem=self.send.at[way, block, n],
            recv_sem=self.recv.at[block, n],
            device_id={"tensor": self.place + 1 - 2 * way},
            device_id_type=MESH,
        )

    def start(self, n=0):
        @pl.when(self.place < self.count - 1)
        def _():
            self.copy(self.place, n, 0).start()

        @pl.when(self.place > 0)
        def _():
            self.copy(self.place, n, 1).start()

    def step(self, distance, n=0):
        below, above = self.place - distance, self.place + distance

        @pl.when(below >= 0)
        def _():
            self.copy(below, n, 0).wait_recv()

            @pl.when(self.place < self.count - 1)
            def _():
                self.copy(below, n, 0).start()

        @pl.when(above < self.count)
        def _():
            self.copy(above, n, 1).wait_recv()

            @pl.when(self.place > 0)
            def _():
                self.copy(above, n, 1).start()

    def finish(self, pieces=None):
        pieces = range(self.pieces) if pieces is None else pieces
        for distance in range(self.count):
            below, above = self.place - distance, self.place + distance

            @pl.when((below >= 0) & (self.place < self.count - 1))
            def _(below=below):
                for n in pieces:
                    self.copy(below, n, 0).wait_send()

            @pl.when((above < self.count) & (self.place > 0))
            def _(above=above):
                for n in pieces:
                    self.copy(above, n, 1).wait_send()


class LineScatter:
    def __init__(self, parts, arrived, send, recv, place, pieces):
        self.parts, self.arrived, self.send, self.recv = parts, arrived, send, recv
        self.place, self.count, self.pieces = place, parts.shape[0], pieces
        self.rows = parts.shape[1] // pieces
        self.drained = set()

    def piece(self, ref, block, n):
        return ref.at[block, pl.ds(n * self.rows, self.rows)]

    def copy(self, block, n, way, own=False):
        there = self.piece(self.arrived, block + 1 - way, n)
        return pltpu.make_async_remote_copy(
            src_ref=self.piece(self.parts, block, n) if own else there,
            dst_ref=there,
            send_sem=self.send.at[way, block, n],
            recv_sem=self.recv.at[way, block, n],
            device_id={"tensor": self.place + 1 - 2 * way},
            device_id_type=MESH,
        )

    def originate(self, blocks, pieces=None):
        for way, first in ((0, 0), (1, self.count - 1)):
            sent = [block for block in blocks if block != first]
            if sent:

                @pl.when(self.place == first)
                def _(way=way, sent=sent):
                    for n in pieces or range(self.pieces):
                        for block in sent:
                            self.copy(block, n, way, own=True).start()

    def drain(self, blocks, n):
        for way, first in ((0, 0), (1, self.count - 1)):
            sent = [block for block in blocks if block != first]
            self.drained.update((first, block, n) for block in sent)
            if sent:

                @pl.when(self.place == first)
                def _(way=way, sent=sent):
                    for block in sent:
                        self.copy(block, n, way).wait_send()

    def pass_piece(self, block, n, way):
        self.copy(block, n, way).wait_recv()
        there = self.piece(self.arrived, block + 1 - way, n)
        mine = self.piece(self.parts, block, n)
        there[...] = (there[...].astype(jnp.float32) + mine[...].astype(jnp.float32)).astype(
            there.dtype
        )
        self.copy(block, n, way).start()

    def hops(self, place, way):
        return place if way == 0 else self.count - 1 - place

    def forward(self, turn, blocks):
        for place in range(1, self.count - 1):
            passed = []
            for block in blocks:
                way = 0 if place < block else 1
                n = turn - self.hops(place, way) + 1
                if place != block and 0 <= n < self.pieces:
                    passed.append((self.hops(place, way), block, n, way))
            if passed:

                @pl.when(self.place == place)
                def _(passed=passed):
                    for _, block, n, way in sorted(passed, key=lambda item: -item[0]):
                        self.pass_piece(block, n, way)

    def forward_all(self, block):
        for turn in range(self.pieces + self.count - 3):
            self.forward(turn, (block,))

    def collect(self, total, n):
        place = self.place
        rows = slice(n * self.rows, (n + 1) * self.rows)
        total[rows, :] = self.parts[place, rows, :].astype(jnp.float32)
        for way in (0, 1):

            @pl.when(place > 0 if way == 0 else place < self.count - 1)
            def _(way=way):
                self.copy(place, n, way).wait_recv()
                total[rows, :] += self.arrived[place + 1 - way, rows, :].astype(jnp.float32)

    def finish(self):
        for place in range(self.count):
            left = [
                (block, n)
                for block in range(self.count)
                for n in range(self.pieces)
                if block != place and (place, block, n) not in self.drained
            ]
            if left:

                @pl.when(self.place == place)
                def _(place=place, left=left):
                    for block, n in left:
                        self.copy(block, n, 0 if place < block else 1).wait_send()


class Halving:
    def __init__(self, source, kept, first, stages, sems, dp, dp_bits, splits):
        self.source, self.kept, self.first, self.stages = source, kept, first, stages
        self.first_send, self.first_recv, self.local, self.send, self.recv = sems
        self.dp, self.bits, self.splits = dp, dp_bits, splits
        self.core = bit_of(dp, 0)
        upper = list(range(dp_bits - 1))
        self.orders = (upper, upper[1:] + upper[:1])

    def first_copy(self, e):
        return pltpu.make_async_remote_copy(
            src_ref=self.source.at[e, 1 - self.core],
            dst_ref=self.first.at[e],
            send_sem=self.first_send.at[e],
            recv_sem=self.first_recv.at[e],
            device_id={"dp": flipped(self.dp, 0)},
            device_id_type=MESH,
        )

    def local_copy(self, e):
        return pltpu.make_async_copy(
            self.source.at[e, self.core], self.kept.at[e], self.local.at[e]
        )

    def blocks(self, part, stage, k, mine):
        order = self.orders[part]
        index = 0
        for done in order[:stage]:
            index = index + (1 << done) * bit_of(self.dp, done + 1)
        here = bit_of(self.dp, order[stage] + 1)
        index = index + (1 << order[stage]) * (here if mine else 1 - here)
        for n, free in enumerate(order[stage + 1 :]):
            index = index + (1 << free) * (k // (1 << n) % 2)
        return index

    def width(self, part):
        return pl.ds(*self.splits[part])

    def stage_copy(self, e, part, stage, k):
        start, size = self.splits[part]
        return pltpu.make_async_remote_copy(
            src_ref=self.kept.at[e, self.blocks(part, stage, k, False), :, pl.ds(start, size)],
            dst_ref=self.stages[stage].at[e, k, :, pl.ds(start, size)],
            send_sem=self.send[stage].at[e, part, k],
            recv_sem=self.recv[stage].at[e, part, k],
            device_id={"dp": flipped(self.dp, self.orders[part][stage] + 1)},
            device_id_type=MESH,
        )

    def number(self, stage):
        return 1 << (self.bits - 2 - stage)

    def start(self, e):
        self.first_copy(e).start()
        self.local_copy(e).start()

    def send_stage(self, e, stage):
        for k in range(self.number(stage)):
            for part in (0, 1):
                self.stage_copy(e, part, stage, k).start()

    def add_rows(self, target, addend):
        rows = target.shape[0]
        step = 32 if rows % 32 == 0 else rows

        def body(n, _):
            at = pl.ds(pl.multiple_of(n * step, step), step)
            target[at, :] = (
                target[at, :].astype(jnp.float32) + addend[at, :].astype(jnp.float32)
            ).astype(target.dtype)
            return 0

        lax.fori_loop(0, rows // step, body, 0)

    def open(self, e):
        self.first_copy(e).wait_recv()
        self.local_copy(e).wait()
        for block in range(self.kept.shape[1]):
            self.add_rows(self.kept.at[e, block], self.first.at[e, block])
        self.send_stage(e, 0)

    def advance(self, e, stage):
        for k in range(self.number(stage)):
            for part in (0, 1):
                self.stage_copy(e, part, stage, k).wait_recv()
                block = self.blocks(part, stage, k, True)
                self.add_rows(
                    self.kept.at[e, block, :, self.width(part)],
                    self.stages[stage].at[e, k, :, self.width(part)],
                )
        self.send_stage(e, stage + 1)

    def close(self, e, out):
        stage = self.bits - 2
        for part in (0, 1):
            self.stage_copy(e, part, stage, 0).wait_recv()
            block = self.blocks(part, stage, 0, True)
            columns = self.width(part)
            out[:, columns] = self.kept[e, block, :, columns].astype(jnp.float32) + self.stages[
                stage
            ][e, 0, :, columns].astype(jnp.float32)

    def finish(self, e):
        self.first_copy(e).wait_send()
        for stage in range(self.bits - 1):
            for k in range(self.number(stage)):
                for part in (0, 1):
                    self.stage_copy(e, part, stage, k).wait_send()


class PairedHalving(Halving):
    def first_copy(self, e):
        slot = e % self.first.shape[0]
        return pltpu.make_async_copy(self.source[1].at[e], self.first.at[slot], self.first_recv.at[e])

    def local_copy(self, e):
        return pltpu.make_async_copy(self.source[0].at[e], self.kept.at[e], self.local.at[e])

    def begin(self, count):
        for e in range(count):
            if e < self.first.shape[0]:
                self.first_copy(e).start()
            self.local_copy(e).start()

    def open(self, e, count):
        self.first_copy(e).wait()
        self.local_copy(e).wait()
        for block in range(self.kept.shape[1]):
            self.add_rows(self.kept.at[e, block], self.first.at[e % self.first.shape[0], block])
        self.send_stage(e, 0)
        if e + self.first.shape[0] < count:
            self.first_copy(e + self.first.shape[0]).start()

    def finish(self, e):
        for stage in range(self.bits - 1):
            for k in range(self.number(stage)):
                for part in (0, 1):
                    self.stage_copy(e, part, stage, k).wait_send()


class Butterfly:
    def __init__(self, total, arrived, send, recv, dp, place, dp_bits, tensor_bits):
        self.total, self.arrived, self.send, self.recv = total, arrived, send, recv
        self.partners = [{"dp": flipped(dp, b)} for b in range(dp_bits)]
        self.partners += [{"tensor": flipped(place, b)} for b in range(tensor_bits)]

    def copy(self, n):
        return pltpu.make_async_remote_copy(
            src_ref=self.total,
            dst_ref=self.arrived.at[n],
            send_sem=self.send.at[n],
            recv_sem=self.recv.at[n],
            device_id=self.partners[n],
            device_id_type=MESH,
        )

    def start(self, n):
        self.copy(n).start()

    def take(self, n):
        self.copy(n).wait()
        self.total[...] += self.arrived[n]


class Exchange:
    def __init__(self, totals, arrived, sends, recvs, axes):
        self.totals, self.arrived, self.sends, self.recvs, self.axes = (
            totals,
            arrived,
            sends,
            recvs,
            axes,
        )

    def copy(self, turn, step):
        axis, index, count = self.axes[turn]
        return pltpu.make_async_remote_copy(
            src_ref=self.totals.at[turn],
            dst_ref=self.arrived[turn].at[step],
            send_sem=self.sends[turn].at[step],
            recv_sem=self.recvs[turn].at[step],
            device_id={axis: (index + step + 1) % count},
            device_id_type=MESH,
        )

    def start(self, turn):
        def body(step, _):
            self.copy(turn, step).start()
            return 0

        lax.fori_loop(0, self.axes[turn][2] - 1, body, 0)

    def take(self, turn):
        self.totals[turn + 1] = self.totals[turn]

        def body(step, _):
            self.copy(turn, step).wait()
            self.totals[turn + 1] += self.arrived[turn][step]
            return 0

        lax.fori_loop(0, self.axes[turn][2] - 1, body, 0)


def reduced_inside(step):
    return step % 32 == 0


class Nothing:
    def __getattr__(self, name):
        return lambda *arguments: None


def select_lanes(rows, columns, source):
    row = lax.broadcasted_iota(jnp.int32, (rows, columns), 0)
    column = lax.broadcasted_iota(jnp.int32, (rows, columns), 1)
    return jnp.where(row == source(column), 1.0, 0.0).astype(jnp.bfloat16)


def forward_kernel(
    n_t,
    input_ref,
    attn_gain_ref,
    moe_gain_ref,
    q_w_ref,
    k_w_ref,
    v_w_ref,
    out_w_ref,
    grad_ref,
    cos_ref,
    sin_ref,
    q_out,
    k_out,
    v_out,
    o_out,
    lse_out,
    rows_out,
    moe_out,
    grad_out,
    hidden_out,
    qkv_out,
    double_out,
    weights,
    part,
    arrived,
    acc,
    rows_send,
    rows_recv,
    grad_send,
    grad_recv,
    moe_send,
    moe_recv,
    line_send,
    line_recv,
):
    place = lax.axis_index("tensor")
    heads = q_out.shape[0]
    local, width = input_ref.shape
    barrier = pltpu.get_barrier_semaphore()
    for step in range(1, n_t):
        pl.semaphore_signal(
            barrier,
            inc=1,
            device_id={"tensor": (place + step) % n_t},
            device_id_type=MESH,
        )
    wide = input_ref[...].astype(jnp.float32)
    scale = lax.rsqrt(jnp.mean(wide * wide, axis=1, keepdims=True) + EPSILON)
    rows_out[place] = (wide * scale * attn_gain_ref[...].reshape(1, width)).astype(jnp.bfloat16)
    grad_out[place] = grad_ref[...]
    pl.semaphore_wait(barrier, n_t - 1)

    rows_gather = LineGather(rows_out, rows_send, rows_recv, place)
    grad_gather = LineGather(grad_out, grad_send, grad_recv, place, GRAD_PIECES)
    moe_gather = LineGather(moe_out, moe_send, moe_recv, place, PIECES)
    line = LineScatter(part, arrived, line_send, line_recv, place, PIECES)
    rows_gather.start()

    columns = heads * HD
    twice = select_lanes(columns, heads * 128, lambda c: c // 128 * HD + c % HD)
    swapped = select_lanes(
        columns,
        heads * 128,
        lambda c: c // 128 * HD + (c % HD + c % 128 // HD * (HD // 2)) % HD,
    )
    for n, (ref, lanes) in enumerate(
        ((q_w_ref, swapped), (k_w_ref, swapped), (v_w_ref, twice))
    ):
        weights[n * heads * 128 : (n + 1) * heads * 128, :] = dot_tn(lanes, ref[...]).astype(
            jnp.bfloat16
        )
    for n, ref in enumerate((q_w_ref, k_w_ref, v_w_ref)):
        qkv_out[n * columns : (n + 1) * columns, :] = ref[...]
    qkv_out[3 * columns :, :] = jnp.zeros(
        (qkv_out.shape[0] - 3 * columns, width), jnp.bfloat16
    )
    double_out[...] = dot_tn(twice, out_w_ref[...]).astype(jnp.bfloat16)

    def project(block):
        at = pl.ds(pl.multiple_of(block * local, local), local)
        product = dot_nt(rows_out[block], weights[...])
        cosine, sine = cos_ref[at, :], sin_ref[at, :]
        for n, target in enumerate((q_out, k_out, v_out)):
            for h in range(heads):
                start = (n * heads + h) * 128
                piece = product[:, start : start + 128]
                if n < 2:
                    piece = piece * cosine + pltpu.roll(piece, 64, 1) * sine
                target[h, at, :] = piece.astype(jnp.bfloat16)

    def arrive(distance, _):
        @pl.when(distance > 0)
        def _():
            rows_gather.step(distance)

        def side(way, _):
            block = place + (2 * way - 1) * distance

            @pl.when((block >= 0) & (block < n_t) & ((distance > 0) | (way == 0)))
            def _():
                project(block)

            return 0

        lax.fori_loop(0, 2, side, 0)
        return 0

    lax.fori_loop(0, n_t, arrive, 0)
    grad_gather.start()

    factor = 0.5 * HD ** (-0.5)

    lse_out[...] = jnp.zeros_like(lse_out)

    def attend(block):
        at = slice(block * local, (block + 1) * local)
        seen = (block + 1) * local
        mixed = []
        for h in range(heads):
            scores = dot_nt(q_out[h, at, :], k_out[h, 0:seen, :]) * factor
            top = jnp.max(scores, axis=1, keepdims=True)
            exps = jnp.exp(scores - top)
            total = jnp.sum(exps, axis=1, keepdims=True)
            probs = (exps / total).astype(jnp.bfloat16)
            out = dot(probs, v_out[h, 0:seen, :]).astype(jnp.bfloat16)
            o_out[h, at, :] = out
            mixed.append(out)
            log_total = jnp.broadcast_to(top + jnp.log(total), (local, 128))
            lse_out[h : h + 1, at] = log_total.T[0:1, :]
        mixed = jnp.concatenate(mixed, axis=1)
        part[block] = (0.5 * dot(mixed, double_out[...])).astype(jnp.bfloat16)

    for block in range(n_t):
        attend(block)
    ends_first = (n_t - 1, 0, *range(n_t - 2, 0, -1))
    line.originate(ends_first, (0,))
    lag = n_t - 2
    for turn in range(PIECES + lag + n_t - 1):
        line.forward(turn, ends_first)
        if turn + 1 < PIECES:
            line.drain(ends_first, turn)
            line.originate(ends_first, (turn + 1,))
        if 0 <= turn - lag < PIECES:
            n = turn - lag
            line.collect(acc, n)
            at = slice(n * (local // PIECES), (n + 1) * (local // PIECES))
            hidden = input_ref[at, :].astype(jnp.float32) + acc[at, :]
            hidden_out[at, :] = hidden
            scale = lax.rsqrt(jnp.mean(hidden * hidden, axis=1, keepdims=True) + EPSILON)
            moe_out[place, at, :] = (hidden * scale * moe_gain_ref[...].reshape(1, width)).astype(jnp.bfloat16)
            moe_gather.start(n)
        for step in range(1, n_t):
            if 0 <= turn - lag - step < PIECES:
                moe_gather.step(step, turn - lag - step)
        if turn % 2 == 0 and turn // 2 + 1 < n_t:
            grad_gather.step(turn // 2 + 1)
    for exchange in (rows_gather, moe_gather, line):
        exchange.finish()
    grad_gather.finish((0,))


def forward(n_t, layer_input, attn_gain, moe_gain, q_w, k_w, v_w, out_w, grad_out, cosine, sine):
    local, width = layer_input.shape
    group = local * n_t
    heads = q_w.shape[0] // HD
    bf, f32 = jnp.bfloat16, jnp.float32
    dma = pltpu.SemaphoreType.DMA
    vmem = pl.BlockSpec(memory_space=pltpu.VMEM)
    blocks = (n_t, local, width)
    qkv_width = -(-3 * heads * HD // 128) * 128
    outs = (
        *[jax.ShapeDtypeStruct((heads, group, 128), bf)] * 4,
        jax.ShapeDtypeStruct((8, group), f32),
        *[jax.ShapeDtypeStruct(blocks, bf)] * 3,
        jax.ShapeDtypeStruct((local, width), f32),
        jax.ShapeDtypeStruct((qkv_width, width), bf),
        jax.ShapeDtypeStruct((heads * 128, width), bf),
    )
    return pl.pallas_call(
        functools.partial(forward_kernel, n_t),
        out_shape=outs,
        in_specs=[vmem] * 10,
        out_specs=(vmem,) * len(outs),
        scratch_shapes=[
            pltpu.VMEM((3 * heads * 128, width), bf),
            pltpu.VMEM(blocks, bf),
            pltpu.VMEM((n_t + 1, local, width), bf),
            pltpu.VMEM((local, width), f32),
            *[s for n in (1, GRAD_PIECES, PIECES) for s in (dma((2, n_t, n)), dma((n_t, n)))],
            dma((2, n_t, PIECES)),
            dma((2, n_t, PIECES)),
        ],
        compiler_params=pltpu.CompilerParams(
            collective_id=2, has_side_effects=True, vmem_limit_bytes=56 << 20
        ),
        name="forward",
    )(layer_input, attn_gain, moe_gain, q_w, k_w, v_w, out_w, grad_out, cosine, sine)


def expert_kernel(
    sizes,
    moe_ref,
    half_ref,
    grad_ref,
    routes_ref,
    residual_ref,
    router_ref,
    gate_ref,
    up_ref,
    down_ref,
    back_ref,
    sum_ref,
    chosen_ref,
    *rest,
):
    n_dp, n_t, ffn_count, route_count, inside = sizes
    weight_outs = rest[: 2 if inside else 1]
    (
        probs_s,
        rank_s,
        router_s,
        hit_s,
        turned_s,
        slot_s,
        rows_s,
        gate_s,
        up_s,
        active_s,
        out_s,
        grad_s,
        part_s,
        arrived_s,
        acc,
        weight_s,
        grad_send,
        grad_recv,
        half_sem,
        line_send,
        line_recv,
        own_sem,
        pair_send,
        pair_recv,
    ) = rest[2 if inside else 1 :]
    turn = pl.program_id(0)
    expert = turn % ffn_count
    slot = turn % 2
    dp = lax.axis_index("dp")
    place = lax.axis_index("tensor")
    local, width = grad_ref.shape
    rows = n_t * local
    hidden = gate_ref.shape[2]
    step = width // n_dp
    grad_rows = local // GRAD_PIECES
    gather = LineGather(grad_s, grad_send, grad_recv, place, GRAD_PIECES)
    line = LineScatter(part_s, arrived_s, line_send, line_recv, place, SUM_PIECES)
    blocks = tuple(range(n_t))
    ends_first = (n_t - 1, 0, *range(n_t - 2, 0, -1))

    def line_turn(n):
        line.forward(n, ends_first)
        if n + 1 < SUM_PIECES:
            line.drain(ends_first, n)
            line.originate(ends_first, (n + 1,))

    def half_copy(block):
        return pltpu.make_async_copy(
            half_ref.at[block, pl.ds(0, grad_rows)],
            grad_s.at[block, pl.ds(0, grad_rows)],
            half_sem.at[block],
        )

    def own_copy(e, at):
        core = bit_of(dp, 0)
        return pltpu.make_async_copy(
            weight_s.at[at, core] if inside else weight_s.at[at],
            weight_outs[0].at[e],
            own_sem.at[e],
        )

    def pair_copy(e, at):
        return pltpu.make_async_remote_copy(
            src_ref=weight_s.at[at, 1 - bit_of(dp, 0)],
            dst_ref=weight_outs[1].at[e],
            send_sem=pair_send.at[e],
            recv_sem=pair_recv.at[e],
            device_id={"dp": flipped(dp, 0)},
            device_id_type=MESH,
        )

    def left(e, at):
        own_copy(e, at).wait()
        if inside:
            pair_copy(e, at).wait_send()

    def combine(block):
        at = slice(block * local, (block + 1) * local)
        out = out_s[...].reshape(ffn_count * CAP, width)
        return dot(turned_s[at, :], out).astype(jnp.bfloat16)

    @pl.when(turn == 0)
    def _():
        for block in blocks:
            half_copy(block).start()
        grad_s[place, grad_rows:, :] = grad_ref[grad_rows:, :]
        greet((("tensor", place, n_t), ("dp", dp, n_dp)))
        gather.start(1)
        router_s[...] = jnp.zeros_like(router_s)
        router_s[0:route_count, :] = router_ref[...]
        parts = three_parts(router_s[...])
        logits = jnp.concatenate(
            [residual_ref[...], jnp.zeros((EXP_PAD - route_count, rows), jnp.float32)], axis=0
        )
        moe = moe_ref[...].reshape(rows, width)
        for part in parts:
            logits = logits + dot_nt(part, moe)
        index = lax.broadcasted_iota(jnp.int32, (EXP_PAD, rows), 0)
        logits = jnp.where(index < route_count, logits, MASKED)
        top = jnp.max(logits, axis=0, keepdims=True)
        exps = jnp.exp(logits - top)
        probs_s[...] = exps / jnp.sum(exps, axis=0, keepdims=True)
        named = (routes_ref[0:1, :] == index) | (routes_ref[1:2, :] == index)
        named = jnp.where(named, 1.0, 0.0)
        before = lax.broadcasted_iota(jnp.int32, (256, 256), 0)
        after = lax.broadcasted_iota(jnp.int32, (256, 256), 1)
        earlier = jnp.where(before < after, 1.0, 0.0).astype(jnp.bfloat16)
        total = jnp.zeros((EXP_PAD, 1), jnp.float32)
        for start in range(0, rows, 256):
            block = named[:, start : start + 256]
            rank = dot(block.astype(jnp.bfloat16), earlier) + total
            rank_s[:, start : start + 256] = jnp.where(block > 0.5, rank, -1.0)
            total = total + jnp.sum(block, axis=1, keepdims=True)

    @pl.when(turn < ffn_count)
    def _():
        place_in = lax.broadcasted_iota(jnp.int32, (CAP, rows), 0).astype(jnp.float32)
        hit = rank_s[pl.ds(expert, 1), :] == place_in
        slot_weight = jnp.sum(
            jnp.where(hit, probs_s[pl.ds(expert, 1), :], 0.0), axis=1, keepdims=True
        )
        slot_s[expert] = slot_weight
        dispatch = jnp.where(hit, 1.0, 0.0).astype(jnp.bfloat16)
        hit_s[expert] = dispatch
        turned_s[:, pl.ds(pl.multiple_of(expert * CAP, CAP), CAP)] = dispatch.T
        rows_in = dot(dispatch, moe_ref[...].reshape(rows, width)).astype(jnp.bfloat16)
        rows_s[expert] = rows_in
        gate_pre = dot(rows_in, gate_ref[0])
        up_pre = dot(rows_in, up_ref[0])
        sigmoid = 1.0 / (1.0 + jnp.exp(-gate_pre))
        silu = gate_pre * sigmoid
        active = (silu * up_pre).astype(jnp.bfloat16)
        active_s[expert] = active
        gate_s[expert] = up_pre * (sigmoid + silu * (1.0 - sigmoid))
        up_s[expert] = silu
        out_s[expert] = (dot(active, down_ref[0]) * slot_weight).astype(jnp.bfloat16)
        for distance in range(1, n_t - 1):

            @pl.when(turn == 3 * distance - 2)
            def _(distance=distance):
                gather.step(distance, 1)

    @pl.when(turn == ffn_count)
    def _():
        for block in blocks:
            part_s[block] = combine(block)
            half_copy(block).wait()
        line.originate(ends_first, (0,))
        gather.step(n_t - 1, 1)

    @pl.when(turn >= ffn_count)
    def _():
        active = active_s[expert]
        rows_grad = dot(hit_s[expert], grad_s[...].reshape(rows, width))
        low = rows_grad.astype(jnp.bfloat16)
        grad_active = dot_nt(low, down_ref[0])
        slot_weight = slot_s[expert]
        inner = jnp.sum(grad_active * active.astype(jnp.float32), axis=1, keepdims=True)
        lane = lax.broadcasted_iota(jnp.int32, (CAP, 128), 1)
        inner_parts = jnp.zeros((CAP, 128), jnp.float32)
        for n, inner_part in enumerate(three_parts(inner)):
            inner_parts = jnp.where(lane == n, inner_part.astype(jnp.float32), inner_parts)
        chosen_rows = dot_tn(inner_parts.astype(jnp.bfloat16), hit_s[expert])
        chosen_row = chosen_rows[0:1] + chosen_rows[1:2] + chosen_rows[2:3]
        for n in blocks:
            chosen_ref[n, pl.ds(expert, 1), :] = chosen_row[:, n * local : (n + 1) * local]
        grad_low = (rows_grad * slot_weight).astype(jnp.bfloat16)
        grad_active = grad_active * slot_weight
        grad_gate = (grad_active * gate_s[expert]).astype(jnp.bfloat16)
        grad_up = (grad_active * up_s[expert]).astype(jnp.bfloat16)
        out_s[expert] = (dot_nt(grad_gate, gate_ref[0]) + dot_nt(grad_up, up_ref[0])).astype(
            jnp.bfloat16
        )

        @pl.when(expert >= 2)
        def _():
            left(expert - 2, slot)

        rows_in = rows_s[expert]
        for n, (one, other) in enumerate(
            ((rows_in, grad_gate), (rows_in, grad_up), (grad_low, active))
        ):
            product = dot_tn(one, other).astype(jnp.bfloat16)
            for d in range(n_dp):
                weight_s[slot, d % 2, d // 2, :, n * hidden : (n + 1) * hidden] = product[
                    d * step : (d + 1) * step
                ]
        own_copy(expert, slot).start()
        if inside:
            pair_copy(expert, slot).start()
        for n, at in enumerate(LINE_TURNS):

            @pl.when(expert == at)
            def _(n=n):
                line_turn(n)

    @pl.when(turn == 2 * ffn_count - 1)
    def _():
        for block in blocks:
            back_ref[block] = combine(block)
        for e in range(ffn_count - 2, ffn_count):
            left(e, e % 2)
        for n in range(len(LINE_TURNS), SUM_PIECES + n_t - 3):
            line_turn(n)
        for n in range(SUM_PIECES):
            line.collect(acc, n)
        sum_ref[...] = acc[...]
        line.finish()
        gather.finish((1,))
        if inside:
            for e in range(ffn_count):
                pair_copy(e, e % 2).wait_recv()


def experts(n_dp, n_t, moe_rows, grad_half, grad_out, routes_t, residual_t, router_t, gate_w, up_w, down_w):
    _, local, width = moe_rows.shape
    rows = n_t * local
    route_count = router_t.shape[0]
    ffn_count, _, hidden = gate_w.shape
    step = width // n_dp
    half = n_dp // 2
    inside = reduced_inside(step)
    bf, f32 = jnp.bfloat16, jnp.float32
    dma = pltpu.SemaphoreType.DMA

    def whole(shape):
        return pl.BlockSpec(shape, lambda s: (0,) * len(shape), pipeline_mode=pl.Buffered(1))

    any_space = pl.BlockSpec(memory_space=pl.ANY)
    item = (half, step, 3 * hidden)
    weights = (
        [jax.ShapeDtypeStruct((ffn_count, *item), bf)] * 2
        if inside
        else [jax.ShapeDtypeStruct((ffn_count, 2, *item), bf)]
    )
    blocks = (n_t, local, width)
    return pl.pallas_call(
        functools.partial(expert_kernel, (n_dp, n_t, ffn_count, route_count, inside)),
        grid=(2 * ffn_count,),
        out_shape=(
            jax.ShapeDtypeStruct(blocks, bf),
            jax.ShapeDtypeStruct((local, width), f32),
            jax.ShapeDtypeStruct((n_t, ffn_count, local), f32),
            *weights,
        ),
        in_specs=[
            whole(blocks),
            any_space,
            whole((local, width)),
            whole((2, rows)),
            whole((route_count, rows)),
            whole((route_count, width)),
            pl.BlockSpec((1, width, hidden), lambda s: (s % ffn_count, 0, 0)),
            pl.BlockSpec((1, width, hidden), lambda s: (s % ffn_count, 0, 0)),
            pl.BlockSpec((1, hidden, width), lambda s: (s % ffn_count, 0, 0)),
        ],
        out_specs=(
            whole(blocks),
            whole((local, width)),
            whole((n_t, ffn_count, local)),
            *[any_space for _ in weights],
        ),
        scratch_shapes=[
            pltpu.VMEM((EXP_PAD, rows), f32),
            pltpu.VMEM((EXP_PAD, rows), f32),
            pltpu.VMEM((EXP_PAD, width), f32),
            pltpu.VMEM((ffn_count, CAP, rows), bf),
            pltpu.VMEM((rows, ffn_count * CAP), bf),
            pltpu.VMEM((ffn_count, CAP, 1), f32),
            pltpu.VMEM((ffn_count, CAP, width), bf),
            pltpu.VMEM((ffn_count, CAP, hidden), f32),
            pltpu.VMEM((ffn_count, CAP, hidden), f32),
            pltpu.VMEM((ffn_count, CAP, hidden), bf),
            pltpu.VMEM((ffn_count, CAP, width), bf),
            pltpu.VMEM(blocks, bf),
            pltpu.VMEM(blocks, bf),
            pltpu.VMEM((n_t + 1, local, width), bf),
            pltpu.VMEM((local, width), f32),
            pltpu.VMEM((2, 2, *item), bf),
            dma((2, n_t, GRAD_PIECES)),
            dma((n_t, GRAD_PIECES)),
            dma((n_t,)),
            dma((2, n_t, SUM_PIECES)),
            dma((2, n_t, SUM_PIECES)),
            dma((ffn_count,)),
            dma((ffn_count,)),
            dma((ffn_count,)),
        ],
        compiler_params=pltpu.CompilerParams(
            dimension_semantics=("arbitrary",),
            collective_id=3,
            has_side_effects=True,
            vmem_limit_bytes=62 << 20,
        ),
        name="experts",
    )(moe_rows, grad_half, grad_out, routes_t, residual_t, router_t, gate_w, up_w, down_w)


def side_forward(norm, named, residual, weight_parts, const_value, route_count, ffn_count):
    lane = lax.broadcasted_iota(jnp.int32, named.shape, 1)
    low = norm.astype(jnp.bfloat16)
    both = sum(dot_nt(low, part) for part in weight_parts)
    logits = jnp.where(lane < route_count, both + residual, MASKED)
    exps = jnp.exp(logits - jnp.max(logits, axis=1, keepdims=True))
    probs = exps / jnp.sum(exps, axis=1, keepdims=True)
    chosen = probs * named
    shares, keeps, rests = [], chosen[:, ffn_count + 1 : ffn_count + 2], []
    for c in range(2):
        at = route_count + 2 * c
        share = 1.0 / (1.0 + jnp.exp(both[:, at + 1 : at + 2] - both[:, at : at + 1]))
        weight = chosen[:, ffn_count + 2 + c : ffn_count + 3 + c]
        shares.append(share)
        keeps = keeps + weight * share
        rests.append(weight * (1.0 - share))
    special = keeps * norm + rests[0] * const_value[0:1] + rests[1] * const_value[1:2]
    return probs, chosen, shares, keeps, rests, special


def side_backward(
    norm, grad, named, forward, chosen_back, weight_parts, const_value, route_count, ffn_count
):
    probs, chosen, shares, keeps, rests, _ = forward
    lane = lax.broadcasted_iota(jnp.int32, named.shape, 1)
    self_dot = jnp.sum(grad * norm, axis=1, keepdims=True)
    value_dots = [
        jnp.sum(grad * const_value[c : c + 1], axis=1, keepdims=True) for c in range(2)
    ]
    d_probs = jnp.where(lane < ffn_count, chosen_back, 0.0)
    d_probs = jnp.where(lane == ffn_count + 1, self_dot, d_probs)
    for c in range(2):
        mixed = shares[c] * self_dot + (1.0 - shares[c]) * value_dots[c]
        d_probs = jnp.where(lane == ffn_count + 2 + c, mixed, d_probs)
    d_probs = d_probs * named
    d_both = probs * (d_probs - jnp.sum(probs * d_probs, axis=1, keepdims=True))
    d_both = jnp.where(lane < route_count, d_both, 0.0)
    for c in range(2):
        weight = chosen[:, ffn_count + 2 + c : ffn_count + 3 + c]
        d_share = shares[c] * (1.0 - shares[c]) * weight * (self_dot - value_dots[c])
        d_both = jnp.where(lane == route_count + 2 * c, d_share, d_both)
        d_both = jnp.where(lane == route_count + 2 * c + 1, -d_share, d_both)
    d_parts = three_parts(d_both)
    back = keeps * grad
    for m, n in ((0, 0), (0, 1), (1, 0), (1, 1)):
        back = back + dot(d_parts[m], weight_parts[n])
    low = norm.astype(jnp.bfloat16)
    weight_part = dot_tn(d_parts[0], low) + dot_tn(d_parts[1], low) + dot_tn(d_parts[2], low)
    value_part = [jnp.sum(rests[c] * grad, axis=0, keepdims=True) for c in range(2)]
    return back, weight_part, value_part


def backward_kernel(
    sizes,
    sum_ref,
    back_ref,
    chosen_ref,
    hidden_ref,
    moe_ref,
    grad_ref,
    input_ref,
    routes_ref,
    residual_ref,
    router_ref,
    gates_ref,
    value_ref,
    moe_gain_ref,
    attn_gain_ref,
    q_ref,
    k_ref,
    v_ref,
    o_ref,
    lse_ref,
    rows_ref,
    qkv_ref,
    out_w_ref,
    table_ref,
    *rest,
):
    dp_bits, n_t, ffn_count, route_count, attn_split, inside = sizes
    stage_count = dp_bits - 1 if inside else 0
    expert_refs = rest[: 2 if inside else 0]
    rest = rest[2 if inside else 0 :]
    (
        output_ref,
        input_grad_ref,
        expert_out,
        attn_out,
        small_out,
        gain_out,
        chosen_in,
        pair_buf,
        line_back,
        staged,
        both_s,
        turned_s,
        grad_rows,
        attn_part,
        acc,
        hidden_grad,
        double_grad,
        delta,
        dq,
        dk,
        dv,
        packed,
    ) = rest[:22]
    rest = rest[22:]
    if inside:
        attn_pairs, kept, first = rest[:3]
        stages = rest[3 : 3 + stage_count]
        rest = rest[3 + stage_count :]
        a_kept, a_first = rest[:2]
        a_stages = rest[2 : 2 + stage_count]
        rest = rest[2 + stage_count :]
    else:
        attn_pairs = attn_out
    small_in, gains, gain_dp, gain_tensor, side_back = rest[:5]
    rest = list(rest[5:])

    def sems(count):
        taken = rest[:count]
        del rest[:count]
        return taken

    (chosen_send, chosen_recv, gather_send, gather_recv) = sems(4)
    line_sems = [sems(2) for _ in range(2)]
    if inside:
        e_sems = [None] + sems(2) + [sems(stage_count), sems(stage_count)]
        a_sems = sems(3) + [sems(stage_count), sems(stage_count)]
    small_sems = sems(2)
    gain_sems = [sems(2), sems(2)]
    (staged_sem,) = sems(1)

    dp = lax.axis_index("dp")
    place = lax.axis_index("tensor")
    local = hidden_ref.shape[0]
    width = hidden_ref.shape[1]
    hidden_units = expert_out.shape[-1]
    heads = q_ref.shape[0]
    tensor_bits = log2_of(n_t)
    greet((("dp", dp, 1 << dp_bits), ("tensor", place, n_t)))

    back_line = LineScatter(back_ref, line_back, *line_sems[0], place, PIECES)
    attn_line = LineScatter(attn_part, line_back, *line_sems[1], place, PIECES)
    gather = LineGather(grad_rows, gather_send, gather_recv, place, PIECES)
    half = hidden_units // 2
    attn_width = attn_pairs.shape[-1]
    expert = attn = Nothing()
    if inside:
        splits = ((0, half), (half, half))
        expert = PairedHalving(expert_refs, kept, first, stages, e_sems, dp, dp_bits, splits)
        splits = ((0, attn_split), (attn_split, attn_width - attn_split))
        attn = Halving(attn_pairs, a_kept, a_first, a_stages, a_sems, dp, dp_bits, splits)
    small = Butterfly(small_out, small_in, *small_sems, dp, place, dp_bits, tensor_bits)
    gain = Exchange(
        gains, (gain_dp, gain_tensor), *gain_sems, (("dp", dp, 1 << dp_bits), ("tensor", place, n_t))
    )

    def chosen_copy(step):
        there = (place + step) % n_t
        return pltpu.make_async_remote_copy(
            src_ref=chosen_ref.at[there],
            dst_ref=chosen_in.at[step - 1],
            send_sem=chosen_send.at[step - 1],
            recv_sem=chosen_recv.at[step - 1],
            device_id={"tensor": there},
            device_id_type=MESH,
        )

    ends_first = (n_t - 1, 0, *range(n_t - 2, 0, -1))
    for step in range(1, n_t):
        chosen_copy(step).start()
    back_line.originate(ends_first, (0,))

    def over_experts(action):
        def body(e, _):
            action(e)
            return 0

        def run(first, last):
            lax.fori_loop(first, last, body, 0)

        return run

    expert.begin(ffn_count)

    norm = moe_ref[place].astype(jnp.float32)
    lane = lax.broadcasted_iota(jnp.int32, (local, 128), 1)
    mine = pl.ds(pl.multiple_of(place * local, local), local)
    turned_s[...] = jnp.zeros_like(turned_s)
    turned_s[0:route_count, :] = residual_ref[:, mine]
    turned_s[16:18, :] = routes_ref[:, mine].astype(jnp.float32)
    turned = turned_s[...].T
    residual = turned
    kind = lane.astype(jnp.float32)
    named = jnp.where((turned[:, 16:17] == kind) | (turned[:, 17:18] == kind), 1.0, 0.0)
    both_s[...] = jnp.zeros_like(both_s)
    both_s[0:route_count, :] = router_ref[...]
    for c in range(2):
        both_s[route_count + 2 * c : route_count + 2 * c + 2, :] = gates_ref[c]
    weight_parts = three_parts(both_s[...])
    const_value = value_ref[...]
    grad = grad_ref[...].astype(jnp.float32)
    forward = side_forward(
        norm, named, residual, weight_parts, const_value, route_count, ffn_count
    )
    pair_buf[...] = hidden_ref[...] + forward[-1]
    chosen_total = chosen_ref[place]
    for step in range(1, n_t):
        chosen_copy(step).wait_recv()
        chosen_total = chosen_total + chosen_in[step - 1]
    chosen_back = jnp.concatenate(
        [chosen_total, jnp.zeros((128 - ffn_count, local), jnp.float32)], axis=0
    ).T
    back, weight_part, value_part = side_backward(
        norm, grad, named, forward, chosen_back, weight_parts, const_value, route_count, ffn_count
    )
    side_back[...] = back
    small_out[1:2, :] = value_part[0]
    small_out[2:3, :] = value_part[1]
    small_out[3:8, :] = jnp.zeros((5, width), jnp.float32)
    small_out[8:24, :] = weight_part[0:16]

    opening = -(-ffn_count // PIECES)
    moe_gain_total = jnp.zeros((1, width), jnp.float32)
    lag = n_t - 2
    for turn in range(PIECES + lag + n_t - 1):
        back_line.forward(turn, ends_first)
        if turn + 1 < PIECES:
            back_line.drain(ends_first, turn)
            back_line.originate(ends_first, (turn + 1,))
        for e in range(turn * opening, min((turn + 1) * opening, ffn_count)):
            expert.open(e, ffn_count)
        if 0 <= turn - lag < PIECES:
            n = turn - lag
            at = slice(n * (local // PIECES), (n + 1) * (local // PIECES))
            back_line.collect(acc, n)
            norm_grad = acc[at, :] + side_back[at, :]
            hidden = hidden_ref[at, :]
            scale = lax.rsqrt(jnp.mean(hidden * hidden, axis=1, keepdims=True) + EPSILON)
            u = norm_grad * moe_gain_ref[...].reshape(1, width)
            moe_gain_total = moe_gain_total + jnp.sum(
                norm_grad * hidden * scale, axis=0, keepdims=True
            )
            hidden_grad[at, :] = (
                grad_ref[at, :].astype(jnp.float32)
                + scale * u
                - hidden
                * (scale * scale * scale)
                * jnp.mean(u * hidden, axis=1, keepdims=True)
            )
            grad_rows[place, at, :] = hidden_grad[at, :].astype(jnp.bfloat16)
            if n == PIECES - 1:
                back_line.finish()
            gather.start(n)
        for step in range(1, n_t):
            if 0 <= turn - lag - step < PIECES:
                gather.step(step, turn - lag - step)
    small_out[0:1, :] = moe_gain_total
    small.start(0)
    output_ref[...] = (pair_buf[...] + sum_ref[...]).astype(output_ref.dtype)
    advance = over_experts(lambda e: expert.advance(e, 0))

    rows = local

    def row_block(n):
        return pl.ds(pl.multiple_of(n * rows, rows), rows)

    count = n_t
    head_lane = lax.broadcasted_iota(jnp.int32, (rows, 128), 1)
    low_half = head_lane < 64
    for block in range(count):
        at = pl.ds(block * rows, rows)
        product = dot_nt(grad_rows[block], out_w_ref[...])
        for h in range(heads):
            piece = product[:, h * 128 : (h + 1) * 128].astype(jnp.bfloat16)
            double_grad[h, at, :] = piece
            both = piece.astype(jnp.float32) * o_ref[h, at, :].astype(jnp.float32)
            delta[h : h + 1, at] = 0.5 * jnp.sum(both.T, axis=0, keepdims=True)
    out_pack = []
    for h in range(0, heads, 2):
        o_a = o_ref[h]
        o_b = o_ref[h + 1] if h + 1 < heads else jnp.zeros_like(o_a)
        lanes = lax.broadcasted_iota(jnp.int32, o_a.shape, 1)
        out_pack.append(jnp.where(lanes < 64, o_a, o_b))
    n_half = attn_pairs.shape[2]
    step_rows = attn_pairs.shape[3]
    qkv_width = packed.shape[1]

    def spread(product, start, stop):
        low = product.astype(jnp.bfloat16)
        for d in range(2 * n_half):
            attn_pairs[0, d % 2, d // 2, :, start:stop] = low[d * step_rows : (d + 1) * step_rows]

    for n, pack in enumerate(out_pack):
        total = jnp.zeros((width, 128), jnp.float32)
        for block in range(count):
            total = total + dot_tn(grad_rows[block], pack[block * rows : (block + 1) * rows])
        spread(total, qkv_width + n * 128, qkv_width + (n + 1) * 128)

    dq[...] = jnp.zeros_like(dq)
    factor = 64 ** (-0.5)
    gain_total = jnp.zeros((1, width), jnp.float32)
    small_turn = 0
    for key_block in range(count):
        keys = pl.ds(key_block * rows, rows)
        dk[...] = jnp.zeros_like(dk)
        dv[...] = jnp.zeros_like(dv)

        def query_step(query_block, _, keys=keys):
            at = row_block(query_block)
            for h in range(heads):
                q, g = q_ref[h, at, :], double_grad[h, at, :]
                k, v = k_ref[h, keys, :], v_ref[h, keys, :]
                scores = dot_nt(k, q) * (0.5 * factor)
                probs = jnp.exp(scores - lse_ref[h : h + 1, at])
                d_probs = dot_nt(v, g) * 0.5
                d_scores = (probs * (d_probs - delta[h : h + 1, at])).astype(jnp.bfloat16)
                dk[h] += dot(d_scores, q)
                dv[h] += dot(probs.astype(jnp.bfloat16), g)
                dq[h, at, :] += dot_tn(d_scores, k)
            return 0

        lax.fori_loop(key_block, count, query_step, 0)
        table = table_ref[keys, :]
        pieces = []
        for source in (dq.at[:, keys, :], dk):
            for h in range(heads):
                turned = source[h] * (table * factor)
                pieces.append(turned + pltpu.roll(turned, 64, 1))
        for h in range(heads):
            pieces.append(dv[h])
        if len(pieces) % 2:
            pieces.append(jnp.zeros((rows, 128), jnp.float32))
        for n in range(0, len(pieces), 2):
            packed[keys, n * 64 : n * 64 + 128] = jnp.where(
                low_half, pieces[n], pieces[n + 1]
            ).astype(jnp.bfloat16)
        back_rows = dot(packed[keys, :], qkv_ref[...])
        gain_total = gain_total + jnp.sum(
            back_rows * rows_ref[key_block].astype(jnp.float32), axis=0, keepdims=True
        )
        attn_part[key_block] = back_rows.astype(jnp.bfloat16)
        attn_line.originate((key_block,))
        if key_block > 0:
            attn_line.forward_all(key_block - 1)
        if key_block < n_t - 1:
            first_e = key_block * ffn_count // (n_t - 1)
            advance(first_e, (key_block + 1) * ffn_count // (n_t - 1))
        if small_turn < small_in.shape[0]:
            small.take(small_turn)
            small_turn += 1
            if small_turn < small_in.shape[0]:
                small.start(small_turn)

    gains[0] = gain_total / attn_gain_ref[...].reshape(1, width)
    gain.start(0)
    for n in range(qkv_width // 128):
        total = jnp.zeros((width, 128), jnp.float32)
        for block in range(count):
            total = total + dot_tn(
                rows_ref[block], packed[pl.ds(block * rows, rows), n * 128 : (n + 1) * 128]
            )
        spread(total, n * 128, (n + 1) * 128)
    attn.start(0)
    attn_line.forward_all(count - 1)
    gain.take(0)
    gain.start(1)
    attn.open(0)
    for stage in range(1, stage_count - 1):
        over_experts(lambda e, stage=stage: expert.advance(e, stage))(0, ffn_count)
    while small_turn < small_in.shape[0]:
        small.take(small_turn)
        small_turn += 1
        if small_turn < small_in.shape[0]:
            small.start(small_turn)
    for stage in range(stage_count - 1):
        attn.advance(0, stage)
    gain.take(1)
    gain_out[...] = jnp.broadcast_to(gains[2], gain_out.shape)
    for n in range(PIECES):
        attn_line.collect(acc, n)
    wide = input_ref[...].astype(jnp.float32)
    scale = lax.rsqrt(jnp.mean(wide * wide, axis=1, keepdims=True) + EPSILON)
    w = acc[...] * attn_gain_ref[...].reshape(1, width)
    input_grad_ref[...] = (
        hidden_grad[...]
        + scale * w
        - wide * (scale * scale * scale) * jnp.mean(w * wide, axis=1, keepdims=True)
    ).astype(input_grad_ref.dtype)
    def stored(e):
        return pltpu.make_async_copy(staged.at[e % 2], expert_out.at[e], staged_sem.at[e])

    for e in range(ffn_count if inside else 0):
        if e > 1:
            stored(e - 2).wait()
        expert.close(e, staged.at[e % 2])
        stored(e).start()
    attn.close(0, attn_out)

    attn_line.finish()
    for step in range(1, n_t):
        chosen_copy(step).wait_send()
    gather.finish()

    def ended(e, _):
        expert.finish(e)
        return 0

    lax.fori_loop(0, ffn_count, ended, 0)
    attn.finish(0)
    for e in range(ffn_count - 2, ffn_count if inside else 0):
        stored(e).wait()


def backward(dp_count, n_t, ffn_sum, ffn_back, chosen, weight_pairs, hidden, moe_rows, grad_out,
             layer_input, routes, residual, router, gates, const_value, moe_gain, attn_gain,
             q2, k2, v2, o2, lse, attn_rows, qkv_weight, out_double, table):
    local, width = hidden.shape
    group = local * n_t
    ffn_count = weight_pairs[0].shape[0]
    units = weight_pairs[0].shape[-1]
    step = width // dp_count
    half = dp_count // 2
    dp_bits = log2_of(dp_count)
    inside = reduced_inside(step)
    stage_count = dp_bits - 1 if inside else 0
    tensor_bits = log2_of(n_t)
    heads = q2.shape[0]
    qkv_width = qkv_weight.shape[0]
    attn_width = qkv_width + -(-heads // 2) * 128
    attn_split = attn_width // 2 // 128 * 128
    bf, f32 = jnp.bfloat16, jnp.float32
    dma = pltpu.SemaphoreType.DMA
    rounds = dp_bits + tensor_bits

    def numbers(stage):
        return half >> (stage + 1)

    def line(rows_shape):
        return pltpu.VMEM((n_t + 1, *rows_shape[1:]), bf)

    block_shape = (n_t, local, width)
    reduction = []
    if inside:
        reduction = [
            pltpu.VMEM((1, 2, half, step, attn_width), bf),
            pltpu.VMEM((ffn_count, half, step, units), bf),
            pltpu.VMEM((min(4, ffn_count), half, step, units), bf),
            *[pltpu.VMEM((ffn_count, numbers(s), step, units), bf) for s in range(stage_count)],
            pltpu.VMEM((1, half, step, attn_width), bf),
            pltpu.VMEM((1, half, step, attn_width), bf),
            *[pltpu.VMEM((1, numbers(s), step, attn_width), bf) for s in range(stage_count)],
        ]
    scratch = [
        pltpu.VMEM((n_t - 1, ffn_count, local), f32),
        pltpu.VMEM((local, width), f32),
        line(block_shape),
        pltpu.VMEM((2, step, units), f32),
        pltpu.VMEM((128, width), f32),
        pltpu.VMEM((128, local), f32),
        pltpu.VMEM(block_shape, bf),
        pltpu.VMEM(block_shape, bf),
        pltpu.VMEM((local, width), f32),
        pltpu.VMEM((local, width), f32),
        pltpu.VMEM((heads, group, 128), bf),
        pltpu.VMEM((8, group), f32),
        pltpu.VMEM((heads, group, 128), f32),
        pltpu.VMEM((heads, local, 128), f32),
        pltpu.VMEM((heads, local, 128), f32),
        pltpu.VMEM((group, qkv_width), bf),
        *reduction,
        pltpu.VMEM((rounds, 24, width), f32),
        pltpu.VMEM((3, 1, width), f32),
        pltpu.VMEM((dp_count - 1, 1, width), f32),
        pltpu.VMEM((n_t - 1, 1, width), f32),
        pltpu.VMEM((local, width), f32),
        dma((n_t - 1,)),
        dma((n_t - 1,)),
        dma((2, n_t, PIECES)),
        dma((n_t, PIECES)),
        dma((2, n_t, PIECES)),
        dma((2, n_t, PIECES)),
        dma((2, n_t, PIECES)),
        dma((2, n_t, PIECES)),
        *[
            s
            for n in ((ffn_count, 1) if inside else ())
            for s in (
                *[dma((n,)) for _ in range(2 if n == ffn_count else 3)],
                *[dma((n, 2, numbers(s))) for s in range(stage_count)],
                *[dma((n, 2, numbers(s))) for s in range(stage_count)],
            )
        ],
        dma((rounds,)),
        dma((rounds,)),
        dma((dp_count - 1,)),
        dma((n_t - 1,)),
        dma((dp_count - 1,)),
        dma((n_t - 1,)),
        dma((ffn_count,)),
    ]
    vmem = pl.BlockSpec(memory_space=pltpu.VMEM)
    operands = (ffn_sum, ffn_back, chosen, hidden, moe_rows, grad_out, layer_input, routes, residual,
                router, gates, const_value, moe_gain, attn_gain, q2, k2, v2, o2, lse, attn_rows,
                qkv_weight, out_double, table)
    specs = [vmem] * len(operands)
    if inside:
        operands = (*operands, *weight_pairs)
        specs += [pl.BlockSpec(memory_space=pl.ANY)] * 2
    return pl.pallas_call(
        functools.partial(
            backward_kernel, (dp_bits, n_t, ffn_count, residual.shape[0], attn_split, inside)
        ),
        out_shape=(
            jax.ShapeDtypeStruct((local, width), bf),
            jax.ShapeDtypeStruct((local, width), bf),
            jax.ShapeDtypeStruct((ffn_count, step, units) if inside else (8, 128), f32),
            jax.ShapeDtypeStruct((step, attn_width), f32)
            if inside
            else jax.ShapeDtypeStruct((1, 2, half, step, attn_width), bf),
            jax.ShapeDtypeStruct((24, width), f32),
            jax.ShapeDtypeStruct((8, width), f32),
        ),
        in_specs=specs,
        out_specs=(vmem, vmem, pl.BlockSpec(memory_space=pl.ANY), vmem, vmem, vmem),
        scratch_shapes=scratch,
        compiler_params=pltpu.CompilerParams(
            collective_id=1, has_side_effects=True, vmem_limit_bytes=62 << 20
        ),
        name="backward",
    )(*operands)


def rope_lanes(length, head_width):
    position = np.arange(length, dtype=np.float64)[:, None]
    inverse = np.exp(np.arange(head_width // 2) * (-2.0 * math.log(10000.0) / head_width))
    angle = position * inverse[None, :]
    c, s = np.cos(angle), np.sin(angle)
    cosine = np.concatenate([c, c, c, c], axis=1).astype(np.float32)
    sine = np.concatenate([-s, s, s, -s], axis=1).astype(np.float32)
    return cosine, sine


def tidy_kernel(
    wide, route_count, gate_ref, up_ref, down_ref, attn_ref, small_ref, gain_ref, output_ref, grad_ref, *outs
):
    (output, grad, attn_gain, q_out, k_out, v_out, out_out, moe_gain, router, gates, value) = outs[:11]
    for source, target in zip((gate_ref, up_ref, down_ref), outs[11:]):
        target[...] = source[...]

    @pl.when(pl.program_id(0) == 0)
    def _():
        output[...] = output_ref[...]
        grad[...] = grad_ref[...]
        attn_gain[...] = gain_ref[0, :]
        moe_gain[...] = small_ref[0, :]
        value[...] = small_ref[1:3, :]
        router[...] = small_ref[8 : 8 + route_count, :]
        for c in range(2):
            at = 8 + route_count + 2 * c
            gates[c] = small_ref[at : at + 2, :]
        for n, ref in enumerate((q_out, k_out, v_out)):
            ref[...] = attn_ref[:, n * wide : (n + 1) * wide]
        at = -(-3 * wide // 128) * 128
        out_out[...] = attn_ref[:, at : at + -(-wide // 128) * 128].T[0:wide, :]


def tidy(wide, route_count, expert_sum, attn_sum, small, gain, output, input_grad):
    count, step, units = expert_sum.shape
    units = units // 3
    width = small.shape[1]
    f32 = jnp.float32
    group = 2 if count % 2 == 0 else 1

    def whole(shape):
        return pl.BlockSpec(shape, lambda e: (0,) * len(shape), pipeline_mode=pl.Buffered(1))

    small_shapes = (
        (width,),
        (step, wide),
        (step, wide),
        (step, wide),
        (wide, step),
        (width,),
        (route_count, width),
        (2, 2, width),
        (2, width),
    )
    shapes = [output, input_grad]
    shapes += [jax.ShapeDtypeStruct(shape, f32) for shape in small_shapes]
    shapes += [jax.ShapeDtypeStruct((count, step, units), f32)] * 3
    piece = [
        pl.BlockSpec((group, step, units), lambda e, n=n: (e, 0, n)) for n in (0, 1, 2, 0, 0, 0)
    ]
    rest = (attn_sum, small, gain, output, input_grad)
    return pl.pallas_call(
        functools.partial(tidy_kernel, wide, route_count),
        grid=(count // group,),
        out_shape=tuple(jax.ShapeDtypeStruct(s.shape, s.dtype) for s in shapes),
        in_specs=[*piece[:3], *[whole(a.shape) for a in rest]],
        out_specs=(*[whole(s.shape) for s in shapes[:11]], *piece[3:]),
        compiler_params=pltpu.CompilerParams(
            dimension_semantics=("arbitrary",), vmem_limit_bytes=32 << 20
        ),
        name="tidy",
    )(expert_sum, expert_sum, expert_sum, *rest)


def on_device(
    layer_input,
    attn_gain,
    query_weight,
    key_weight,
    value_weight,
    out_weight,
    moe_gain,
    router_weight,
    gate_residual,
    const_gate,
    const_value,
    gate_weight,
    up_weight,
    down_weight,
    routes,
    grad_out,
):
    local_rows, model_width = layer_input.shape
    tensor_size = lax.axis_size("tensor")
    head_count = query_weight.shape[1] // HD
    ffn_count = gate_weight.shape[0]
    route_count = router_weight.shape[1]
    cosine, sine = rope_lanes(LENGTH, HD)
    q2, k2, v2, o2, lse, attn_rows, moe_rows, grad_half, hidden, qkv_weight, out_double = forward(
        tensor_size,
        layer_input,
        attn_gain,
        moe_gain,
        query_weight.T,
        key_weight.T,
        value_weight.T,
        out_weight,
        grad_out,
        jnp.asarray(cosine),
        jnp.asarray(sine),
    )
    n_dp = lax.axis_size("dp")
    ffn_back, ffn_sum, chosen_t, *weight_pairs = experts(
        n_dp,
        tensor_size,
        moe_rows,
        grad_half,
        grad_out,
        routes.T,
        gate_residual.T,
        router_weight.T,
        gate_weight,
        up_weight,
        down_weight,
    )
    output, input_grad, expert_sum, attn_sum_rows, small, gain = backward(
        n_dp,
        tensor_size,
        ffn_sum,
        ffn_back,
        chosen_t,
        weight_pairs,
        hidden,
        moe_rows,
        grad_out,
        layer_input,
        routes.T,
        gate_residual.T,
        router_weight.T,
        jnp.transpose(const_gate, (0, 2, 1)),
        const_value,
        moe_gain,
        attn_gain,
        q2,
        k2,
        v2,
        o2,
        lse,
        attn_rows,
        qkv_weight,
        out_double,
        jnp.asarray(np.concatenate([cosine[:, :HD], sine[:, HD:]], axis=1)),
    )
    if not reduced_inside(model_width // n_dp):

        def scattered(pairs):
            pairs = jnp.transpose(pairs, (2, 1, 3, 0, 4)).reshape(model_width, -1)
            return lax.psum_scatter(pairs, "dp", scatter_dimension=0, tiled=True).astype(
                jnp.float32
            )

        attn_sum_rows = scattered(attn_sum_rows)
        expert_sum = scattered(weight_pairs[0]).reshape(
            model_width // n_dp, ffn_count, weight_pairs[0].shape[-1]
        )
        expert_sum = jnp.transpose(expert_sum, (1, 0, 2))
    outs = list(
        tidy(
            head_count * HD, route_count, expert_sum, attn_sum_rows, small, gain, output, input_grad
        )
    )
    outs[8] = outs[8].T
    outs[9] = jnp.transpose(outs[9], (0, 2, 1))
    outs[13] = jnp.transpose(outs[13], (0, 2, 1))
    return tuple(outs)


def solution(mesh):
    in_specs = (
        P(("dp", "tensor"), None),
        P(),
        P(None, "tensor"),
        P(None, "tensor"),
        P(None, "tensor"),
        P("tensor", None),
        P(),
        P(),
        P("dp", None),
        P(),
        P(),
        P(None, None, "tensor"),
        P(None, None, "tensor"),
        P(None, "tensor", None),
        P("dp", None),
        P(("dp", "tensor"), None),
    )
    out_specs = (
        P(("dp", "tensor"), None),
        P(("dp", "tensor"), None),
        P(),
        P("dp", "tensor"),
        P("dp", "tensor"),
        P("dp", "tensor"),
        P("tensor", "dp"),
        P(),
        P(),
        P(),
        P(),
        P(None, "dp", "tensor"),
        P(None, "dp", "tensor"),
        P(None, "tensor", "dp"),
    )
    return jax.shard_map(
        on_device, mesh=mesh, in_specs=in_specs, out_specs=out_specs, check_vma=False
    )
```

```python
import functools
import math

import jax
import jax.numpy as jnp
import numpy as np
from jax import lax
from jax.experimental import pallas as pl
from jax.experimental.pallas import tpu as pltpu
from jax.sharding import PartitionSpec as P

HD = 64
LENGTH = 1024
BLOCK = 256
CAP = 256


EPSILON = 1e-06
MASKED = -1e30


EXP_PAD = 16


def dot(a, b):
    return jnp.dot(a, b, preferred_element_type=jnp.float32)


def dot_nt(a, b):
    return lax.dot_general(a, b, (((1,), (1,)), ((), ())), preferred_element_type=jnp.float32)


def dot_tn(a, b):
    return lax.dot_general(a, b, (((0,), (0,)), ((), ())), preferred_element_type=jnp.float32)


def three_parts(values):
    first = values.astype(jnp.bfloat16)
    rest = values - first.astype(jnp.float32)
    second = rest.astype(jnp.bfloat16)
    third = (rest - second.astype(jnp.float32)).astype(jnp.bfloat16)
    return (first, second, third)


MESH = pl.DeviceIdType.MESH
PIECES = 8
GRAD_PIECES = 2
SUM_PIECES = 4
LINE_TURNS = (1, 3, 5, 7)
EARLY = 4


def bit_of(index, position):
    return index // (1 << position) % 2


def flipped(index, position):
    return index + (1 << position) * (1 - 2 * bit_of(index, position))


def log2_of(count):
    return count.bit_length() - 1


def greet(axes):
    barrier = pltpu.get_barrier_semaphore()
    for axis, index, count in axes:

        def body(step, _, axis=axis, index=index, count=count):
            pl.semaphore_signal(
                barrier, inc=1, device_id={axis: (index + step) % count}, device_id_type=MESH
            )
            return 0

        lax.fori_loop(1, count, body, 0)
    pl.semaphore_wait(barrier, sum(count - 1 for _, _, count in axes))


class LineGather:
    def __init__(self, blocks, send, recv, place, pieces=1):
        self.blocks, self.send, self.recv, self.place = blocks, send, recv, place
        self.count, self.pieces = blocks.shape[0], pieces
        self.rows = blocks.shape[1] // pieces

    def copy(self, block, n, way):
        piece = self.blocks.at[block, pl.ds(n * self.rows, self.rows)]
        return pltpu.make_async_remote_copy(
            src_ref=piece,
            dst_ref=piece,
            send_sem=self.send.at[way, block, n],
            recv_sem=self.recv.at[block, n],
            device_id={"tensor": self.place + 1 - 2 * way},
            device_id_type=MESH,
        )

    def start(self, n=0):
        @pl.when(self.place < self.count - 1)
        def _():
            self.copy(self.place, n, 0).start()

        @pl.when(self.place > 0)
        def _():
            self.copy(self.place, n, 1).start()

    def step(self, distance, n=0):
        below, above = self.place - distance, self.place + distance

        @pl.when(below >= 0)
        def _():
            self.copy(below, n, 0).wait_recv()

            @pl.when(self.place < self.count - 1)
            def _():
                self.copy(below, n, 0).start()

        @pl.when(above < self.count)
        def _():
            self.copy(above, n, 1).wait_recv()

            @pl.when(self.place > 0)
            def _():
                self.copy(above, n, 1).start()

    def finish(self, pieces=None):
        pieces = range(self.pieces) if pieces is None else pieces
        for distance in range(self.count):
            below, above = self.place - distance, self.place + distance

            @pl.when((below >= 0) & (self.place < self.count - 1))
            def _(below=below):
                for n in pieces:
                    self.copy(below, n, 0).wait_send()

            @pl.when((above < self.count) & (self.place > 0))
            def _(above=above):
                for n in pieces:
                    self.copy(above, n, 1).wait_send()


class LineScatter:
    def __init__(self, parts, arrived, send, recv, place, pieces):
        self.parts, self.arrived, self.send, self.recv = parts, arrived, send, recv
        self.place, self.count, self.pieces = place, parts.shape[0], pieces
        self.rows = parts.shape[1] // pieces
        self.drained = set()

    def piece(self, ref, block, n):
        return ref.at[block, pl.ds(n * self.rows, self.rows)]

    def copy(self, block, n, way, own=False):
        there = self.piece(self.arrived, block + 1 - way, n)
        return pltpu.make_async_remote_copy(
            src_ref=self.piece(self.parts, block, n) if own else there,
            dst_ref=there,
            send_sem=self.send.at[way, block, n],
            recv_sem=self.recv.at[way, block, n],
            device_id={"tensor": self.place + 1 - 2 * way},
            device_id_type=MESH,
        )

    def originate(self, blocks, pieces=None):
        for way, first in ((0, 0), (1, self.count - 1)):
            sent = [block for block in blocks if block != first]
            if sent:

                @pl.when(self.place == first)
                def _(way=way, sent=sent):
                    for n in pieces or range(self.pieces):
                        for block in sent:
                            self.copy(block, n, way, own=True).start()

    def drain(self, blocks, n):
        for way, first in ((0, 0), (1, self.count - 1)):
            sent = [block for block in blocks if block != first]
            self.drained.update((first, block, n) for block in sent)
            if sent:

                @pl.when(self.place == first)
                def _(way=way, sent=sent):
                    for block in sent:
                        self.copy(block, n, way).wait_send()

    def pass_piece(self, block, n, way):
        self.copy(block, n, way).wait_recv()
        there = self.piece(self.arrived, block + 1 - way, n)
        mine = self.piece(self.parts, block, n)
        there[...] = (there[...].astype(jnp.float32) + mine[...].astype(jnp.float32)).astype(
            there.dtype
        )
        self.copy(block, n, way).start()

    def hops(self, place, way):
        return place if way == 0 else self.count - 1 - place

    def forward(self, turn, blocks):
        for place in range(1, self.count - 1):
            passed = []
            for block in blocks:
                way = 0 if place < block else 1
                n = turn - self.hops(place, way) + 1
                if place != block and 0 <= n < self.pieces:
                    passed.append((self.hops(place, way), block, n, way))
            if passed:

                @pl.when(self.place == place)
                def _(passed=passed):
                    for _, block, n, way in sorted(passed, key=lambda item: -item[0]):
                        self.pass_piece(block, n, way)

    def forward_all(self, block):
        for turn in range(self.pieces + self.count - 3):
            self.forward(turn, (block,))

    def collect(self, total, n):
        place = self.place
        rows = slice(n * self.rows, (n + 1) * self.rows)
        total[rows, :] = self.parts[place, rows, :].astype(jnp.float32)
        for way in (0, 1):

            @pl.when(place > 0 if way == 0 else place < self.count - 1)
            def _(way=way):
                self.copy(place, n, way).wait_recv()
                total[rows, :] += self.arrived[place + 1 - way, rows, :].astype(jnp.float32)

    def finish(self):
        for place in range(self.count):
            left = [
                (block, n)
                for block in range(self.count)
                for n in range(self.pieces)
                if block != place and (place, block, n) not in self.drained
            ]
            if left:

                @pl.when(self.place == place)
                def _(place=place, left=left):
                    for block, n in left:
                        self.copy(block, n, 0 if place < block else 1).wait_send()


class Halving:
    def __init__(self, source, kept, first, stages, sems, dp, dp_bits, splits):
        self.source, self.kept, self.first, self.stages = source, kept, first, stages
        self.first_send, self.first_recv, self.local, self.send, self.recv = sems
        self.dp, self.bits, self.splits = dp, dp_bits, splits
        self.core = bit_of(dp, 0)
        upper = list(range(dp_bits - 1))
        self.orders = (upper, upper[1:] + upper[:1])

    def first_copy(self, e):
        return pltpu.make_async_remote_copy(
            src_ref=self.source.at[e, 1 - self.core],
            dst_ref=self.first.at[e],
            send_sem=self.first_send.at[e],
            recv_sem=self.first_recv.at[e],
            device_id={"dp": flipped(self.dp, 0)},
            device_id_type=MESH,
        )

    def local_copy(self, e):
        return pltpu.make_async_copy(
            self.source.at[e, self.core], self.kept.at[e], self.local.at[e]
        )

    def blocks(self, part, stage, k, mine):
        order = self.orders[part]
        index = 0
        for done in order[:stage]:
            index = index + (1 << done) * bit_of(self.dp, done + 1)
        here = bit_of(self.dp, order[stage] + 1)
        index = index + (1 << order[stage]) * (here if mine else 1 - here)
        for n, free in enumerate(order[stage + 1 :]):
            index = index + (1 << free) * (k // (1 << n) % 2)
        return index

    def width(self, part):
        return pl.ds(*self.splits[part])

    def stage_copy(self, e, part, stage, k):
        start, size = self.splits[part]
        return pltpu.make_async_remote_copy(
            src_ref=self.kept.at[e, self.blocks(part, stage, k, False), :, pl.ds(start, size)],
            dst_ref=self.stages[stage].at[e, k, :, pl.ds(start, size)],
            send_sem=self.send[stage].at[e, part, k],
            recv_sem=self.recv[stage].at[e, part, k],
            device_id={"dp": flipped(self.dp, self.orders[part][stage] + 1)},
            device_id_type=MESH,
        )

    def number(self, stage):
        return 1 << (self.bits - 2 - stage)

    def start(self, e):
        self.first_copy(e).start()
        self.local_copy(e).start()

    def send_stage(self, e, stage):
        for k in range(self.number(stage)):
            for part in (0, 1):
                self.stage_copy(e, part, stage, k).start()

    def add_rows(self, target, addend):
        rows = target.shape[0]
        step = 32 if rows % 32 == 0 else rows

        def body(n, _):
            at = pl.ds(pl.multiple_of(n * step, step), step)
            target[at, :] = (
                target[at, :].astype(jnp.float32) + addend[at, :].astype(jnp.float32)
            ).astype(target.dtype)
            return 0

        lax.fori_loop(0, rows // step, body, 0)

    def open(self, e):
        self.first_copy(e).wait_recv()
        self.local_copy(e).wait()
        for block in range(self.kept.shape[1]):
            self.add_rows(self.kept.at[e, block], self.first.at[e, block])
        self.send_stage(e, 0)

    def advance(self, e, stage, arrived=False):
        for k in range(self.number(stage)):
            for part in (0, 1):
                if not arrived:
                    self.stage_copy(e, part, stage, k).wait_recv()
                block = self.blocks(part, stage, k, True)
                self.add_rows(
                    self.kept.at[e, block, :, self.width(part)],
                    self.stages[stage].at[e, k, :, self.width(part)],
                )
        self.send_stage(e, stage + 1)

    def close(self, e, out):
        stage = self.bits - 2
        for part in (0, 1):
            self.stage_copy(e, part, stage, 0).wait_recv()
            block = self.blocks(part, stage, 0, True)
            columns = self.width(part)
            out[:, columns] = self.kept[e, block, :, columns].astype(jnp.float32) + self.stages[
                stage
            ][e, 0, :, columns].astype(jnp.float32)

    def finish(self, e):
        self.first_copy(e).wait_send()
        for stage in range(self.bits - 1):
            for k in range(self.number(stage)):
                for part in (0, 1):
                    self.stage_copy(e, part, stage, k).wait_send()


class LateHalving(Halving):
    def item_copy(self, e):
        return pltpu.make_async_copy(self.source[0].at[e], self.kept.at[e], self.local.at[e])

    def stage_item(self, e):
        return pltpu.make_async_copy(
            self.source[1].at[e], self.stages[0].at[e], self.first_recv.at[e]
        )

    def begin(self, early, count):
        for e in range(count):
            self.item_copy(e).start()
            if e < early:
                self.stage_item(e).start()

    def open(self, e, early):
        self.item_copy(e).wait()
        if e < early:
            self.stage_item(e).wait()
            self.advance(e, 0, arrived=True)
        else:
            self.send_stage(e, 0)

    def finish(self, e, early):
        for stage in range(self.bits - 1):
            if stage > 0 or e >= early:
                for k in range(self.number(stage)):
                    for part in (0, 1):
                        self.stage_copy(e, part, stage, k).wait_send()


class Exchange:
    def __init__(self, totals, arrived, sends, recvs, axes):
        self.totals, self.arrived, self.sends, self.recvs, self.axes = (
            totals,
            arrived,
            sends,
            recvs,
            axes,
        )

    def copy(self, turn, step):
        axis, index, count = self.axes[turn]
        return pltpu.make_async_remote_copy(
            src_ref=self.totals.at[turn],
            dst_ref=self.arrived[turn].at[step],
            send_sem=self.sends[turn].at[step],
            recv_sem=self.recvs[turn].at[step],
            device_id={axis: (index + step + 1) % count},
            device_id_type=MESH,
        )

    def start(self, turn):
        def body(step, _):
            self.copy(turn, step).start()
            return 0

        lax.fori_loop(0, self.axes[turn][2] - 1, body, 0)

    def take(self, turn):
        self.totals[turn + 1] = self.totals[turn]

        def body(step, _):
            self.copy(turn, step).wait()
            self.totals[turn + 1] += self.arrived[turn][step]
            return 0

        lax.fori_loop(0, self.axes[turn][2] - 1, body, 0)


def reduced_inside(step):
    return step % 32 == 0


class Nothing:
    def __getattr__(self, name):
        return lambda *arguments: None


def select_lanes(rows, columns, source):
    row = lax.broadcasted_iota(jnp.int32, (rows, columns), 0)
    column = lax.broadcasted_iota(jnp.int32, (rows, columns), 1)
    return jnp.where(row == source(column), 1.0, 0.0).astype(jnp.bfloat16)


def forward_kernel(
    n_t,
    input_ref,
    attn_gain_ref,
    moe_gain_ref,
    q_w_ref,
    k_w_ref,
    v_w_ref,
    out_w_ref,
    grad_ref,
    cos_ref,
    sin_ref,
    q_out,
    k_out,
    v_out,
    o_out,
    lse_out,
    rows_out,
    moe_out,
    grad_out,
    hidden_out,
    qkv_out,
    double_out,
    weights,
    part,
    arrived,
    acc,
    rows_send,
    rows_recv,
    grad_send,
    grad_recv,
    moe_send,
    moe_recv,
    line_send,
    line_recv,
):
    place = lax.axis_index("tensor")
    heads = q_out.shape[0]
    local, width = input_ref.shape
    barrier = pltpu.get_barrier_semaphore()
    for step in range(1, n_t):
        pl.semaphore_signal(
            barrier,
            inc=1,
            device_id={"tensor": (place + step) % n_t},
            device_id_type=MESH,
        )
    wide = input_ref[...].astype(jnp.float32)
    scale = lax.rsqrt(jnp.mean(wide * wide, axis=1, keepdims=True) + EPSILON)
    rows_out[place] = (wide * scale * attn_gain_ref[...].reshape(1, width)).astype(jnp.bfloat16)
    grad_out[place] = grad_ref[...]
    pl.semaphore_wait(barrier, n_t - 1)

    rows_gather = LineGather(rows_out, rows_send, rows_recv, place)
    grad_gather = LineGather(grad_out, grad_send, grad_recv, place, GRAD_PIECES)
    moe_gather = LineGather(moe_out, moe_send, moe_recv, place, PIECES)
    line = LineScatter(part, arrived, line_send, line_recv, place, PIECES)
    rows_gather.start()

    columns = heads * HD
    twice = select_lanes(columns, heads * 128, lambda c: c // 128 * HD + c % HD)
    swapped = select_lanes(
        columns,
        heads * 128,
        lambda c: c // 128 * HD + (c % HD + c % 128 // HD * (HD // 2)) % HD,
    )
    for n, (ref, lanes) in enumerate(
        ((q_w_ref, swapped), (k_w_ref, swapped), (v_w_ref, twice))
    ):
        weights[n * heads * 128 : (n + 1) * heads * 128, :] = dot_tn(lanes, ref[...]).astype(
            jnp.bfloat16
        )
    for n, ref in enumerate((q_w_ref, k_w_ref, v_w_ref)):
        qkv_out[n * columns : (n + 1) * columns, :] = ref[...]
    qkv_out[3 * columns :, :] = jnp.zeros(
        (qkv_out.shape[0] - 3 * columns, width), jnp.bfloat16
    )
    double_out[...] = dot_tn(twice, out_w_ref[...]).astype(jnp.bfloat16)

    def project(block):
        at = pl.ds(pl.multiple_of(block * local, local), local)
        product = dot_nt(rows_out[block], weights[...])
        cosine, sine = cos_ref[at, :], sin_ref[at, :]
        for n, target in enumerate((q_out, k_out, v_out)):
            for h in range(heads):
                start = (n * heads + h) * 128
                piece = product[:, start : start + 128]
                if n < 2:
                    piece = piece * cosine + pltpu.roll(piece, 64, 1) * sine
                target[h, at, :] = piece.astype(jnp.bfloat16)

    def arrive(distance, _):
        @pl.when(distance > 0)
        def _():
            rows_gather.step(distance)

        def side(way, _):
            block = place + (2 * way - 1) * distance

            @pl.when((block >= 0) & (block < n_t) & ((distance > 0) | (way == 0)))
            def _():
                project(block)

            return 0

        lax.fori_loop(0, 2, side, 0)
        return 0

    lax.fori_loop(0, n_t, arrive, 0)
    grad_gather.start()

    factor = 0.5 * HD ** (-0.5)

    lse_out[...] = jnp.zeros_like(lse_out)

    def attend(block):
        at = slice(block * local, (block + 1) * local)
        seen = (block + 1) * local
        mixed = []
        for h in range(heads):
            scores = dot_nt(q_out[h, at, :], k_out[h, 0:seen, :]) * factor
            top = jnp.max(scores, axis=1, keepdims=True)
            exps = jnp.exp(scores - top)
            total = jnp.sum(exps, axis=1, keepdims=True)
            probs = (exps / total).astype(jnp.bfloat16)
            out = dot(probs, v_out[h, 0:seen, :]).astype(jnp.bfloat16)
            o_out[h, at, :] = out
            mixed.append(out)
            log_total = jnp.broadcast_to(top + jnp.log(total), (local, 128))
            lse_out[h : h + 1, at] = log_total.T[0:1, :]
        mixed = jnp.concatenate(mixed, axis=1)
        part[block] = (0.5 * dot(mixed, double_out[...])).astype(jnp.bfloat16)

    for block in range(n_t):
        attend(block)
    ends_first = (n_t - 1, 0, *range(n_t - 2, 0, -1))
    line.originate(ends_first, (0,))
    lag = n_t - 2
    for turn in range(PIECES + lag + n_t - 1):
        line.forward(turn, ends_first)
        if turn + 1 < PIECES:
            line.drain(ends_first, turn)
            line.originate(ends_first, (turn + 1,))
        if 0 <= turn - lag < PIECES:
            n = turn - lag
            line.collect(acc, n)
            at = slice(n * (local // PIECES), (n + 1) * (local // PIECES))
            hidden = input_ref[at, :].astype(jnp.float32) + acc[at, :]
            hidden_out[at, :] = hidden
            scale = lax.rsqrt(jnp.mean(hidden * hidden, axis=1, keepdims=True) + EPSILON)
            moe_out[place, at, :] = (hidden * scale * moe_gain_ref[...].reshape(1, width)).astype(jnp.bfloat16)
            moe_gather.start(n)
        for step in range(1, n_t):
            if 0 <= turn - lag - step < PIECES:
                moe_gather.step(step, turn - lag - step)
        if turn % 2 == 0 and turn // 2 + 1 < n_t:
            grad_gather.step(turn // 2 + 1)
    for exchange in (rows_gather, moe_gather, line):
        exchange.finish()
    grad_gather.finish((0,))


def forward(n_t, layer_input, attn_gain, moe_gain, q_w, k_w, v_w, out_w, grad_out, cosine, sine):
    local, width = layer_input.shape
    group = local * n_t
    heads = q_w.shape[0] // HD
    bf, f32 = jnp.bfloat16, jnp.float32
    dma = pltpu.SemaphoreType.DMA
    vmem = pl.BlockSpec(memory_space=pltpu.VMEM)
    blocks = (n_t, local, width)
    qkv_width = -(-3 * heads * HD // 128) * 128
    outs = (
        *[jax.ShapeDtypeStruct((heads, group, 128), bf)] * 4,
        jax.ShapeDtypeStruct((8, group), f32),
        *[jax.ShapeDtypeStruct(blocks, bf)] * 3,
        jax.ShapeDtypeStruct((local, width), f32),
        jax.ShapeDtypeStruct((qkv_width, width), bf),
        jax.ShapeDtypeStruct((heads * 128, width), bf),
    )
    return pl.pallas_call(
        functools.partial(forward_kernel, n_t),
        out_shape=outs,
        in_specs=[vmem] * 10,
        out_specs=(vmem,) * len(outs),
        scratch_shapes=[
            pltpu.VMEM((3 * heads * 128, width), bf),
            pltpu.VMEM(blocks, bf),
            pltpu.VMEM((n_t + 1, local, width), bf),
            pltpu.VMEM((local, width), f32),
            *[s for n in (1, GRAD_PIECES, PIECES) for s in (dma((2, n_t, n)), dma((n_t, n)))],
            dma((2, n_t, PIECES)),
            dma((2, n_t, PIECES)),
        ],
        compiler_params=pltpu.CompilerParams(
            collective_id=2, has_side_effects=True, vmem_limit_bytes=56 << 20
        ),
        name="forward",
    )(layer_input, attn_gain, moe_gain, q_w, k_w, v_w, out_w, grad_out, cosine, sine)


def expert_kernel(
    sizes,
    moe_ref,
    half_ref,
    grad_ref,
    routes_ref,
    residual_ref,
    router_ref,
    gate_ref,
    up_ref,
    down_ref,
    back_ref,
    sum_ref,
    chosen_ref,
    *rest,
):
    n_dp, n_t, ffn_count, route_count, inside = sizes
    weight_outs = rest[: 2 if inside else 1]
    (
        probs_s,
        rank_s,
        router_s,
        hit_s,
        turned_s,
        slot_s,
        rows_s,
        gate_s,
        up_s,
        active_s,
        out_s,
        grad_s,
        part_s,
        arrived_s,
        acc,
        weight_s,
        grad_send,
        grad_recv,
        half_sem,
        line_send,
        line_recv,
        own_sem,
        *paired,
    ) = rest[2 if inside else 1 :]
    turn = pl.program_id(0)
    expert = turn % ffn_count
    slot = turn % 2
    dp = lax.axis_index("dp")
    place = lax.axis_index("tensor")
    local, width = grad_ref.shape
    rows = n_t * local
    hidden = gate_ref.shape[2]
    step = width // n_dp
    grad_rows = local // GRAD_PIECES
    gather = LineGather(grad_s, grad_send, grad_recv, place, GRAD_PIECES)
    line = LineScatter(part_s, arrived_s, line_send, line_recv, place, SUM_PIECES)
    blocks = tuple(range(n_t))
    ends_first = (n_t - 1, 0, *range(n_t - 2, 0, -1))

    def line_turn(n):
        line.forward(n, ends_first)
        if n + 1 < SUM_PIECES:
            line.drain(ends_first, n)
            line.originate(ends_first, (n + 1,))

    def half_copy(block):
        return pltpu.make_async_copy(
            half_ref.at[block, pl.ds(0, grad_rows)],
            grad_s.at[block, pl.ds(0, grad_rows)],
            half_sem.at[block],
        )

    early = min(EARLY, ffn_count)
    core = bit_of(dp, 0)
    if inside:
        pair_s, pair_send, pair_recv, stage_send, stage_recv = paired
        splits = ((0, 3 * hidden // 2), (3 * hidden // 2, 3 * hidden // 2))
        sems = (None, None, None, [stage_send], [stage_recv])
        halving = Halving(
            None, pair_s, None, [weight_outs[1]], sems, dp, log2_of(n_dp), splits
        )

    def own_copy(e, at):
        return pltpu.make_async_copy(
            pair_s.at[e] if inside else weight_s.at[at], weight_outs[0].at[e], own_sem.at[e]
        )

    def pair_copy(e, at):
        return pltpu.make_async_remote_copy(
            src_ref=weight_s.at[at, 1 - core],
            dst_ref=pair_s.at[e],
            send_sem=pair_send.at[e],
            recv_sem=pair_recv.at[e],
            device_id={"dp": flipped(dp, 0)},
            device_id_type=MESH,
        )

    def left(e, at):
        if inside:
            pair_copy(e, at).wait_send()
        else:
            own_copy(e, at).wait()

    def settle(e, at):
        pair_copy(e, at).wait_recv()
        for block in range(n_dp // 2):
            halving.add_rows(pair_s.at[e, block], weight_s.at[at, core, block])
        own_copy(e, at).start()

        @pl.when(e < early)
        def _():
            halving.send_stage(e, 0)

    def combine(block):
        at = slice(block * local, (block + 1) * local)
        out = out_s[...].reshape(ffn_count * CAP, width)
        return dot(turned_s[at, :], out).astype(jnp.bfloat16)

    @pl.when(turn == 0)
    def _():
        for block in blocks:
            half_copy(block).start()
        grad_s[place, grad_rows:, :] = grad_ref[grad_rows:, :]
        greet((("tensor", place, n_t), ("dp", dp, n_dp)))
        gather.start(1)
        router_s[...] = jnp.zeros_like(router_s)
        router_s[0:route_count, :] = router_ref[...]
        parts = three_parts(router_s[...])
        logits = jnp.concatenate(
            [residual_ref[...], jnp.zeros((EXP_PAD - route_count, rows), jnp.float32)], axis=0
        )
        moe = moe_ref[...].reshape(rows, width)
        for part in parts:
            logits = logits + dot_nt(part, moe)
        index = lax.broadcasted_iota(jnp.int32, (EXP_PAD, rows), 0)
        logits = jnp.where(index < route_count, logits, MASKED)
        top = jnp.max(logits, axis=0, keepdims=True)
        exps = jnp.exp(logits - top)
        probs_s[...] = exps / jnp.sum(exps, axis=0, keepdims=True)
        named = (routes_ref[0:1, :] == index) | (routes_ref[1:2, :] == index)
        named = jnp.where(named, 1.0, 0.0)
        before = lax.broadcasted_iota(jnp.int32, (256, 256), 0)
        after = lax.broadcasted_iota(jnp.int32, (256, 256), 1)
        earlier = jnp.where(before < after, 1.0, 0.0).astype(jnp.bfloat16)
        total = jnp.zeros((EXP_PAD, 1), jnp.float32)
        for start in range(0, rows, 256):
            block = named[:, start : start + 256]
            rank = dot(block.astype(jnp.bfloat16), earlier) + total
            rank_s[:, start : start + 256] = jnp.where(block > 0.5, rank, -1.0)
            total = total + jnp.sum(block, axis=1, keepdims=True)

    @pl.when(turn < ffn_count)
    def _():
        place_in = lax.broadcasted_iota(jnp.int32, (CAP, rows), 0).astype(jnp.float32)
        hit = rank_s[pl.ds(expert, 1), :] == place_in
        slot_weight = jnp.sum(
            jnp.where(hit, probs_s[pl.ds(expert, 1), :], 0.0), axis=1, keepdims=True
        )
        slot_s[expert] = slot_weight
        dispatch = jnp.where(hit, 1.0, 0.0).astype(jnp.bfloat16)
        hit_s[expert] = dispatch
        turned_s[:, pl.ds(pl.multiple_of(expert * CAP, CAP), CAP)] = dispatch.T
        rows_in = dot(dispatch, moe_ref[...].reshape(rows, width)).astype(jnp.bfloat16)
        rows_s[expert] = rows_in
        gate_pre = dot(rows_in, gate_ref[0])
        up_pre = dot(rows_in, up_ref[0])
        sigmoid = 1.0 / (1.0 + jnp.exp(-gate_pre))
        silu = gate_pre * sigmoid
        active = (silu * up_pre).astype(jnp.bfloat16)
        active_s[expert] = active
        gate_s[expert] = up_pre * (sigmoid + silu * (1.0 - sigmoid))
        up_s[expert] = silu
        out_s[expert] = (dot(active, down_ref[0]) * slot_weight).astype(jnp.bfloat16)
        for distance in range(1, n_t - 1):

            @pl.when(turn == 3 * distance - 2)
            def _(distance=distance):
                gather.step(distance, 1)

    @pl.when(turn == ffn_count)
    def _():
        for block in blocks:
            part_s[block] = combine(block)
            half_copy(block).wait()
        line.originate(ends_first, (0,))
        gather.step(n_t - 1, 1)

    @pl.when(turn >= ffn_count)
    def _():
        active = active_s[expert]
        rows_grad = dot(hit_s[expert], grad_s[...].reshape(rows, width))
        low = rows_grad.astype(jnp.bfloat16)
        grad_active = dot_nt(low, down_ref[0])
        slot_weight = slot_s[expert]
        inner = jnp.sum(grad_active * active.astype(jnp.float32), axis=1, keepdims=True)
        lane = lax.broadcasted_iota(jnp.int32, (CAP, 128), 1)
        inner_parts = jnp.zeros((CAP, 128), jnp.float32)
        for n, inner_part in enumerate(three_parts(inner)):
            inner_parts = jnp.where(lane == n, inner_part.astype(jnp.float32), inner_parts)
        chosen_rows = dot_tn(inner_parts.astype(jnp.bfloat16), hit_s[expert])
        chosen_row = chosen_rows[0:1] + chosen_rows[1:2] + chosen_rows[2:3]
        for n in blocks:
            chosen_ref[n, pl.ds(expert, 1), :] = chosen_row[:, n * local : (n + 1) * local]
        grad_low = (rows_grad * slot_weight).astype(jnp.bfloat16)
        grad_active = grad_active * slot_weight
        grad_gate = (grad_active * gate_s[expert]).astype(jnp.bfloat16)
        grad_up = (grad_active * up_s[expert]).astype(jnp.bfloat16)
        out_s[expert] = (dot_nt(grad_gate, gate_ref[0]) + dot_nt(grad_up, up_ref[0])).astype(
            jnp.bfloat16
        )

        @pl.when(expert >= 2)
        def _():
            left(expert - 2, slot)

        rows_in = rows_s[expert]
        for n, (one, other) in enumerate(
            ((rows_in, grad_gate), (rows_in, grad_up), (grad_low, active))
        ):
            product = dot_tn(one, other).astype(jnp.bfloat16)
            for d in range(n_dp):
                weight_s[slot, d % 2, d // 2, :, n * hidden : (n + 1) * hidden] = product[
                    d * step : (d + 1) * step
                ]
        if inside:
            pair_copy(expert, slot).start()

            @pl.when(expert >= 1)
            def _():
                settle(expert - 1, 1 - slot)

        else:
            own_copy(expert, slot).start()
        for n, at in enumerate(LINE_TURNS):

            @pl.when(expert == at)
            def _(n=n):
                line_turn(n)

    @pl.when(turn == 2 * ffn_count - 1)
    def _():
        for block in blocks:
            back_ref[block] = combine(block)
        if inside:
            settle(ffn_count - 1, (ffn_count - 1) % 2)
        for e in range(ffn_count - 2, ffn_count):
            left(e, e % 2)
        for n in range(len(LINE_TURNS), SUM_PIECES + n_t - 3):
            line_turn(n)
        for n in range(SUM_PIECES):
            line.collect(acc, n)
        sum_ref[...] = acc[...]
        line.finish()
        gather.finish((1,))
        if inside:
            for e in range(ffn_count):
                own_copy(e, e % 2).wait()
            for e in range(early):
                for k in range(halving.number(0)):
                    for part in (0, 1):
                        halving.stage_copy(e, part, 0, k).wait()


def experts(n_dp, n_t, moe_rows, grad_half, grad_out, routes_t, residual_t, router_t, gate_w, up_w, down_w):
    _, local, width = moe_rows.shape
    rows = n_t * local
    route_count = router_t.shape[0]
    ffn_count, _, hidden = gate_w.shape
    step = width // n_dp
    half = n_dp // 2
    inside = reduced_inside(step)
    bf, f32 = jnp.bfloat16, jnp.float32
    dma = pltpu.SemaphoreType.DMA

    def whole(shape):
        return pl.BlockSpec(shape, lambda s: (0,) * len(shape), pipeline_mode=pl.Buffered(1))

    any_space = pl.BlockSpec(memory_space=pl.ANY)
    item = (half, step, 3 * hidden)
    weights = (
        [
            jax.ShapeDtypeStruct((ffn_count, *item), bf),
            jax.ShapeDtypeStruct((min(EARLY, ffn_count), half // 2, *item[1:]), bf),
        ]
        if inside
        else [jax.ShapeDtypeStruct((ffn_count, 2, *item), bf)]
    )
    paired = []
    if inside:
        stage = dma((min(EARLY, ffn_count), 2, half // 2))
        paired = [pltpu.VMEM((ffn_count, *item), bf), dma((ffn_count,)), dma((ffn_count,)), stage, stage]
    blocks = (n_t, local, width)
    return pl.pallas_call(
        functools.partial(expert_kernel, (n_dp, n_t, ffn_count, route_count, inside)),
        grid=(2 * ffn_count,),
        out_shape=(
            jax.ShapeDtypeStruct(blocks, bf),
            jax.ShapeDtypeStruct((local, width), f32),
            jax.ShapeDtypeStruct((n_t, ffn_count, local), f32),
            *weights,
        ),
        in_specs=[
            whole(blocks),
            any_space,
            whole((local, width)),
            whole((2, rows)),
            whole((route_count, rows)),
            whole((route_count, width)),
            pl.BlockSpec((1, width, hidden), lambda s: (s % ffn_count, 0, 0)),
            pl.BlockSpec((1, width, hidden), lambda s: (s % ffn_count, 0, 0)),
            pl.BlockSpec((1, hidden, width), lambda s: (s % ffn_count, 0, 0)),
        ],
        out_specs=(
            whole(blocks),
            whole((local, width)),
            whole((n_t, ffn_count, local)),
            *[any_space for _ in weights],
        ),
        scratch_shapes=[
            pltpu.VMEM((EXP_PAD, rows), f32),
            pltpu.VMEM((EXP_PAD, rows), f32),
            pltpu.VMEM((EXP_PAD, width), f32),
            pltpu.VMEM((ffn_count, CAP, rows), bf),
            pltpu.VMEM((rows, ffn_count * CAP), bf),
            pltpu.VMEM((ffn_count, CAP, 1), f32),
            pltpu.VMEM((ffn_count, CAP, width), bf),
            pltpu.VMEM((ffn_count, CAP, hidden), f32),
            pltpu.VMEM((ffn_count, CAP, hidden), f32),
            pltpu.VMEM((ffn_count, CAP, hidden), bf),
            pltpu.VMEM((ffn_count, CAP, width), bf),
            pltpu.VMEM(blocks, bf),
            pltpu.VMEM(blocks, bf),
            pltpu.VMEM((n_t + 1, local, width), bf),
            pltpu.VMEM((local, width), f32),
            pltpu.VMEM((2, 2, *item), bf),
            dma((2, n_t, GRAD_PIECES)),
            dma((n_t, GRAD_PIECES)),
            dma((n_t,)),
            dma((2, n_t, SUM_PIECES)),
            dma((2, n_t, SUM_PIECES)),
            dma((ffn_count,)),
            *paired,
        ],
        compiler_params=pltpu.CompilerParams(
            dimension_semantics=("arbitrary",),
            collective_id=3,
            has_side_effects=True,
            vmem_limit_bytes=62 << 20,
        ),
        name="experts",
    )(moe_rows, grad_half, grad_out, routes_t, residual_t, router_t, gate_w, up_w, down_w)


def side_forward(norm, named, residual, weight_parts, const_value, route_count, ffn_count):
    lane = lax.broadcasted_iota(jnp.int32, named.shape, 1)
    low = norm.astype(jnp.bfloat16)
    both = sum(dot_nt(low, part) for part in weight_parts)
    logits = jnp.where(lane < route_count, both + residual, MASKED)
    exps = jnp.exp(logits - jnp.max(logits, axis=1, keepdims=True))
    probs = exps / jnp.sum(exps, axis=1, keepdims=True)
    chosen = probs * named
    shares, keeps, rests = [], chosen[:, ffn_count + 1 : ffn_count + 2], []
    for c in range(2):
        at = route_count + 2 * c
        share = 1.0 / (1.0 + jnp.exp(both[:, at + 1 : at + 2] - both[:, at : at + 1]))
        weight = chosen[:, ffn_count + 2 + c : ffn_count + 3 + c]
        shares.append(share)
        keeps = keeps + weight * share
        rests.append(weight * (1.0 - share))
    special = keeps * norm + rests[0] * const_value[0:1] + rests[1] * const_value[1:2]
    return probs, chosen, shares, keeps, rests, special


def side_backward(
    norm, grad, named, forward, chosen_back, weight_parts, const_value, route_count, ffn_count
):
    probs, chosen, shares, keeps, rests, _ = forward
    lane = lax.broadcasted_iota(jnp.int32, named.shape, 1)
    self_dot = jnp.sum(grad * norm, axis=1, keepdims=True)
    value_dots = [
        jnp.sum(grad * const_value[c : c + 1], axis=1, keepdims=True) for c in range(2)
    ]
    d_probs = jnp.where(lane < ffn_count, chosen_back, 0.0)
    d_probs = jnp.where(lane == ffn_count + 1, self_dot, d_probs)
    for c in range(2):
        mixed = shares[c] * self_dot + (1.0 - shares[c]) * value_dots[c]
        d_probs = jnp.where(lane == ffn_count + 2 + c, mixed, d_probs)
    d_probs = d_probs * named
    d_both = probs * (d_probs - jnp.sum(probs * d_probs, axis=1, keepdims=True))
    d_both = jnp.where(lane < route_count, d_both, 0.0)
    for c in range(2):
        weight = chosen[:, ffn_count + 2 + c : ffn_count + 3 + c]
        d_share = shares[c] * (1.0 - shares[c]) * weight * (self_dot - value_dots[c])
        d_both = jnp.where(lane == route_count + 2 * c, d_share, d_both)
        d_both = jnp.where(lane == route_count + 2 * c + 1, -d_share, d_both)
    d_parts = three_parts(d_both)
    back = keeps * grad
    for m, n in ((0, 0), (0, 1), (1, 0), (1, 1)):
        back = back + dot(d_parts[m], weight_parts[n])
    low = norm.astype(jnp.bfloat16)
    weight_part = dot_tn(d_parts[0], low) + dot_tn(d_parts[1], low) + dot_tn(d_parts[2], low)
    value_part = [jnp.sum(rests[c] * grad, axis=0, keepdims=True) for c in range(2)]
    return back, weight_part, value_part


def backward_kernel(
    sizes,
    sum_ref,
    back_ref,
    chosen_ref,
    hidden_ref,
    moe_ref,
    grad_ref,
    input_ref,
    routes_ref,
    residual_ref,
    router_ref,
    gates_ref,
    value_ref,
    moe_gain_ref,
    attn_gain_ref,
    q_ref,
    k_ref,
    v_ref,
    o_ref,
    lse_ref,
    rows_ref,
    qkv_ref,
    out_w_ref,
    table_ref,
    *rest,
):
    dp_bits, n_t, ffn_count, route_count, attn_split, inside = sizes
    stage_count = dp_bits - 1 if inside else 0
    expert_refs = rest[: 2 if inside else 0]
    rest = rest[2 if inside else 0 :]
    (
        output_ref,
        input_grad_ref,
        expert_out,
        attn_out,
        small_out,
        gain_out,
        chosen_in,
        pair_buf,
        line_back,
        staged,
        both_s,
        turned_s,
        grad_rows,
        attn_part,
        acc,
        hidden_grad,
        double_grad,
        delta,
        dq,
        dk,
        dv,
        packed,
    ) = rest[:22]
    rest = rest[22:]
    if inside:
        attn_pairs, kept = rest[:2]
        stages = rest[2 : 2 + stage_count]
        rest = rest[2 + stage_count :]
        a_kept, a_first = rest[:2]
        a_stages = rest[2 : 2 + stage_count]
        rest = rest[2 + stage_count :]
    else:
        attn_pairs = attn_out
    smalls, small_dp, small_tensor, gains, gain_dp, gain_tensor, side_back = rest[:7]
    rest = list(rest[7:])

    def sems(count):
        taken = rest[:count]
        del rest[:count]
        return taken

    (chosen_send, chosen_recv, gather_send, gather_recv) = sems(4)
    line_sems = [sems(2) for _ in range(2)]
    if inside:
        e_sems = [None] + sems(2) + [sems(stage_count), sems(stage_count)]
        a_sems = sems(3) + [sems(stage_count), sems(stage_count)]
    small_sems = [sems(2), sems(2)]
    gain_sems = [sems(2), sems(2)]
    (staged_sem,) = sems(1)

    dp = lax.axis_index("dp")
    place = lax.axis_index("tensor")
    local = hidden_ref.shape[0]
    width = hidden_ref.shape[1]
    hidden_units = expert_out.shape[-1]
    heads = q_ref.shape[0]
    greet((("dp", dp, 1 << dp_bits), ("tensor", place, n_t)))

    back_line = LineScatter(back_ref, line_back, *line_sems[0], place, PIECES)
    attn_line = LineScatter(attn_part, line_back, *line_sems[1], place, PIECES)
    gather = LineGather(grad_rows, gather_send, gather_recv, place, PIECES)
    half = hidden_units // 2
    attn_width = attn_pairs.shape[-1]
    expert = attn = Nothing()
    if inside:
        splits = ((0, half), (half, half))
        expert = LateHalving(expert_refs, kept, None, stages, e_sems, dp, dp_bits, splits)
        splits = ((0, attn_split), (attn_split, attn_width - attn_split))
        attn = Halving(attn_pairs, a_kept, a_first, a_stages, a_sems, dp, dp_bits, splits)
    everyone = (("dp", dp, 1 << dp_bits), ("tensor", place, n_t))
    small = Exchange(smalls, (small_dp, small_tensor), *small_sems, everyone)
    gain = Exchange(gains, (gain_dp, gain_tensor), *gain_sems, everyone)

    def chosen_copy(step):
        there = (place + step) % n_t
        return pltpu.make_async_remote_copy(
            src_ref=chosen_ref.at[there],
            dst_ref=chosen_in.at[step - 1],
            send_sem=chosen_send.at[step - 1],
            recv_sem=chosen_recv.at[step - 1],
            device_id={"tensor": there},
            device_id_type=MESH,
        )

    ends_first = (n_t - 1, 0, *range(n_t - 2, 0, -1))
    for step in range(1, n_t):
        chosen_copy(step).start()
    back_line.originate(ends_first, (0,))

    def over_experts(action):
        def body(e, _):
            action(e)
            return 0

        def run(first, last):
            lax.fori_loop(first, last, body, 0)

        return run

    early = min(EARLY, ffn_count)
    expert.begin(early, ffn_count)

    norm = moe_ref[place].astype(jnp.float32)
    lane = lax.broadcasted_iota(jnp.int32, (local, 128), 1)
    mine = pl.ds(pl.multiple_of(place * local, local), local)
    turned_s[...] = jnp.zeros_like(turned_s)
    turned_s[0:route_count, :] = residual_ref[:, mine]
    turned_s[16:18, :] = routes_ref[:, mine].astype(jnp.float32)
    turned = turned_s[...].T
    residual = turned
    kind = lane.astype(jnp.float32)
    named = jnp.where((turned[:, 16:17] == kind) | (turned[:, 17:18] == kind), 1.0, 0.0)
    both_s[...] = jnp.zeros_like(both_s)
    both_s[0:route_count, :] = router_ref[...]
    for c in range(2):
        both_s[route_count + 2 * c : route_count + 2 * c + 2, :] = gates_ref[c]
    weight_parts = three_parts(both_s[...])
    const_value = value_ref[...]
    grad = grad_ref[...].astype(jnp.float32)
    forward = side_forward(
        norm, named, residual, weight_parts, const_value, route_count, ffn_count
    )
    pair_buf[...] = hidden_ref[...] + forward[-1]
    chosen_total = chosen_ref[place]
    for step in range(1, n_t):
        chosen_copy(step).wait_recv()
        chosen_total = chosen_total + chosen_in[step - 1]
    chosen_back = jnp.concatenate(
        [chosen_total, jnp.zeros((128 - ffn_count, local), jnp.float32)], axis=0
    ).T
    back, weight_part, value_part = side_backward(
        norm, grad, named, forward, chosen_back, weight_parts, const_value, route_count, ffn_count
    )
    side_back[...] = back
    smalls[0, 1:2, :] = value_part[0]
    smalls[0, 2:3, :] = value_part[1]
    smalls[0, 3:8, :] = jnp.zeros((5, width), jnp.float32)
    smalls[0, 8:24, :] = weight_part[0:16]

    opening = -(-ffn_count // PIECES)
    moe_gain_total = jnp.zeros((1, width), jnp.float32)
    lag = n_t - 2
    for turn in range(PIECES + lag + n_t - 1):
        back_line.forward(turn, ends_first)
        if turn + 1 < PIECES:
            back_line.drain(ends_first, turn)
            back_line.originate(ends_first, (turn + 1,))
        for e in range(turn * opening, min((turn + 1) * opening, ffn_count)):
            expert.open(e, early)
        if 0 <= turn - lag < PIECES:
            n = turn - lag
            at = slice(n * (local // PIECES), (n + 1) * (local // PIECES))
            back_line.collect(acc, n)
            norm_grad = acc[at, :] + side_back[at, :]
            hidden = hidden_ref[at, :]
            scale = lax.rsqrt(jnp.mean(hidden * hidden, axis=1, keepdims=True) + EPSILON)
            u = norm_grad * moe_gain_ref[...].reshape(1, width)
            moe_gain_total = moe_gain_total + jnp.sum(
                norm_grad * hidden * scale, axis=0, keepdims=True
            )
            hidden_grad[at, :] = (
                grad_ref[at, :].astype(jnp.float32)
                + scale * u
                - hidden
                * (scale * scale * scale)
                * jnp.mean(u * hidden, axis=1, keepdims=True)
            )
            grad_rows[place, at, :] = hidden_grad[at, :].astype(jnp.bfloat16)
            if n == PIECES - 1:
                back_line.finish()
            gather.start(n)
        for step in range(1, n_t):
            if 0 <= turn - lag - step < PIECES:
                gather.step(step, turn - lag - step)
    smalls[0, 0:1, :] = moe_gain_total
    small.start(0)
    output_ref[...] = (pair_buf[...] + sum_ref[...]).astype(output_ref.dtype)
    advance = over_experts(lambda e: expert.advance(e, 0))

    rows = local

    def row_block(n):
        return pl.ds(pl.multiple_of(n * rows, rows), rows)

    count = n_t
    head_lane = lax.broadcasted_iota(jnp.int32, (rows, 128), 1)
    low_half = head_lane < 64
    for block in range(count):
        at = pl.ds(block * rows, rows)
        product = dot_nt(grad_rows[block], out_w_ref[...])
        for h in range(heads):
            piece = product[:, h * 128 : (h + 1) * 128].astype(jnp.bfloat16)
            double_grad[h, at, :] = piece
            both = piece.astype(jnp.float32) * o_ref[h, at, :].astype(jnp.float32)
            delta[h : h + 1, at] = 0.5 * jnp.sum(both.T, axis=0, keepdims=True)
    out_pack = []
    for h in range(0, heads, 2):
        o_a = o_ref[h]
        o_b = o_ref[h + 1] if h + 1 < heads else jnp.zeros_like(o_a)
        lanes = lax.broadcasted_iota(jnp.int32, o_a.shape, 1)
        out_pack.append(jnp.where(lanes < 64, o_a, o_b))
    n_half = attn_pairs.shape[2]
    step_rows = attn_pairs.shape[3]
    qkv_width = packed.shape[1]

    def spread(product, start, stop):
        low = product.astype(jnp.bfloat16)
        for d in range(2 * n_half):
            attn_pairs[0, d % 2, d // 2, :, start:stop] = low[d * step_rows : (d + 1) * step_rows]

    for n, pack in enumerate(out_pack):
        total = jnp.zeros((width, 128), jnp.float32)
        for block in range(count):
            total = total + dot_tn(grad_rows[block], pack[block * rows : (block + 1) * rows])
        spread(total, qkv_width + n * 128, qkv_width + (n + 1) * 128)

    dq[...] = jnp.zeros_like(dq)
    factor = 64 ** (-0.5)
    gain_total = jnp.zeros((1, width), jnp.float32)
    for turn, key_block in enumerate(range(count)):
        keys = pl.ds(key_block * rows, rows)
        dk[...] = jnp.zeros_like(dk)
        dv[...] = jnp.zeros_like(dv)

        def query_step(query_block, _, keys=keys):
            at = row_block(query_block)
            for h in range(heads):
                q, g = q_ref[h, at, :], double_grad[h, at, :]
                k, v = k_ref[h, keys, :], v_ref[h, keys, :]
                scores = dot_nt(k, q) * (0.5 * factor)
                probs = jnp.exp(scores - lse_ref[h : h + 1, at])
                d_probs = dot_nt(v, g) * 0.5
                d_scores = (probs * (d_probs - delta[h : h + 1, at])).astype(jnp.bfloat16)
                dk[h] += dot(d_scores, q)
                dv[h] += dot(probs.astype(jnp.bfloat16), g)
                dq[h, at, :] += dot_tn(d_scores, k)
            return 0

        lax.fori_loop(key_block, count, query_step, 0)
        table = table_ref[keys, :]
        pieces = []
        for source in (dq.at[:, keys, :], dk):
            for h in range(heads):
                turned = source[h] * (table * factor)
                pieces.append(turned + pltpu.roll(turned, 64, 1))
        for h in range(heads):
            pieces.append(dv[h])
        if len(pieces) % 2:
            pieces.append(jnp.zeros((rows, 128), jnp.float32))
        for n in range(0, len(pieces), 2):
            packed[keys, n * 64 : n * 64 + 128] = jnp.where(
                low_half, pieces[n], pieces[n + 1]
            ).astype(jnp.bfloat16)
        back_rows = dot(packed[keys, :], qkv_ref[...])
        gain_total = gain_total + jnp.sum(
            back_rows * rows_ref[key_block].astype(jnp.float32), axis=0, keepdims=True
        )
        attn_part[key_block] = back_rows.astype(jnp.bfloat16)
        attn_line.originate((key_block,))
        if turn > 0:
            attn_line.forward_all(key_block - 1)
        if turn == 0:
            advance(early, ffn_count)
        if turn == 1:
            small.take(0)
            small.start(1)

    gains[0] = gain_total / attn_gain_ref[...].reshape(1, width)
    gain.start(0)
    for n in range(qkv_width // 128):
        total = jnp.zeros((width, 128), jnp.float32)
        for block in range(count):
            total = total + dot_tn(
                rows_ref[block], packed[pl.ds(block * rows, rows), n * 128 : (n + 1) * 128]
            )
        spread(total, n * 128, (n + 1) * 128)
    attn.start(0)
    attn_line.forward_all(count - 1)
    gain.take(0)
    gain.start(1)
    attn.open(0)
    for stage in range(1, stage_count - 1):
        over_experts(lambda e, stage=stage: expert.advance(e, stage))(0, ffn_count)
    small.take(1)
    small_out[...] = smalls[2]
    for stage in range(stage_count - 1):
        attn.advance(0, stage)
    gain.take(1)
    gain_out[...] = jnp.broadcast_to(gains[2], gain_out.shape)
    for n in range(PIECES):
        attn_line.collect(acc, n)
    wide = input_ref[...].astype(jnp.float32)
    scale = lax.rsqrt(jnp.mean(wide * wide, axis=1, keepdims=True) + EPSILON)
    w = acc[...] * attn_gain_ref[...].reshape(1, width)
    input_grad_ref[...] = (
        hidden_grad[...]
        + scale * w
        - wide * (scale * scale * scale) * jnp.mean(w * wide, axis=1, keepdims=True)
    ).astype(input_grad_ref.dtype)
    def stored(e):
        return pltpu.make_async_copy(staged.at[e % 2], expert_out.at[e], staged_sem.at[e])

    for e in range(ffn_count if inside else 0):
        if e > 1:
            stored(e - 2).wait()
        expert.close(e, staged.at[e % 2])
        stored(e).start()
    attn.close(0, attn_out)

    attn_line.finish()
    for step in range(1, n_t):
        chosen_copy(step).wait_send()
    gather.finish()

    for e in range(ffn_count):
        expert.finish(e, early)
    attn.finish(0)
    for e in range(ffn_count - 2, ffn_count if inside else 0):
        stored(e).wait()


def backward(dp_count, n_t, ffn_sum, ffn_back, chosen, weight_pairs, hidden, moe_rows, grad_out,
             layer_input, routes, residual, router, gates, const_value, moe_gain, attn_gain,
             q2, k2, v2, o2, lse, attn_rows, qkv_weight, out_double, table):
    local, width = hidden.shape
    group = local * n_t
    ffn_count = weight_pairs[0].shape[0]
    units = weight_pairs[0].shape[-1]
    step = width // dp_count
    half = dp_count // 2
    dp_bits = log2_of(dp_count)
    inside = reduced_inside(step)
    stage_count = dp_bits - 1 if inside else 0
    heads = q2.shape[0]
    qkv_width = qkv_weight.shape[0]
    attn_width = qkv_width + -(-heads // 2) * 128
    attn_split = attn_width // 2 // 128 * 128
    bf, f32 = jnp.bfloat16, jnp.float32
    dma = pltpu.SemaphoreType.DMA

    def numbers(stage):
        return half >> (stage + 1)

    def line(rows_shape):
        return pltpu.VMEM((n_t + 1, *rows_shape[1:]), bf)

    block_shape = (n_t, local, width)
    reduction = []
    if inside:
        reduction = [
            pltpu.VMEM((1, 2, half, step, attn_width), bf),
            pltpu.VMEM((ffn_count, half, step, units), bf),
            *[pltpu.VMEM((ffn_count, numbers(s), step, units), bf) for s in range(stage_count)],
            pltpu.VMEM((1, half, step, attn_width), bf),
            pltpu.VMEM((1, half, step, attn_width), bf),
            *[pltpu.VMEM((1, numbers(s), step, attn_width), bf) for s in range(stage_count)],
        ]
    scratch = [
        pltpu.VMEM((n_t - 1, ffn_count, local), f32),
        pltpu.VMEM((local, width), f32),
        line(block_shape),
        pltpu.VMEM((2, step, units), f32),
        pltpu.VMEM((128, width), f32),
        pltpu.VMEM((128, local), f32),
        pltpu.VMEM(block_shape, bf),
        pltpu.VMEM(block_shape, bf),
        pltpu.VMEM((local, width), f32),
        pltpu.VMEM((local, width), f32),
        pltpu.VMEM((heads, group, 128), bf),
        pltpu.VMEM((8, group), f32),
        pltpu.VMEM((heads, group, 128), f32),
        pltpu.VMEM((heads, local, 128), f32),
        pltpu.VMEM((heads, local, 128), f32),
        pltpu.VMEM((group, qkv_width), bf),
        *reduction,
        pltpu.VMEM((3, 24, width), f32),
        pltpu.VMEM((dp_count - 1, 24, width), f32),
        pltpu.VMEM((n_t - 1, 24, width), f32),
        pltpu.VMEM((3, 1, width), f32),
        pltpu.VMEM((dp_count - 1, 1, width), f32),
        pltpu.VMEM((n_t - 1, 1, width), f32),
        pltpu.VMEM((local, width), f32),
        dma((n_t - 1,)),
        dma((n_t - 1,)),
        dma((2, n_t, PIECES)),
        dma((n_t, PIECES)),
        dma((2, n_t, PIECES)),
        dma((2, n_t, PIECES)),
        dma((2, n_t, PIECES)),
        dma((2, n_t, PIECES)),
        *[
            s
            for n in ((ffn_count, 1) if inside else ())
            for s in (
                *[dma((n,)) for _ in range(2 if n == ffn_count else 3)],
                *[dma((n, 2, numbers(s))) for s in range(stage_count)],
                *[dma((n, 2, numbers(s))) for s in range(stage_count)],
            )
        ],
        *[dma((n - 1,)) for _ in range(4) for n in (dp_count, n_t)],
        dma((ffn_count,)),
    ]
    vmem = pl.BlockSpec(memory_space=pltpu.VMEM)
    operands = (ffn_sum, ffn_back, chosen, hidden, moe_rows, grad_out, layer_input, routes, residual,
                router, gates, const_value, moe_gain, attn_gain, q2, k2, v2, o2, lse, attn_rows,
                qkv_weight, out_double, table)
    specs = [vmem] * len(operands)
    if inside:
        operands = (*operands, *weight_pairs)
        specs += [pl.BlockSpec(memory_space=pl.ANY)] * 2
    return pl.pallas_call(
        functools.partial(
            backward_kernel, (dp_bits, n_t, ffn_count, residual.shape[0], attn_split, inside)
        ),
        out_shape=(
            jax.ShapeDtypeStruct((local, width), bf),
            jax.ShapeDtypeStruct((local, width), bf),
            jax.ShapeDtypeStruct((ffn_count, step, units) if inside else (8, 128), f32),
            jax.ShapeDtypeStruct((step, attn_width), f32)
            if inside
            else jax.ShapeDtypeStruct((1, 2, half, step, attn_width), bf),
            jax.ShapeDtypeStruct((24, width), f32),
            jax.ShapeDtypeStruct((8, width), f32),
        ),
        in_specs=specs,
        out_specs=(vmem, vmem, pl.BlockSpec(memory_space=pl.ANY), vmem, vmem, vmem),
        scratch_shapes=scratch,
        compiler_params=pltpu.CompilerParams(
            collective_id=1, has_side_effects=True, vmem_limit_bytes=62 << 20
        ),
        name="backward",
    )(*operands)


def rope_lanes(length, head_width):
    position = np.arange(length, dtype=np.float64)[:, None]
    inverse = np.exp(np.arange(head_width // 2) * (-2.0 * math.log(10000.0) / head_width))
    angle = position * inverse[None, :]
    c, s = np.cos(angle), np.sin(angle)
    cosine = np.concatenate([c, c, c, c], axis=1).astype(np.float32)
    sine = np.concatenate([-s, s, s, -s], axis=1).astype(np.float32)
    return cosine, sine


def tidy_kernel(
    wide, route_count, gate_ref, up_ref, down_ref, attn_ref, small_ref, gain_ref, output_ref, grad_ref, *outs
):
    (output, grad, attn_gain, q_out, k_out, v_out, out_out, moe_gain, router, gates, value) = outs[:11]
    for source, target in zip((gate_ref, up_ref, down_ref), outs[11:]):
        target[...] = source[...]

    @pl.when(pl.program_id(0) == 0)
    def _():
        output[...] = output_ref[...]
        grad[...] = grad_ref[...]
        attn_gain[...] = gain_ref[0, :]
        moe_gain[...] = small_ref[0, :]
        value[...] = small_ref[1:3, :]
        router[...] = small_ref[8 : 8 + route_count, :]
        for c in range(2):
            at = 8 + route_count + 2 * c
            gates[c] = small_ref[at : at + 2, :]
        for n, ref in enumerate((q_out, k_out, v_out)):
            ref[...] = attn_ref[:, n * wide : (n + 1) * wide]
        at = -(-3 * wide // 128) * 128
        out_out[...] = attn_ref[:, at : at + -(-wide // 128) * 128].T[0:wide, :]


def tidy(wide, route_count, expert_sum, attn_sum, small, gain, output, input_grad):
    count, step, units = expert_sum.shape
    units = units // 3
    width = small.shape[1]
    f32 = jnp.float32
    group = 2 if count % 2 == 0 else 1

    def whole(shape):
        return pl.BlockSpec(shape, lambda e: (0,) * len(shape), pipeline_mode=pl.Buffered(1))

    small_shapes = (
        (width,),
        (step, wide),
        (step, wide),
        (step, wide),
        (wide, step),
        (width,),
        (route_count, width),
        (2, 2, width),
        (2, width),
    )
    shapes = [output, input_grad]
    shapes += [jax.ShapeDtypeStruct(shape, f32) for shape in small_shapes]
    shapes += [jax.ShapeDtypeStruct((count, step, units), f32)] * 3
    piece = [
        pl.BlockSpec((group, step, units), lambda e, n=n: (e, 0, n)) for n in (0, 1, 2, 0, 0, 0)
    ]
    rest = (attn_sum, small, gain, output, input_grad)
    return pl.pallas_call(
        functools.partial(tidy_kernel, wide, route_count),
        grid=(count // group,),
        out_shape=tuple(jax.ShapeDtypeStruct(s.shape, s.dtype) for s in shapes),
        in_specs=[*piece[:3], *[whole(a.shape) for a in rest]],
        out_specs=(*[whole(s.shape) for s in shapes[:11]], *piece[3:]),
        compiler_params=pltpu.CompilerParams(
            dimension_semantics=("arbitrary",), vmem_limit_bytes=62 << 20
        ),
        name="tidy",
    )(expert_sum, expert_sum, expert_sum, *rest)


def on_device(
    layer_input,
    attn_gain,
    query_weight,
    key_weight,
    value_weight,
    out_weight,
    moe_gain,
    router_weight,
    gate_residual,
    const_gate,
    const_value,
    gate_weight,
    up_weight,
    down_weight,
    routes,
    grad_out,
):
    local_rows, model_width = layer_input.shape
    tensor_size = lax.axis_size("tensor")
    head_count = query_weight.shape[1] // HD
    ffn_count = gate_weight.shape[0]
    route_count = router_weight.shape[1]
    cosine, sine = rope_lanes(LENGTH, HD)
    q2, k2, v2, o2, lse, attn_rows, moe_rows, grad_half, hidden, qkv_weight, out_double = forward(
        tensor_size,
        layer_input,
        attn_gain,
        moe_gain,
        query_weight.T,
        key_weight.T,
        value_weight.T,
        out_weight,
        grad_out,
        jnp.asarray(cosine),
        jnp.asarray(sine),
    )
    n_dp = lax.axis_size("dp")
    ffn_back, ffn_sum, chosen_t, *weight_pairs = experts(
        n_dp,
        tensor_size,
        moe_rows,
        grad_half,
        grad_out,
        routes.T,
        gate_residual.T,
        router_weight.T,
        gate_weight,
        up_weight,
        down_weight,
    )
    output, input_grad, expert_sum, attn_sum_rows, small, gain = backward(
        n_dp,
        tensor_size,
        ffn_sum,
        ffn_back,
        chosen_t,
        weight_pairs,
        hidden,
        moe_rows,
        grad_out,
        layer_input,
        routes.T,
        gate_residual.T,
        router_weight.T,
        jnp.transpose(const_gate, (0, 2, 1)),
        const_value,
        moe_gain,
        attn_gain,
        q2,
        k2,
        v2,
        o2,
        lse,
        attn_rows,
        qkv_weight,
        out_double,
        jnp.asarray(np.concatenate([cosine[:, :HD], sine[:, HD:]], axis=1)),
    )
    if not reduced_inside(model_width // n_dp):

        def scattered(pairs):
            pairs = jnp.transpose(pairs, (2, 1, 3, 0, 4)).reshape(model_width, -1)
            return lax.psum_scatter(pairs, "dp", scatter_dimension=0, tiled=True).astype(
                jnp.float32
            )

        attn_sum_rows = scattered(attn_sum_rows)
        expert_sum = scattered(weight_pairs[0]).reshape(
            model_width // n_dp, ffn_count, weight_pairs[0].shape[-1]
        )
        expert_sum = jnp.transpose(expert_sum, (1, 0, 2))
    outs = list(
        tidy(
            head_count * HD, route_count, expert_sum, attn_sum_rows, small, gain, output, input_grad
        )
    )
    outs[8] = outs[8].T
    outs[9] = jnp.transpose(outs[9], (0, 2, 1))
    outs[13] = jnp.transpose(outs[13], (0, 2, 1))
    return tuple(outs)


def solution(mesh):
    in_specs = (
        P(("dp", "tensor"), None),
        P(),
        P(None, "tensor"),
        P(None, "tensor"),
        P(None, "tensor"),
        P("tensor", None),
        P(),
        P(),
        P("dp", None),
        P(),
        P(),
        P(None, None, "tensor"),
        P(None, None, "tensor"),
        P(None, "tensor", None),
        P("dp", None),
        P(("dp", "tensor"), None),
    )
    out_specs = (
        P(("dp", "tensor"), None),
        P(("dp", "tensor"), None),
        P(),
        P("dp", "tensor"),
        P("dp", "tensor"),
        P("dp", "tensor"),
        P("tensor", "dp"),
        P(),
        P(),
        P(),
        P(),
        P(None, "dp", "tensor"),
        P(None, "dp", "tensor"),
        P(None, "tensor", "dp"),
    )
    return jax.shard_map(
        on_device, mesh=mesh, in_specs=in_specs, out_specs=out_specs, check_vma=False
    )
```

```python
import functools
import math

import jax
import jax.numpy as jnp
import numpy as np
from jax import lax
from jax.experimental import pallas as pl
from jax.experimental.pallas import tpu as pltpu
from jax.sharding import PartitionSpec as P

HD = 64
LENGTH = 1024
BLOCK = 256
CAP = 256


EPSILON = 1e-06
MASKED = -1e30


EXP_PAD = 16


def dot(a, b):
    return jnp.dot(a, b, preferred_element_type=jnp.float32)


def dot_nt(a, b):
    return lax.dot_general(a, b, (((1,), (1,)), ((), ())), preferred_element_type=jnp.float32)


def dot_tn(a, b):
    return lax.dot_general(a, b, (((0,), (0,)), ((), ())), preferred_element_type=jnp.float32)


def three_parts(values):
    first = values.astype(jnp.bfloat16)
    rest = values - first.astype(jnp.float32)
    second = rest.astype(jnp.bfloat16)
    third = (rest - second.astype(jnp.float32)).astype(jnp.bfloat16)
    return (first, second, third)


MESH = pl.DeviceIdType.MESH
PIECES = 8
GRAD_PIECES = 2
SUM_PIECES = 4
LINE_TURNS = (1, 3, 5, 7)
EARLY = 4


def bit_of(index, position):
    return index // (1 << position) % 2


def flipped(index, position):
    return index + (1 << position) * (1 - 2 * bit_of(index, position))


def log2_of(count):
    return count.bit_length() - 1


def greet(axes):
    barrier = pltpu.get_barrier_semaphore()
    for axis, index, count in axes:

        def body(step, _, axis=axis, index=index, count=count):
            pl.semaphore_signal(
                barrier, inc=1, device_id={axis: (index + step) % count}, device_id_type=MESH
            )
            return 0

        lax.fori_loop(1, count, body, 0)
    pl.semaphore_wait(barrier, sum(count - 1 for _, _, count in axes))


class LineGather:
    def __init__(self, blocks, send, recv, place, pieces=1):
        self.blocks, self.send, self.recv, self.place = blocks, send, recv, place
        self.count, self.pieces = blocks.shape[0], pieces
        self.rows = blocks.shape[1] // pieces

    def copy(self, block, n, way):
        piece = self.blocks.at[block, pl.ds(n * self.rows, self.rows)]
        return pltpu.make_async_remote_copy(
            src_ref=piece,
            dst_ref=piece,
            send_sem=self.send.at[way, block, n],
            recv_sem=self.recv.at[block, n],
            device_id={"tensor": self.place + 1 - 2 * way},
            device_id_type=MESH,
        )

    def start(self, n=0):
        @pl.when(self.place < self.count - 1)
        def _():
            self.copy(self.place, n, 0).start()

        @pl.when(self.place > 0)
        def _():
            self.copy(self.place, n, 1).start()

    def step(self, distance, n=0):
        below, above = self.place - distance, self.place + distance

        @pl.when(below >= 0)
        def _():
            self.copy(below, n, 0).wait_recv()

            @pl.when(self.place < self.count - 1)
            def _():
                self.copy(below, n, 0).start()

        @pl.when(above < self.count)
        def _():
            self.copy(above, n, 1).wait_recv()

            @pl.when(self.place > 0)
            def _():
                self.copy(above, n, 1).start()

    def finish(self, pieces=None):
        pieces = range(self.pieces) if pieces is None else pieces
        for distance in range(self.count):
            below, above = self.place - distance, self.place + distance

            @pl.when((below >= 0) & (self.place < self.count - 1))
            def _(below=below):
                for n in pieces:
                    self.copy(below, n, 0).wait_send()

            @pl.when((above < self.count) & (self.place > 0))
            def _(above=above):
                for n in pieces:
                    self.copy(above, n, 1).wait_send()


class LineScatter:
    def __init__(self, parts, arrived, send, recv, place, pieces):
        self.parts, self.arrived, self.send, self.recv = parts, arrived, send, recv
        self.place, self.count, self.pieces = place, parts.shape[0], pieces
        self.rows = parts.shape[1] // pieces
        self.drained = set()

    def piece(self, ref, block, n):
        return ref.at[block, pl.ds(n * self.rows, self.rows)]

    def copy(self, block, n, way, own=False):
        there = self.piece(self.arrived, block + 1 - way, n)
        return pltpu.make_async_remote_copy(
            src_ref=self.piece(self.parts, block, n) if own else there,
            dst_ref=there,
            send_sem=self.send.at[way, block, n],
            recv_sem=self.recv.at[way, block, n],
            device_id={"tensor": self.place + 1 - 2 * way},
            device_id_type=MESH,
        )

    def originate(self, blocks, pieces=None):
        for way, first in ((0, 0), (1, self.count - 1)):
            sent = [block for block in blocks if block != first]
            if sent:

                @pl.when(self.place == first)
                def _(way=way, sent=sent):
                    for n in pieces or range(self.pieces):
                        for block in sent:
                            self.copy(block, n, way, own=True).start()

    def drain(self, blocks, n):
        for way, first in ((0, 0), (1, self.count - 1)):
            sent = [block for block in blocks if block != first]
            self.drained.update((first, block, n) for block in sent)
            if sent:

                @pl.when(self.place == first)
                def _(way=way, sent=sent):
                    for block in sent:
                        self.copy(block, n, way).wait_send()

    def pass_piece(self, block, n, way):
        self.copy(block, n, way).wait_recv()
        there = self.piece(self.arrived, block + 1 - way, n)
        mine = self.piece(self.parts, block, n)
        there[...] = (there[...].astype(jnp.float32) + mine[...].astype(jnp.float32)).astype(
            there.dtype
        )
        self.copy(block, n, way).start()

    def hops(self, place, way):
        return place if way == 0 else self.count - 1 - place

    def forward(self, turn, blocks):
        for place in range(1, self.count - 1):
            passed = []
            for block in blocks:
                way = 0 if place < block else 1
                n = turn - self.hops(place, way) + 1
                if place != block and 0 <= n < self.pieces:
                    passed.append((self.hops(place, way), block, n, way))
            if passed:

                @pl.when(self.place == place)
                def _(passed=passed):
                    for _, block, n, way in sorted(passed, key=lambda item: -item[0]):
                        self.pass_piece(block, n, way)

    def forward_all(self, block):
        for turn in range(self.pieces + self.count - 3):
            self.forward(turn, (block,))

    def collect(self, total, n):
        place = self.place
        rows = slice(n * self.rows, (n + 1) * self.rows)
        total[rows, :] = self.parts[place, rows, :].astype(jnp.float32)
        for way in (0, 1):

            @pl.when(place > 0 if way == 0 else place < self.count - 1)
            def _(way=way):
                self.copy(place, n, way).wait_recv()
                total[rows, :] += self.arrived[place + 1 - way, rows, :].astype(jnp.float32)

    def finish(self):
        for place in range(self.count):
            left = [
                (block, n)
                for block in range(self.count)
                for n in range(self.pieces)
                if block != place and (place, block, n) not in self.drained
            ]
            if left:

                @pl.when(self.place == place)
                def _(place=place, left=left):
                    for block, n in left:
                        self.copy(block, n, 0 if place < block else 1).wait_send()


class Halving:
    def __init__(self, source, kept, first, stages, sems, dp, dp_bits, splits):
        self.source, self.kept, self.first, self.stages = source, kept, first, stages
        self.first_send, self.first_recv, self.local, self.send, self.recv = sems
        self.dp, self.bits, self.splits = dp, dp_bits, splits
        self.core = bit_of(dp, 0)
        upper = list(range(dp_bits - 1))
        self.orders = (upper, upper[1:] + upper[:1])

    def first_copy(self, e):
        return pltpu.make_async_remote_copy(
            src_ref=self.source.at[e, 1 - self.core],
            dst_ref=self.first.at[e],
            send_sem=self.first_send.at[e],
            recv_sem=self.first_recv.at[e],
            device_id={"dp": flipped(self.dp, 0)},
            device_id_type=MESH,
        )

    def local_copy(self, e):
        return pltpu.make_async_copy(
            self.source.at[e, self.core], self.kept.at[e], self.local.at[e]
        )

    def blocks(self, part, stage, k, mine):
        order = self.orders[part]
        index = 0
        for done in order[:stage]:
            index = index + (1 << done) * bit_of(self.dp, done + 1)
        here = bit_of(self.dp, order[stage] + 1)
        index = index + (1 << order[stage]) * (here if mine else 1 - here)
        for n, free in enumerate(order[stage + 1 :]):
            index = index + (1 << free) * (k // (1 << n) % 2)
        return index

    def width(self, part):
        return pl.ds(*self.splits[part])

    def stage_copy(self, e, part, stage, k):
        start, size = self.splits[part]
        return pltpu.make_async_remote_copy(
            src_ref=self.kept.at[e, self.blocks(part, stage, k, False), :, pl.ds(start, size)],
            dst_ref=self.stages[stage].at[e, k, :, pl.ds(start, size)],
            send_sem=self.send[stage].at[e, part, k],
            recv_sem=self.recv[stage].at[e, part, k],
            device_id={"dp": flipped(self.dp, self.orders[part][stage] + 1)},
            device_id_type=MESH,
        )

    def number(self, stage):
        return 1 << (self.bits - 2 - stage)

    def start(self, e):
        self.first_copy(e).start()
        self.local_copy(e).start()

    def send_stage(self, e, stage):
        for k in range(self.number(stage)):
            for part in (0, 1):
                self.stage_copy(e, part, stage, k).start()

    def add_rows(self, target, addend):
        rows = target.shape[0]
        step = 32 if rows % 32 == 0 else rows

        def body(n, _):
            at = pl.ds(pl.multiple_of(n * step, step), step)
            target[at, :] = (
                target[at, :].astype(jnp.float32) + addend[at, :].astype(jnp.float32)
            ).astype(target.dtype)
            return 0

        lax.fori_loop(0, rows // step, body, 0)

    def open(self, e):
        self.first_copy(e).wait_recv()
        self.local_copy(e).wait()
        for block in range(self.kept.shape[1]):
            self.add_rows(self.kept.at[e, block], self.first.at[e, block])
        self.send_stage(e, 0)

    def advance(self, e, stage, arrived=False):
        for k in range(self.number(stage)):
            for part in (0, 1):
                if not arrived:
                    self.stage_copy(e, part, stage, k).wait_recv()
                block = self.blocks(part, stage, k, True)
                self.add_rows(
                    self.kept.at[e, block, :, self.width(part)],
                    self.stages[stage].at[e, k, :, self.width(part)],
                )
        self.send_stage(e, stage + 1)

    def close(self, e, out):
        stage = self.bits - 2
        for part in (0, 1):
            self.stage_copy(e, part, stage, 0).wait_recv()
            block = self.blocks(part, stage, 0, True)
            columns = self.width(part)
            out[:, columns] = self.kept[e, block, :, columns].astype(jnp.float32) + self.stages[
                stage
            ][e, 0, :, columns].astype(jnp.float32)

    def finish(self, e):
        self.first_copy(e).wait_send()
        for stage in range(self.bits - 1):
            for k in range(self.number(stage)):
                for part in (0, 1):
                    self.stage_copy(e, part, stage, k).wait_send()


class LateHalving(Halving):
    def item_copy(self, e):
        return pltpu.make_async_copy(self.source[0].at[e], self.kept.at[e], self.local.at[e])

    def stage_item(self, e):
        return pltpu.make_async_copy(
            self.source[1].at[e], self.stages[0].at[e], self.first_recv.at[e]
        )

    def begin(self, early, count):
        for e in range(count):
            self.item_copy(e).start()
            if e < early:
                self.stage_item(e).start()

    def open(self, e, early):
        self.item_copy(e).wait()
        if e < early:
            self.stage_item(e).wait()
            self.advance(e, 0, arrived=True)
        else:
            self.send_stage(e, 0)

    def finish(self, e, early):
        for stage in range(self.bits - 1):
            if stage > 0 or e >= early:
                for k in range(self.number(stage)):
                    for part in (0, 1):
                        self.stage_copy(e, part, stage, k).wait_send()


class Exchange:
    def __init__(self, totals, arrived, sends, recvs, axes):
        self.totals, self.arrived, self.sends, self.recvs, self.axes = (
            totals,
            arrived,
            sends,
            recvs,
            axes,
        )

    def copy(self, turn, step):
        axis, index, count = self.axes[turn]
        return pltpu.make_async_remote_copy(
            src_ref=self.totals.at[turn],
            dst_ref=self.arrived[turn].at[step],
            send_sem=self.sends[turn].at[step],
            recv_sem=self.recvs[turn].at[step],
            device_id={axis: (index + step + 1) % count},
            device_id_type=MESH,
        )

    def start(self, turn):
        def body(step, _):
            self.copy(turn, step).start()
            return 0

        lax.fori_loop(0, self.axes[turn][2] - 1, body, 0)

    def take(self, turn):
        self.totals[turn + 1] = self.totals[turn]

        def body(step, _):
            self.copy(turn, step).wait()
            self.totals[turn + 1] += self.arrived[turn][step]
            return 0

        lax.fori_loop(0, self.axes[turn][2] - 1, body, 0)


def reduced_inside(step):
    return step % 32 == 0


class Nothing:
    def __getattr__(self, name):
        return lambda *arguments: None


def select_lanes(rows, columns, source):
    row = lax.broadcasted_iota(jnp.int32, (rows, columns), 0)
    column = lax.broadcasted_iota(jnp.int32, (rows, columns), 1)
    return jnp.where(row == source(column), 1.0, 0.0).astype(jnp.bfloat16)


def forward_kernel(
    n_t,
    input_ref,
    attn_gain_ref,
    moe_gain_ref,
    q_w_ref,
    k_w_ref,
    v_w_ref,
    out_w_ref,
    grad_ref,
    cos_ref,
    sin_ref,
    *rest,
):
    stored, rest = rest[:7], rest[7:]
    (
        moe_out,
        grad_out,
        hidden_out,
        lse_out,
        q_out,
        k_out,
        v_out,
        o_out,
        rows_out,
        qkv_out,
        double_out,
        store_sem,
        weights,
        part,
        arrived,
        acc,
        rows_send,
        rows_recv,
        grad_send,
        grad_recv,
        moe_send,
        moe_recv,
        line_send,
        line_recv,
    ) = rest
    held = (q_out, k_out, v_out, o_out, rows_out, qkv_out, double_out)
    place = lax.axis_index("tensor")
    heads = q_out.shape[0]
    local, width = input_ref.shape
    barrier = pltpu.get_barrier_semaphore()
    for step in range(1, n_t):
        pl.semaphore_signal(
            barrier,
            inc=1,
            device_id={"tensor": (place + step) % n_t},
            device_id_type=MESH,
        )
    wide = input_ref[...].astype(jnp.float32)
    scale = lax.rsqrt(jnp.mean(wide * wide, axis=1, keepdims=True) + EPSILON)
    rows_out[place] = (wide * scale * attn_gain_ref[...].reshape(1, width)).astype(jnp.bfloat16)
    grad_out[place] = grad_ref[...]
    pl.semaphore_wait(barrier, n_t - 1)

    rows_gather = LineGather(rows_out, rows_send, rows_recv, place)
    grad_gather = LineGather(grad_out, grad_send, grad_recv, place, GRAD_PIECES)
    moe_gather = LineGather(moe_out, moe_send, moe_recv, place, PIECES)
    line = LineScatter(part, arrived, line_send, line_recv, place, PIECES)
    rows_gather.start()

    columns = heads * HD
    twice = select_lanes(columns, heads * 128, lambda c: c // 128 * HD + c % HD)
    swapped = select_lanes(
        columns,
        heads * 128,
        lambda c: c // 128 * HD + (c % HD + c % 128 // HD * (HD // 2)) % HD,
    )
    for n, (ref, lanes) in enumerate(
        ((q_w_ref, swapped), (k_w_ref, swapped), (v_w_ref, twice))
    ):
        weights[n * heads * 128 : (n + 1) * heads * 128, :] = dot_tn(lanes, ref[...]).astype(
            jnp.bfloat16
        )
    for n, ref in enumerate((q_w_ref, k_w_ref, v_w_ref)):
        qkv_out[n * columns : (n + 1) * columns, :] = ref[...]
    qkv_out[3 * columns :, :] = jnp.zeros(
        (qkv_out.shape[0] - 3 * columns, width), jnp.bfloat16
    )
    double_out[...] = dot_tn(twice, out_w_ref[...]).astype(jnp.bfloat16)

    def project(block):
        at = pl.ds(pl.multiple_of(block * local, local), local)
        product = dot_nt(rows_out[block], weights[...])
        cosine, sine = cos_ref[at, :], sin_ref[at, :]
        for n, target in enumerate((q_out, k_out, v_out)):
            for h in range(heads):
                start = (n * heads + h) * 128
                piece = product[:, start : start + 128]
                if n < 2:
                    piece = piece * cosine + pltpu.roll(piece, 64, 1) * sine
                target[h, at, :] = piece.astype(jnp.bfloat16)

    def arrive(distance, _):
        @pl.when(distance > 0)
        def _():
            rows_gather.step(distance)

        def side(way, _):
            block = place + (2 * way - 1) * distance

            @pl.when((block >= 0) & (block < n_t) & ((distance > 0) | (way == 0)))
            def _():
                project(block)

            return 0

        lax.fori_loop(0, 2, side, 0)
        return 0

    lax.fori_loop(0, n_t, arrive, 0)
    grad_gather.start()

    factor = 0.5 * HD ** (-0.5)

    lse_out[...] = jnp.zeros_like(lse_out)

    def attend(block):
        at = slice(block * local, (block + 1) * local)
        seen = (block + 1) * local
        mixed = []
        for h in range(heads):
            scores = dot_nt(q_out[h, at, :], k_out[h, 0:seen, :]) * factor
            top = jnp.max(scores, axis=1, keepdims=True)
            exps = jnp.exp(scores - top)
            total = jnp.sum(exps, axis=1, keepdims=True)
            probs = (exps / total).astype(jnp.bfloat16)
            out = dot(probs, v_out[h, 0:seen, :]).astype(jnp.bfloat16)
            o_out[h, at, :] = out
            mixed.append(out)
            log_total = jnp.broadcast_to(top + jnp.log(total), (local, 128))
            lse_out[h : h + 1, at] = log_total.T[0:1, :]
        mixed = jnp.concatenate(mixed, axis=1)
        part[block] = (0.5 * dot(mixed, double_out[...])).astype(jnp.bfloat16)

    for block in range(n_t):
        attend(block)
    ends_first = (n_t - 1, 0, *range(n_t - 2, 0, -1))
    line.originate(ends_first, (0,))
    stores = [
        pltpu.make_async_copy(source, target, store_sem.at[n])
        for n, (source, target) in enumerate(zip(held, stored))
    ]
    for store in stores:
        store.start()
    lag = n_t - 2
    for turn in range(PIECES + lag + n_t - 1):
        line.forward(turn, ends_first)
        if turn + 1 < PIECES:
            line.drain(ends_first, turn)
            line.originate(ends_first, (turn + 1,))
        if 0 <= turn - lag < PIECES:
            n = turn - lag
            line.collect(acc, n)
            at = slice(n * (local // PIECES), (n + 1) * (local // PIECES))
            hidden = input_ref[at, :].astype(jnp.float32) + acc[at, :]
            hidden_out[at, :] = hidden
            scale = lax.rsqrt(jnp.mean(hidden * hidden, axis=1, keepdims=True) + EPSILON)
            moe_out[place, at, :] = (hidden * scale * moe_gain_ref[...].reshape(1, width)).astype(jnp.bfloat16)
            moe_gather.start(n)
        for step in range(1, n_t):
            if 0 <= turn - lag - step < PIECES:
                moe_gather.step(step, turn - lag - step)
        if turn % 2 == 0 and turn // 2 + 1 < n_t:
            grad_gather.step(turn // 2 + 1)
    for exchange in (rows_gather, moe_gather, line):
        exchange.finish()
    grad_gather.finish((0,))
    for store in stores:
        store.wait()


def forward(n_t, layer_input, attn_gain, moe_gain, q_w, k_w, v_w, out_w, grad_out, cosine, sine):
    local, width = layer_input.shape
    group = local * n_t
    heads = q_w.shape[0] // HD
    bf, f32 = jnp.bfloat16, jnp.float32
    dma = pltpu.SemaphoreType.DMA
    vmem = pl.BlockSpec(memory_space=pltpu.VMEM)
    blocks = (n_t, local, width)
    qkv_width = -(-3 * heads * HD // 128) * 128
    stored = (
        *[jax.ShapeDtypeStruct((heads, group, 128), bf)] * 4,
        jax.ShapeDtypeStruct(blocks, bf),
        jax.ShapeDtypeStruct((qkv_width, width), bf),
        jax.ShapeDtypeStruct((heads * 128, width), bf),
    )
    outs = (
        *stored,
        *[jax.ShapeDtypeStruct(blocks, bf)] * 2,
        jax.ShapeDtypeStruct((local, width), f32),
        jax.ShapeDtypeStruct((8, group), f32),
    )
    return pl.pallas_call(
        functools.partial(forward_kernel, n_t),
        out_shape=outs,
        in_specs=[vmem] * 10,
        out_specs=(*[pl.BlockSpec(memory_space=pl.ANY)] * len(stored), *[vmem] * 4),
        scratch_shapes=[
            *[pltpu.VMEM(a.shape, a.dtype) for a in stored],
            dma((len(stored),)),
            pltpu.VMEM((3 * heads * 128, width), bf),
            pltpu.VMEM(blocks, bf),
            pltpu.VMEM((n_t + 1, local, width), bf),
            pltpu.VMEM((local, width), f32),
            *[s for n in (1, GRAD_PIECES, PIECES) for s in (dma((2, n_t, n)), dma((n_t, n)))],
            dma((2, n_t, PIECES)),
            dma((2, n_t, PIECES)),
        ],
        compiler_params=pltpu.CompilerParams(
            collective_id=2, has_side_effects=True, vmem_limit_bytes=56 << 20
        ),
        name="forward",
    )(layer_input, attn_gain, moe_gain, q_w, k_w, v_w, out_w, grad_out, cosine, sine)


def expert_kernel(
    sizes,
    moe_ref,
    half_ref,
    grad_ref,
    routes_ref,
    residual_ref,
    router_ref,
    gate_ref,
    up_ref,
    down_ref,
    back_ref,
    sum_ref,
    chosen_ref,
    *rest,
):
    n_dp, n_t, ffn_count, route_count, inside = sizes
    weight_outs = rest[: 2 if inside else 1]
    (
        probs_s,
        rank_s,
        router_s,
        hit_s,
        turned_s,
        slot_s,
        rows_s,
        gate_s,
        up_s,
        active_s,
        out_s,
        grad_s,
        part_s,
        arrived_s,
        acc,
        weight_s,
        grad_send,
        grad_recv,
        half_sem,
        line_send,
        line_recv,
        own_sem,
        *paired,
    ) = rest[2 if inside else 1 :]
    turn = pl.program_id(0)
    expert = turn % ffn_count
    slot = turn % 2
    dp = lax.axis_index("dp")
    place = lax.axis_index("tensor")
    local, width = grad_ref.shape
    rows = n_t * local
    hidden = gate_ref.shape[2]
    step = width // n_dp
    grad_rows = local // GRAD_PIECES
    gather = LineGather(grad_s, grad_send, grad_recv, place, GRAD_PIECES)
    line = LineScatter(part_s, arrived_s, line_send, line_recv, place, SUM_PIECES)
    blocks = tuple(range(n_t))
    ends_first = (n_t - 1, 0, *range(n_t - 2, 0, -1))

    def line_turn(n):
        line.forward(n, ends_first)
        if n + 1 < SUM_PIECES:
            line.drain(ends_first, n)
            line.originate(ends_first, (n + 1,))

    def half_copy(block):
        return pltpu.make_async_copy(
            half_ref.at[block, pl.ds(0, grad_rows)],
            grad_s.at[block, pl.ds(0, grad_rows)],
            half_sem.at[block],
        )

    early = min(EARLY, ffn_count)
    core = bit_of(dp, 0)
    if inside:
        pair_s, pair_send, pair_recv, stage_send, stage_recv = paired
        splits = ((0, 3 * hidden // 2), (3 * hidden // 2, 3 * hidden // 2))
        sems = (None, None, None, [stage_send], [stage_recv])
        halving = Halving(
            None, pair_s, None, [weight_outs[1]], sems, dp, log2_of(n_dp), splits
        )

    def own_copy(e, at):
        return pltpu.make_async_copy(
            pair_s.at[e] if inside else weight_s.at[at], weight_outs[0].at[e], own_sem.at[e]
        )

    def pair_copy(e, at):
        return pltpu.make_async_remote_copy(
            src_ref=weight_s.at[at, 1 - core],
            dst_ref=pair_s.at[e],
            send_sem=pair_send.at[e],
            recv_sem=pair_recv.at[e],
            device_id={"dp": flipped(dp, 0)},
            device_id_type=MESH,
        )

    def left(e, at):
        if inside:
            pair_copy(e, at).wait_send()
        else:
            own_copy(e, at).wait()

    def settle(e, at):
        pair_copy(e, at).wait_recv()
        for block in range(n_dp // 2):
            halving.add_rows(pair_s.at[e, block], weight_s.at[at, core, block])
        own_copy(e, at).start()

        @pl.when(e < early)
        def _():
            halving.send_stage(e, 0)

    def combine(block):
        at = slice(block * local, (block + 1) * local)
        out = out_s[...].reshape(ffn_count * CAP, width)
        return dot(turned_s[at, :], out).astype(jnp.bfloat16)

    @pl.when(turn == 0)
    def _():
        for block in blocks:
            half_copy(block).start()
        grad_s[place, grad_rows:, :] = grad_ref[grad_rows:, :]
        greet((("tensor", place, n_t), ("dp", dp, n_dp)))
        gather.start(1)
        router_s[...] = jnp.zeros_like(router_s)
        router_s[0:route_count, :] = router_ref[...]
        parts = three_parts(router_s[...])
        logits = jnp.concatenate(
            [residual_ref[...], jnp.zeros((EXP_PAD - route_count, rows), jnp.float32)], axis=0
        )
        moe = moe_ref[...].reshape(rows, width)
        for part in parts:
            logits = logits + dot_nt(part, moe)
        index = lax.broadcasted_iota(jnp.int32, (EXP_PAD, rows), 0)
        logits = jnp.where(index < route_count, logits, MASKED)
        top = jnp.max(logits, axis=0, keepdims=True)
        exps = jnp.exp(logits - top)
        probs_s[...] = exps / jnp.sum(exps, axis=0, keepdims=True)
        named = (routes_ref[0:1, :] == index) | (routes_ref[1:2, :] == index)
        named = jnp.where(named, 1.0, 0.0)
        before = lax.broadcasted_iota(jnp.int32, (256, 256), 0)
        after = lax.broadcasted_iota(jnp.int32, (256, 256), 1)
        earlier = jnp.where(before < after, 1.0, 0.0).astype(jnp.bfloat16)
        total = jnp.zeros((EXP_PAD, 1), jnp.float32)
        for start in range(0, rows, 256):
            block = named[:, start : start + 256]
            rank = dot(block.astype(jnp.bfloat16), earlier) + total
            rank_s[:, start : start + 256] = jnp.where(block > 0.5, rank, -1.0)
            total = total + jnp.sum(block, axis=1, keepdims=True)

    @pl.when(turn < ffn_count)
    def _():
        place_in = lax.broadcasted_iota(jnp.int32, (CAP, rows), 0).astype(jnp.float32)
        hit = rank_s[pl.ds(expert, 1), :] == place_in
        slot_weight = jnp.sum(
            jnp.where(hit, probs_s[pl.ds(expert, 1), :], 0.0), axis=1, keepdims=True
        )
        slot_s[expert] = slot_weight
        dispatch = jnp.where(hit, 1.0, 0.0).astype(jnp.bfloat16)
        hit_s[expert] = dispatch
        turned_s[:, pl.ds(pl.multiple_of(expert * CAP, CAP), CAP)] = dispatch.T
        rows_in = dot(dispatch, moe_ref[...].reshape(rows, width)).astype(jnp.bfloat16)
        rows_s[expert] = rows_in
        gate_pre = dot(rows_in, gate_ref[0])
        up_pre = dot(rows_in, up_ref[0])
        sigmoid = 1.0 / (1.0 + jnp.exp(-gate_pre))
        silu = gate_pre * sigmoid
        active = (silu * up_pre).astype(jnp.bfloat16)
        active_s[expert] = active
        gate_s[expert] = up_pre * (sigmoid + silu * (1.0 - sigmoid))
        up_s[expert] = silu
        out_s[expert] = (dot(active, down_ref[0]) * slot_weight).astype(jnp.bfloat16)
        for distance in range(1, n_t - 1):

            @pl.when(turn == 3 * distance - 2)
            def _(distance=distance):
                gather.step(distance, 1)

    @pl.when(turn == ffn_count)
    def _():
        for block in blocks:
            part_s[block] = combine(block)
            half_copy(block).wait()
        line.originate(ends_first, (0,))
        gather.step(n_t - 1, 1)

    @pl.when(turn >= ffn_count)
    def _():
        active = active_s[expert]
        rows_grad = dot(hit_s[expert], grad_s[...].reshape(rows, width))
        low = rows_grad.astype(jnp.bfloat16)
        grad_active = dot_nt(low, down_ref[0])
        slot_weight = slot_s[expert]
        inner = jnp.sum(grad_active * active.astype(jnp.float32), axis=1, keepdims=True)
        lane = lax.broadcasted_iota(jnp.int32, (CAP, 128), 1)
        inner_parts = jnp.zeros((CAP, 128), jnp.float32)
        for n, inner_part in enumerate(three_parts(inner)):
            inner_parts = jnp.where(lane == n, inner_part.astype(jnp.float32), inner_parts)
        chosen_rows = dot_tn(inner_parts.astype(jnp.bfloat16), hit_s[expert])
        chosen_row = chosen_rows[0:1] + chosen_rows[1:2] + chosen_rows[2:3]
        for n in blocks:
            chosen_ref[n, pl.ds(expert, 1), :] = chosen_row[:, n * local : (n + 1) * local]
        grad_low = (rows_grad * slot_weight).astype(jnp.bfloat16)
        grad_active = grad_active * slot_weight
        grad_gate = (grad_active * gate_s[expert]).astype(jnp.bfloat16)
        grad_up = (grad_active * up_s[expert]).astype(jnp.bfloat16)
        out_s[expert] = (dot_nt(grad_gate, gate_ref[0]) + dot_nt(grad_up, up_ref[0])).astype(
            jnp.bfloat16
        )

        @pl.when(expert >= 2)
        def _():
            left(expert - 2, slot)

        rows_in = rows_s[expert]
        for n, (one, other) in enumerate(
            ((rows_in, grad_gate), (rows_in, grad_up), (grad_low, active))
        ):
            product = dot_tn(one, other).astype(jnp.bfloat16)
            for d in range(n_dp):
                weight_s[slot, d % 2, d // 2, :, n * hidden : (n + 1) * hidden] = product[
                    d * step : (d + 1) * step
                ]
        if inside:
            pair_copy(expert, slot).start()

            @pl.when(expert >= 1)
            def _():
                settle(expert - 1, 1 - slot)

        else:
            own_copy(expert, slot).start()
        for n, at in enumerate(LINE_TURNS):

            @pl.when(expert == at)
            def _(n=n):
                line_turn(n)

    @pl.when(turn == 2 * ffn_count - 1)
    def _():
        for block in blocks:
            back_ref[block] = combine(block)
        if inside:
            settle(ffn_count - 1, (ffn_count - 1) % 2)
        for e in range(ffn_count - 2, ffn_count):
            left(e, e % 2)
        for n in range(len(LINE_TURNS), SUM_PIECES + n_t - 3):
            line_turn(n)
        for n in range(SUM_PIECES):
            line.collect(acc, n)
        sum_ref[...] = acc[...]
        line.finish()
        gather.finish((1,))
        if inside:
            for e in range(ffn_count):
                own_copy(e, e % 2).wait()
            for e in range(early):
                for k in range(halving.number(0)):
                    for part in (0, 1):
                        halving.stage_copy(e, part, 0, k).wait()


def experts(n_dp, n_t, moe_rows, grad_half, grad_out, routes_t, residual_t, router_t, gate_w, up_w, down_w):
    _, local, width = moe_rows.shape
    rows = n_t * local
    route_count = router_t.shape[0]
    ffn_count, _, hidden = gate_w.shape
    step = width // n_dp
    half = n_dp // 2
    inside = reduced_inside(step)
    bf, f32 = jnp.bfloat16, jnp.float32
    dma = pltpu.SemaphoreType.DMA

    def whole(shape):
        return pl.BlockSpec(shape, lambda s: (0,) * len(shape), pipeline_mode=pl.Buffered(1))

    any_space = pl.BlockSpec(memory_space=pl.ANY)
    item = (half, step, 3 * hidden)
    weights = (
        [
            jax.ShapeDtypeStruct((ffn_count, *item), bf),
            jax.ShapeDtypeStruct((min(EARLY, ffn_count), half // 2, *item[1:]), bf),
        ]
        if inside
        else [jax.ShapeDtypeStruct((ffn_count, 2, *item), bf)]
    )
    paired = []
    if inside:
        stage = dma((min(EARLY, ffn_count), 2, half // 2))
        paired = [pltpu.VMEM((ffn_count, *item), bf), dma((ffn_count,)), dma((ffn_count,)), stage, stage]
    blocks = (n_t, local, width)
    return pl.pallas_call(
        functools.partial(expert_kernel, (n_dp, n_t, ffn_count, route_count, inside)),
        grid=(2 * ffn_count,),
        out_shape=(
            jax.ShapeDtypeStruct(blocks, bf),
            jax.ShapeDtypeStruct((local, width), f32),
            jax.ShapeDtypeStruct((n_t, ffn_count, local), f32),
            *weights,
        ),
        in_specs=[
            whole(blocks),
            any_space,
            whole((local, width)),
            whole((2, rows)),
            whole((route_count, rows)),
            whole((route_count, width)),
            pl.BlockSpec((1, width, hidden), lambda s: (s % ffn_count, 0, 0)),
            pl.BlockSpec((1, width, hidden), lambda s: (s % ffn_count, 0, 0)),
            pl.BlockSpec((1, hidden, width), lambda s: (s % ffn_count, 0, 0)),
        ],
        out_specs=(
            whole(blocks),
            whole((local, width)),
            whole((n_t, ffn_count, local)),
            *[any_space for _ in weights],
        ),
        scratch_shapes=[
            pltpu.VMEM((EXP_PAD, rows), f32),
            pltpu.VMEM((EXP_PAD, rows), f32),
            pltpu.VMEM((EXP_PAD, width), f32),
            pltpu.VMEM((ffn_count, CAP, rows), bf),
            pltpu.VMEM((rows, ffn_count * CAP), bf),
            pltpu.VMEM((ffn_count, CAP, 1), f32),
            pltpu.VMEM((ffn_count, CAP, width), bf),
            pltpu.VMEM((ffn_count, CAP, hidden), f32),
            pltpu.VMEM((ffn_count, CAP, hidden), f32),
            pltpu.VMEM((ffn_count, CAP, hidden), bf),
            pltpu.VMEM((ffn_count, CAP, width), bf),
            pltpu.VMEM(blocks, bf),
            pltpu.VMEM(blocks, bf),
            pltpu.VMEM((n_t + 1, local, width), bf),
            pltpu.VMEM((local, width), f32),
            pltpu.VMEM((2, 2, *item), bf),
            dma((2, n_t, GRAD_PIECES)),
            dma((n_t, GRAD_PIECES)),
            dma((n_t,)),
            dma((2, n_t, SUM_PIECES)),
            dma((2, n_t, SUM_PIECES)),
            dma((ffn_count,)),
            *paired,
        ],
        compiler_params=pltpu.CompilerParams(
            dimension_semantics=("arbitrary",),
            collective_id=3,
            has_side_effects=True,
            vmem_limit_bytes=62 << 20,
        ),
        name="experts",
    )(moe_rows, grad_half, grad_out, routes_t, residual_t, router_t, gate_w, up_w, down_w)


def side_forward(norm, named, residual, weight_parts, const_value, route_count, ffn_count):
    lane = lax.broadcasted_iota(jnp.int32, named.shape, 1)
    low = norm.astype(jnp.bfloat16)
    both = sum(dot_nt(low, part) for part in weight_parts)
    logits = jnp.where(lane < route_count, both + residual, MASKED)
    exps = jnp.exp(logits - jnp.max(logits, axis=1, keepdims=True))
    probs = exps / jnp.sum(exps, axis=1, keepdims=True)
    chosen = probs * named
    shares, keeps, rests = [], chosen[:, ffn_count + 1 : ffn_count + 2], []
    for c in range(2):
        at = route_count + 2 * c
        share = 1.0 / (1.0 + jnp.exp(both[:, at + 1 : at + 2] - both[:, at : at + 1]))
        weight = chosen[:, ffn_count + 2 + c : ffn_count + 3 + c]
        shares.append(share)
        keeps = keeps + weight * share
        rests.append(weight * (1.0 - share))
    special = keeps * norm + rests[0] * const_value[0:1] + rests[1] * const_value[1:2]
    return probs, chosen, shares, keeps, rests, special


def side_backward(
    norm, grad, named, forward, chosen_back, weight_parts, const_value, route_count, ffn_count
):
    probs, chosen, shares, keeps, rests, _ = forward
    lane = lax.broadcasted_iota(jnp.int32, named.shape, 1)
    self_dot = jnp.sum(grad * norm, axis=1, keepdims=True)
    value_dots = [
        jnp.sum(grad * const_value[c : c + 1], axis=1, keepdims=True) for c in range(2)
    ]
    d_probs = jnp.where(lane < ffn_count, chosen_back, 0.0)
    d_probs = jnp.where(lane == ffn_count + 1, self_dot, d_probs)
    for c in range(2):
        mixed = shares[c] * self_dot + (1.0 - shares[c]) * value_dots[c]
        d_probs = jnp.where(lane == ffn_count + 2 + c, mixed, d_probs)
    d_probs = d_probs * named
    d_both = probs * (d_probs - jnp.sum(probs * d_probs, axis=1, keepdims=True))
    d_both = jnp.where(lane < route_count, d_both, 0.0)
    for c in range(2):
        weight = chosen[:, ffn_count + 2 + c : ffn_count + 3 + c]
        d_share = shares[c] * (1.0 - shares[c]) * weight * (self_dot - value_dots[c])
        d_both = jnp.where(lane == route_count + 2 * c, d_share, d_both)
        d_both = jnp.where(lane == route_count + 2 * c + 1, -d_share, d_both)
    d_parts = three_parts(d_both)
    back = keeps * grad
    for m, n in ((0, 0), (0, 1), (1, 0), (1, 1)):
        back = back + dot(d_parts[m], weight_parts[n])
    low = norm.astype(jnp.bfloat16)
    weight_part = dot_tn(d_parts[0], low) + dot_tn(d_parts[1], low) + dot_tn(d_parts[2], low)
    value_part = [jnp.sum(rests[c] * grad, axis=0, keepdims=True) for c in range(2)]
    return back, weight_part, value_part


LATE = 9


def backward_kernel(
    sizes,
    sum_ref,
    back_ref,
    chosen_ref,
    hidden_ref,
    moe_ref,
    grad_ref,
    input_ref,
    routes_ref,
    residual_ref,
    router_ref,
    gates_ref,
    value_ref,
    moe_gain_ref,
    attn_gain_ref,
    *rest,
):
    dp_bits, n_t, ffn_count, route_count, attn_split, inside = sizes
    stage_count = dp_bits - 1 if inside else 0
    late_refs, rest = rest[:LATE], rest[LATE:]
    expert_refs = rest[: 2 if inside else 0]
    rest = rest[2 if inside else 0 :]
    (
        output_ref,
        input_grad_ref,
        expert_out,
        attn_out,
        small_out,
        gain_out,
        chosen_in,
        pair_buf,
        line_back,
        staged,
        both_s,
        turned_s,
        grad_rows,
        attn_part,
        acc,
        hidden_grad,
        double_grad,
        delta,
        dq,
        dk,
        dv,
        packed,
    ) = rest[:22]
    loaded, rest = rest[22 : 22 + LATE], rest[22 + LATE :]
    q_ref, k_ref, v_ref, o_ref, lse_ref, rows_ref, qkv_ref, out_w_ref, table_ref = loaded
    if inside:
        attn_pairs, kept = rest[:2]
        stages = rest[2 : 2 + stage_count]
        rest = rest[2 + stage_count :]
        a_kept, a_first = rest[:2]
        a_stages = rest[2 : 2 + stage_count]
        rest = rest[2 + stage_count :]
    else:
        attn_pairs = attn_out
    smalls, small_dp, small_tensor, gains, gain_dp, gain_tensor, side_back = rest[:7]
    rest = list(rest[7:])

    def sems(count):
        taken = rest[:count]
        del rest[:count]
        return taken

    (chosen_send, chosen_recv, gather_send, gather_recv) = sems(4)
    line_sems = [sems(2) for _ in range(2)]
    if inside:
        e_sems = [None] + sems(2) + [sems(stage_count), sems(stage_count)]
        a_sems = sems(3) + [sems(stage_count), sems(stage_count)]
    small_sems = [sems(2), sems(2)]
    gain_sems = [sems(2), sems(2)]
    staged_sem, load_sem = sems(2)
    loads = [
        pltpu.make_async_copy(source, target, load_sem.at[n])
        for n, (source, target) in enumerate(zip(late_refs, loaded))
    ]
    for load in loads:
        load.start()

    dp = lax.axis_index("dp")
    place = lax.axis_index("tensor")
    local = hidden_ref.shape[0]
    width = hidden_ref.shape[1]
    hidden_units = expert_out.shape[-1]
    heads = q_ref.shape[0]
    greet((("dp", dp, 1 << dp_bits), ("tensor", place, n_t)))

    back_line = LineScatter(back_ref, line_back, *line_sems[0], place, PIECES)
    attn_line = LineScatter(attn_part, line_back, *line_sems[1], place, PIECES)
    gather = LineGather(grad_rows, gather_send, gather_recv, place, PIECES)
    half = hidden_units // 2
    attn_width = attn_pairs.shape[-1]
    expert = attn = Nothing()
    if inside:
        splits = ((0, half), (half, half))
        expert = LateHalving(expert_refs, kept, None, stages, e_sems, dp, dp_bits, splits)
        splits = ((0, attn_split), (attn_split, attn_width - attn_split))
        attn = Halving(attn_pairs, a_kept, a_first, a_stages, a_sems, dp, dp_bits, splits)
    everyone = (("dp", dp, 1 << dp_bits), ("tensor", place, n_t))
    small = Exchange(smalls, (small_dp, small_tensor), *small_sems, everyone)
    gain = Exchange(gains, (gain_dp, gain_tensor), *gain_sems, everyone)

    def chosen_copy(step):
        there = (place + step) % n_t
        return pltpu.make_async_remote_copy(
            src_ref=chosen_ref.at[there],
            dst_ref=chosen_in.at[step - 1],
            send_sem=chosen_send.at[step - 1],
            recv_sem=chosen_recv.at[step - 1],
            device_id={"tensor": there},
            device_id_type=MESH,
        )

    ends_first = (n_t - 1, 0, *range(n_t - 2, 0, -1))
    for step in range(1, n_t):
        chosen_copy(step).start()
    back_line.originate(ends_first, (0,))

    def over_experts(action):
        def body(e, _):
            action(e)
            return 0

        def run(first, last):
            lax.fori_loop(first, last, body, 0)

        return run

    early = min(EARLY, ffn_count)
    expert.begin(early, ffn_count)

    norm = moe_ref[place].astype(jnp.float32)
    lane = lax.broadcasted_iota(jnp.int32, (local, 128), 1)
    mine = pl.ds(pl.multiple_of(place * local, local), local)
    turned_s[...] = jnp.zeros_like(turned_s)
    turned_s[0:route_count, :] = residual_ref[:, mine]
    turned_s[16:18, :] = routes_ref[:, mine].astype(jnp.float32)
    turned = turned_s[...].T
    residual = turned
    kind = lane.astype(jnp.float32)
    named = jnp.where((turned[:, 16:17] == kind) | (turned[:, 17:18] == kind), 1.0, 0.0)
    both_s[...] = jnp.zeros_like(both_s)
    both_s[0:route_count, :] = router_ref[...]
    for c in range(2):
        both_s[route_count + 2 * c : route_count + 2 * c + 2, :] = gates_ref[c]
    weight_parts = three_parts(both_s[...])
    const_value = value_ref[...]
    grad = grad_ref[...].astype(jnp.float32)
    forward = side_forward(
        norm, named, residual, weight_parts, const_value, route_count, ffn_count
    )
    pair_buf[...] = hidden_ref[...] + forward[-1]
    chosen_total = chosen_ref[place]
    for step in range(1, n_t):
        chosen_copy(step).wait_recv()
        chosen_total = chosen_total + chosen_in[step - 1]
    chosen_back = jnp.concatenate(
        [chosen_total, jnp.zeros((128 - ffn_count, local), jnp.float32)], axis=0
    ).T
    back, weight_part, value_part = side_backward(
        norm, grad, named, forward, chosen_back, weight_parts, const_value, route_count, ffn_count
    )
    side_back[...] = back
    smalls[0, 1:2, :] = value_part[0]
    smalls[0, 2:3, :] = value_part[1]
    smalls[0, 3:8, :] = jnp.zeros((5, width), jnp.float32)
    smalls[0, 8:24, :] = weight_part[0:16]

    opening = -(-ffn_count // PIECES)
    moe_gain_total = jnp.zeros((1, width), jnp.float32)
    lag = n_t - 2
    for turn in range(PIECES + lag + n_t - 1):
        back_line.forward(turn, ends_first)
        if turn + 1 < PIECES:
            back_line.drain(ends_first, turn)
            back_line.originate(ends_first, (turn + 1,))
        for e in range(turn * opening, min((turn + 1) * opening, ffn_count)):
            expert.open(e, early)
        if 0 <= turn - lag < PIECES:
            n = turn - lag
            at = slice(n * (local // PIECES), (n + 1) * (local // PIECES))
            back_line.collect(acc, n)
            norm_grad = acc[at, :] + side_back[at, :]
            hidden = hidden_ref[at, :]
            scale = lax.rsqrt(jnp.mean(hidden * hidden, axis=1, keepdims=True) + EPSILON)
            u = norm_grad * moe_gain_ref[...].reshape(1, width)
            moe_gain_total = moe_gain_total + jnp.sum(
                norm_grad * hidden * scale, axis=0, keepdims=True
            )
            hidden_grad[at, :] = (
                grad_ref[at, :].astype(jnp.float32)
                + scale * u
                - hidden
                * (scale * scale * scale)
                * jnp.mean(u * hidden, axis=1, keepdims=True)
            )
            grad_rows[place, at, :] = hidden_grad[at, :].astype(jnp.bfloat16)
            if n == PIECES - 1:
                back_line.finish()
            gather.start(n)
        for step in range(1, n_t):
            if 0 <= turn - lag - step < PIECES:
                gather.step(step, turn - lag - step)
    smalls[0, 0:1, :] = moe_gain_total
    small.start(0)
    output_ref[...] = (pair_buf[...] + sum_ref[...]).astype(output_ref.dtype)
    advance = over_experts(lambda e: expert.advance(e, 0))

    for load in loads:
        load.wait()
    rows = local

    def row_block(n):
        return pl.ds(pl.multiple_of(n * rows, rows), rows)

    count = n_t
    head_lane = lax.broadcasted_iota(jnp.int32, (rows, 128), 1)
    low_half = head_lane < 64
    for block in range(count):
        at = pl.ds(block * rows, rows)
        product = dot_nt(grad_rows[block], out_w_ref[...])
        for h in range(heads):
            piece = product[:, h * 128 : (h + 1) * 128].astype(jnp.bfloat16)
            double_grad[h, at, :] = piece
            both = piece.astype(jnp.float32) * o_ref[h, at, :].astype(jnp.float32)
            delta[h : h + 1, at] = 0.5 * jnp.sum(both.T, axis=0, keepdims=True)
    out_pack = []
    for h in range(0, heads, 2):
        o_a = o_ref[h]
        o_b = o_ref[h + 1] if h + 1 < heads else jnp.zeros_like(o_a)
        lanes = lax.broadcasted_iota(jnp.int32, o_a.shape, 1)
        out_pack.append(jnp.where(lanes < 64, o_a, o_b))
    n_half = attn_pairs.shape[2]
    step_rows = attn_pairs.shape[3]
    qkv_width = packed.shape[1]

    def spread(product, start, stop):
        low = product.astype(jnp.bfloat16)
        for d in range(2 * n_half):
            attn_pairs[0, d % 2, d // 2, :, start:stop] = low[d * step_rows : (d + 1) * step_rows]

    for n, pack in enumerate(out_pack):
        total = jnp.zeros((width, 128), jnp.float32)
        for block in range(count):
            total = total + dot_tn(grad_rows[block], pack[block * rows : (block + 1) * rows])
        spread(total, qkv_width + n * 128, qkv_width + (n + 1) * 128)

    dq[...] = jnp.zeros_like(dq)
    factor = 64 ** (-0.5)
    gain_total = jnp.zeros((1, width), jnp.float32)
    for turn, key_block in enumerate(range(count)):
        keys = pl.ds(key_block * rows, rows)
        dk[...] = jnp.zeros_like(dk)
        dv[...] = jnp.zeros_like(dv)

        def query_step(query_block, _, keys=keys):
            at = row_block(query_block)
            for h in range(heads):
                q, g = q_ref[h, at, :], double_grad[h, at, :]
                k, v = k_ref[h, keys, :], v_ref[h, keys, :]
                scores = dot_nt(k, q) * (0.5 * factor)
                probs = jnp.exp(scores - lse_ref[h : h + 1, at])
                d_probs = dot_nt(v, g) * 0.5
                d_scores = (probs * (d_probs - delta[h : h + 1, at])).astype(jnp.bfloat16)
                dk[h] += dot(d_scores, q)
                dv[h] += dot(probs.astype(jnp.bfloat16), g)
                dq[h, at, :] += dot_tn(d_scores, k)
            return 0

        lax.fori_loop(key_block, count, query_step, 0)
        table = table_ref[keys, :]
        pieces = []
        for source in (dq.at[:, keys, :], dk):
            for h in range(heads):
                turned = source[h] * (table * factor)
                pieces.append(turned + pltpu.roll(turned, 64, 1))
        for h in range(heads):
            pieces.append(dv[h])
        if len(pieces) % 2:
            pieces.append(jnp.zeros((rows, 128), jnp.float32))
        for n in range(0, len(pieces), 2):
            packed[keys, n * 64 : n * 64 + 128] = jnp.where(
                low_half, pieces[n], pieces[n + 1]
            ).astype(jnp.bfloat16)
        back_rows = dot(packed[keys, :], qkv_ref[...])
        gain_total = gain_total + jnp.sum(
            back_rows * rows_ref[key_block].astype(jnp.float32), axis=0, keepdims=True
        )
        attn_part[key_block] = back_rows.astype(jnp.bfloat16)
        attn_line.originate((key_block,))
        if turn > 0:
            attn_line.forward_all(key_block - 1)
        if turn == 0:
            advance(early, ffn_count)
        if turn == 1:
            small.take(0)
            small.start(1)

    gains[0] = gain_total / attn_gain_ref[...].reshape(1, width)
    gain.start(0)
    for n in range(qkv_width // 128):
        total = jnp.zeros((width, 128), jnp.float32)
        for block in range(count):
            total = total + dot_tn(
                rows_ref[block], packed[pl.ds(block * rows, rows), n * 128 : (n + 1) * 128]
            )
        spread(total, n * 128, (n + 1) * 128)
    attn.start(0)
    attn_line.forward_all(count - 1)
    gain.take(0)
    gain.start(1)
    attn.open(0)
    for stage in range(1, stage_count - 1):
        over_experts(lambda e, stage=stage: expert.advance(e, stage))(0, ffn_count)
    small.take(1)
    small_out[...] = smalls[2]
    for stage in range(stage_count - 1):
        attn.advance(0, stage)
    gain.take(1)
    gain_out[...] = jnp.broadcast_to(gains[2], gain_out.shape)
    for n in range(PIECES):
        attn_line.collect(acc, n)
    wide = input_ref[...].astype(jnp.float32)
    scale = lax.rsqrt(jnp.mean(wide * wide, axis=1, keepdims=True) + EPSILON)
    w = acc[...] * attn_gain_ref[...].reshape(1, width)
    input_grad_ref[...] = (
        hidden_grad[...]
        + scale * w
        - wide * (scale * scale * scale) * jnp.mean(w * wide, axis=1, keepdims=True)
    ).astype(input_grad_ref.dtype)
    def stored(e):
        return pltpu.make_async_copy(staged.at[e % 2], expert_out.at[e], staged_sem.at[e])

    for e in range(ffn_count if inside else 0):
        if e > 1:
            stored(e - 2).wait()
        expert.close(e, staged.at[e % 2])
        stored(e).start()
    attn.close(0, attn_out)

    attn_line.finish()
    for step in range(1, n_t):
        chosen_copy(step).wait_send()
    gather.finish()

    for e in range(ffn_count):
        expert.finish(e, early)
    attn.finish(0)
    for e in range(ffn_count - 2, ffn_count if inside else 0):
        stored(e).wait()


def backward(dp_count, n_t, ffn_sum, ffn_back, chosen, weight_pairs, hidden, moe_rows, grad_out,
             layer_input, routes, residual, router, gates, const_value, moe_gain, attn_gain,
             q2, k2, v2, o2, lse, attn_rows, qkv_weight, out_double, table):
    late = (q2, k2, v2, o2, lse, attn_rows, qkv_weight, out_double, table)
    local, width = hidden.shape
    group = local * n_t
    ffn_count = weight_pairs[0].shape[0]
    units = weight_pairs[0].shape[-1]
    step = width // dp_count
    half = dp_count // 2
    dp_bits = log2_of(dp_count)
    inside = reduced_inside(step)
    stage_count = dp_bits - 1 if inside else 0
    heads = q2.shape[0]
    qkv_width = qkv_weight.shape[0]
    attn_width = qkv_width + -(-heads // 2) * 128
    attn_split = attn_width // 2 // 128 * 128
    bf, f32 = jnp.bfloat16, jnp.float32
    dma = pltpu.SemaphoreType.DMA

    def numbers(stage):
        return half >> (stage + 1)

    def line(rows_shape):
        return pltpu.VMEM((n_t + 1, *rows_shape[1:]), bf)

    block_shape = (n_t, local, width)
    reduction = []
    if inside:
        reduction = [
            pltpu.VMEM((1, 2, half, step, attn_width), bf),
            pltpu.VMEM((ffn_count, half, step, units), bf),
            *[pltpu.VMEM((ffn_count, numbers(s), step, units), bf) for s in range(stage_count)],
            pltpu.VMEM((1, half, step, attn_width), bf),
            pltpu.VMEM((1, half, step, attn_width), bf),
            *[pltpu.VMEM((1, numbers(s), step, attn_width), bf) for s in range(stage_count)],
        ]
    scratch = [
        pltpu.VMEM((n_t - 1, ffn_count, local), f32),
        pltpu.VMEM((local, width), f32),
        line(block_shape),
        pltpu.VMEM((2, step, units), f32),
        pltpu.VMEM((128, width), f32),
        pltpu.VMEM((128, local), f32),
        pltpu.VMEM(block_shape, bf),
        pltpu.VMEM(block_shape, bf),
        pltpu.VMEM((local, width), f32),
        pltpu.VMEM((local, width), f32),
        pltpu.VMEM((heads, group, 128), bf),
        pltpu.VMEM((8, group), f32),
        pltpu.VMEM((heads, group, 128), f32),
        pltpu.VMEM((heads, local, 128), f32),
        pltpu.VMEM((heads, local, 128), f32),
        pltpu.VMEM((group, qkv_width), bf),
        *[pltpu.VMEM(a.shape, a.dtype) for a in late],
        *reduction,
        pltpu.VMEM((3, 24, width), f32),
        pltpu.VMEM((dp_count - 1, 24, width), f32),
        pltpu.VMEM((n_t - 1, 24, width), f32),
        pltpu.VMEM((3, 1, width), f32),
        pltpu.VMEM((dp_count - 1, 1, width), f32),
        pltpu.VMEM((n_t - 1, 1, width), f32),
        pltpu.VMEM((local, width), f32),
        dma((n_t - 1,)),
        dma((n_t - 1,)),
        dma((2, n_t, PIECES)),
        dma((n_t, PIECES)),
        dma((2, n_t, PIECES)),
        dma((2, n_t, PIECES)),
        dma((2, n_t, PIECES)),
        dma((2, n_t, PIECES)),
        *[
            s
            for n in ((ffn_count, 1) if inside else ())
            for s in (
                *[dma((n,)) for _ in range(2 if n == ffn_count else 3)],
                *[dma((n, 2, numbers(s))) for s in range(stage_count)],
                *[dma((n, 2, numbers(s))) for s in range(stage_count)],
            )
        ],
        *[dma((n - 1,)) for _ in range(4) for n in (dp_count, n_t)],
        dma((ffn_count,)),
        dma((LATE,)),
    ]
    vmem = pl.BlockSpec(memory_space=pltpu.VMEM)
    operands = (ffn_sum, ffn_back, chosen, hidden, moe_rows, grad_out, layer_input, routes, residual,
                router, gates, const_value, moe_gain, attn_gain, *late)
    specs = [vmem] * (len(operands) - LATE) + [pl.BlockSpec(memory_space=pl.ANY)] * LATE
    if inside:
        operands = (*operands, *weight_pairs)
        specs += [pl.BlockSpec(memory_space=pl.ANY)] * 2
    return pl.pallas_call(
        functools.partial(
            backward_kernel, (dp_bits, n_t, ffn_count, residual.shape[0], attn_split, inside)
        ),
        out_shape=(
            jax.ShapeDtypeStruct((local, width), bf),
            jax.ShapeDtypeStruct((local, width), bf),
            jax.ShapeDtypeStruct((ffn_count, step, units) if inside else (8, 128), f32),
            jax.ShapeDtypeStruct((step, attn_width), f32)
            if inside
            else jax.ShapeDtypeStruct((1, 2, half, step, attn_width), bf),
            jax.ShapeDtypeStruct((24, width), f32),
            jax.ShapeDtypeStruct((8, width), f32),
        ),
        in_specs=specs,
        out_specs=(vmem, vmem, pl.BlockSpec(memory_space=pl.ANY), vmem, vmem, vmem),
        scratch_shapes=scratch,
        compiler_params=pltpu.CompilerParams(
            collective_id=1, has_side_effects=True, vmem_limit_bytes=62 << 20
        ),
        name="backward",
    )(*operands)


def rope_lanes(length, head_width):
    position = np.arange(length, dtype=np.float64)[:, None]
    inverse = np.exp(np.arange(head_width // 2) * (-2.0 * math.log(10000.0) / head_width))
    angle = position * inverse[None, :]
    c, s = np.cos(angle), np.sin(angle)
    cosine = np.concatenate([c, c, c, c], axis=1).astype(np.float32)
    sine = np.concatenate([-s, s, s, -s], axis=1).astype(np.float32)
    return cosine, sine


def tidy_kernel(
    wide, route_count, gate_ref, up_ref, down_ref, attn_ref, small_ref, gain_ref, output_ref, grad_ref, *outs
):
    (output, grad, attn_gain, q_out, k_out, v_out, out_out, moe_gain, router, gates, value) = outs[:11]
    for source, target in zip((gate_ref, up_ref, down_ref), outs[11:]):
        target[...] = source[...]

    @pl.when(pl.program_id(0) == 0)
    def _():
        output[...] = output_ref[...]
        grad[...] = grad_ref[...]
        attn_gain[...] = gain_ref[0, :]
        moe_gain[...] = small_ref[0, :]
        value[...] = small_ref[1:3, :]
        router[...] = small_ref[8 : 8 + route_count, :]
        for c in range(2):
            at = 8 + route_count + 2 * c
            gates[c] = small_ref[at : at + 2, :]
        for n, ref in enumerate((q_out, k_out, v_out)):
            ref[...] = attn_ref[:, n * wide : (n + 1) * wide]
        at = -(-3 * wide // 128) * 128
        out_out[...] = attn_ref[:, at : at + -(-wide // 128) * 128].T[0:wide, :]


def tidy(wide, route_count, expert_sum, attn_sum, small, gain, output, input_grad):
    count, step, units = expert_sum.shape
    units = units // 3
    width = small.shape[1]
    f32 = jnp.float32
    group = 2 if count % 2 == 0 else 1

    def whole(shape):
        return pl.BlockSpec(shape, lambda e: (0,) * len(shape), pipeline_mode=pl.Buffered(1))

    small_shapes = (
        (width,),
        (step, wide),
        (step, wide),
        (step, wide),
        (wide, step),
        (width,),
        (route_count, width),
        (2, 2, width),
        (2, width),
    )
    shapes = [output, input_grad]
    shapes += [jax.ShapeDtypeStruct(shape, f32) for shape in small_shapes]
    shapes += [jax.ShapeDtypeStruct((count, step, units), f32)] * 3
    piece = [
        pl.BlockSpec((group, step, units), lambda e, n=n: (e, 0, n)) for n in (0, 1, 2, 0, 0, 0)
    ]
    rest = (attn_sum, small, gain, output, input_grad)
    return pl.pallas_call(
        functools.partial(tidy_kernel, wide, route_count),
        grid=(count // group,),
        out_shape=tuple(jax.ShapeDtypeStruct(s.shape, s.dtype) for s in shapes),
        in_specs=[*piece[:3], *[whole(a.shape) for a in rest]],
        out_specs=(*[whole(s.shape) for s in shapes[:11]], *piece[3:]),
        compiler_params=pltpu.CompilerParams(
            dimension_semantics=("arbitrary",), vmem_limit_bytes=62 << 20
        ),
        name="tidy",
    )(expert_sum, expert_sum, expert_sum, *rest)


def on_device(
    layer_input,
    attn_gain,
    query_weight,
    key_weight,
    value_weight,
    out_weight,
    moe_gain,
    router_weight,
    gate_residual,
    const_gate,
    const_value,
    gate_weight,
    up_weight,
    down_weight,
    routes,
    grad_out,
):
    local_rows, model_width = layer_input.shape
    tensor_size = lax.axis_size("tensor")
    head_count = query_weight.shape[1] // HD
    ffn_count = gate_weight.shape[0]
    route_count = router_weight.shape[1]
    cosine, sine = rope_lanes(LENGTH, HD)
    q2, k2, v2, o2, attn_rows, qkv_weight, out_double, moe_rows, grad_half, hidden, lse = forward(
        tensor_size,
        layer_input,
        attn_gain,
        moe_gain,
        query_weight.T,
        key_weight.T,
        value_weight.T,
        out_weight,
        grad_out,
        jnp.asarray(cosine),
        jnp.asarray(sine),
    )
    n_dp = lax.axis_size("dp")
    ffn_back, ffn_sum, chosen_t, *weight_pairs = experts(
        n_dp,
        tensor_size,
        moe_rows,
        grad_half,
        grad_out,
        routes.T,
        gate_residual.T,
        router_weight.T,
        gate_weight,
        up_weight,
        down_weight,
    )
    output, input_grad, expert_sum, attn_sum_rows, small, gain = backward(
        n_dp,
        tensor_size,
        ffn_sum,
        ffn_back,
        chosen_t,
        weight_pairs,
        hidden,
        moe_rows,
        grad_out,
        layer_input,
        routes.T,
        gate_residual.T,
        router_weight.T,
        jnp.transpose(const_gate, (0, 2, 1)),
        const_value,
        moe_gain,
        attn_gain,
        q2,
        k2,
        v2,
        o2,
        lse,
        attn_rows,
        qkv_weight,
        out_double,
        jnp.asarray(np.concatenate([cosine[:, :HD], sine[:, HD:]], axis=1)),
    )
    if not reduced_inside(model_width // n_dp):

        def scattered(pairs):
            pairs = jnp.transpose(pairs, (2, 1, 3, 0, 4)).reshape(model_width, -1)
            return lax.psum_scatter(pairs, "dp", scatter_dimension=0, tiled=True).astype(
                jnp.float32
            )

        attn_sum_rows = scattered(attn_sum_rows)
        expert_sum = scattered(weight_pairs[0]).reshape(
            model_width // n_dp, ffn_count, weight_pairs[0].shape[-1]
        )
        expert_sum = jnp.transpose(expert_sum, (1, 0, 2))
    outs = list(
        tidy(
            head_count * HD, route_count, expert_sum, attn_sum_rows, small, gain, output, input_grad
        )
    )
    outs[8] = outs[8].T
    outs[9] = jnp.transpose(outs[9], (0, 2, 1))
    outs[13] = jnp.transpose(outs[13], (0, 2, 1))
    return tuple(outs)


def solution(mesh):
    in_specs = (
        P(("dp", "tensor"), None),
        P(),
        P(None, "tensor"),
        P(None, "tensor"),
        P(None, "tensor"),
        P("tensor", None),
        P(),
        P(),
        P("dp", None),
        P(),
        P(),
        P(None, None, "tensor"),
        P(None, None, "tensor"),
        P(None, "tensor", None),
        P("dp", None),
        P(("dp", "tensor"), None),
    )
    out_specs = (
        P(("dp", "tensor"), None),
        P(("dp", "tensor"), None),
        P(),
        P("dp", "tensor"),
        P("dp", "tensor"),
        P("dp", "tensor"),
        P("tensor", "dp"),
        P(),
        P(),
        P(),
        P(),
        P(None, "dp", "tensor"),
        P(None, "dp", "tensor"),
        P(None, "tensor", "dp"),
    )
    return jax.shard_map(
        on_device, mesh=mesh, in_specs=in_specs, out_specs=out_specs, check_vma=False
    )
```

```python
import functools
import math

import jax
import jax.numpy as jnp
import numpy as np
from jax import lax
from jax.experimental import pallas as pl
from jax.experimental.pallas import tpu as pltpu
from jax.sharding import PartitionSpec as P

HD = 64
LENGTH = 1024
BLOCK = 256
CAP = 256


EPSILON = 1e-06
MASKED = -1e30


EXP_PAD = 16


def dot(a, b):
    return jnp.dot(a, b, preferred_element_type=jnp.float32)


def dot_nt(a, b):
    return lax.dot_general(a, b, (((1,), (1,)), ((), ())), preferred_element_type=jnp.float32)


def dot_tn(a, b):
    return lax.dot_general(a, b, (((0,), (0,)), ((), ())), preferred_element_type=jnp.float32)


def three_parts(values):
    first = values.astype(jnp.bfloat16)
    rest = values - first.astype(jnp.float32)
    second = rest.astype(jnp.bfloat16)
    third = (rest - second.astype(jnp.float32)).astype(jnp.bfloat16)
    return (first, second, third)


MESH = pl.DeviceIdType.MESH
PIECES = 8
GRAD_PIECES = 2
SUM_PIECES = 4
LINE_TURNS = (1, 3, 5, 7)
EARLY = 3


def bit_of(index, position):
    return index // (1 << position) % 2


def flipped(index, position):
    return index + (1 << position) * (1 - 2 * bit_of(index, position))


def log2_of(count):
    return count.bit_length() - 1


def greet(axes):
    barrier = pltpu.get_barrier_semaphore()
    for axis, index, count in axes:

        def body(step, _, axis=axis, index=index, count=count):
            pl.semaphore_signal(
                barrier, inc=1, device_id={axis: (index + step) % count}, device_id_type=MESH
            )
            return 0

        lax.fori_loop(1, count, body, 0)
    pl.semaphore_wait(barrier, sum(count - 1 for _, _, count in axes))


class LineGather:
    def __init__(self, blocks, send, recv, place, pieces=1):
        self.blocks, self.send, self.recv, self.place = blocks, send, recv, place
        self.count, self.pieces = blocks.shape[0], pieces
        self.rows = blocks.shape[1] // pieces

    def copy(self, block, n, way):
        piece = self.blocks.at[block, pl.ds(n * self.rows, self.rows)]
        return pltpu.make_async_remote_copy(
            src_ref=piece,
            dst_ref=piece,
            send_sem=self.send.at[way, block, n],
            recv_sem=self.recv.at[block, n],
            device_id={"tensor": self.place + 1 - 2 * way},
            device_id_type=MESH,
        )

    def start(self, n=0):
        @pl.when(self.place < self.count - 1)
        def _():
            self.copy(self.place, n, 0).start()

        @pl.when(self.place > 0)
        def _():
            self.copy(self.place, n, 1).start()

    def step(self, distance, n=0):
        below, above = self.place - distance, self.place + distance

        @pl.when(below >= 0)
        def _():
            self.copy(below, n, 0).wait_recv()

            @pl.when(self.place < self.count - 1)
            def _():
                self.copy(below, n, 0).start()

        @pl.when(above < self.count)
        def _():
            self.copy(above, n, 1).wait_recv()

            @pl.when(self.place > 0)
            def _():
                self.copy(above, n, 1).start()

    def finish(self, pieces=None):
        pieces = range(self.pieces) if pieces is None else pieces
        for distance in range(self.count):
            below, above = self.place - distance, self.place + distance

            @pl.when((below >= 0) & (self.place < self.count - 1))
            def _(below=below):
                for n in pieces:
                    self.copy(below, n, 0).wait_send()

            @pl.when((above < self.count) & (self.place > 0))
            def _(above=above):
                for n in pieces:
                    self.copy(above, n, 1).wait_send()


class LineScatter:
    def __init__(self, parts, arrived, send, recv, place, pieces):
        self.parts, self.arrived, self.send, self.recv = parts, arrived, send, recv
        self.place, self.count, self.pieces = place, parts.shape[0], pieces
        self.rows = parts.shape[1] // pieces
        self.drained = set()

    def piece(self, ref, block, n):
        return ref.at[block, pl.ds(n * self.rows, self.rows)]

    def copy(self, block, n, way, own=False):
        there = self.piece(self.arrived, block + 1 - way, n)
        return pltpu.make_async_remote_copy(
            src_ref=self.piece(self.parts, block, n) if own else there,
            dst_ref=there,
            send_sem=self.send.at[way, block, n],
            recv_sem=self.recv.at[way, block, n],
            device_id={"tensor": self.place + 1 - 2 * way},
            device_id_type=MESH,
        )

    def originate(self, blocks, pieces=None):
        for way, first in ((0, 0), (1, self.count - 1)):
            sent = [block for block in blocks if block != first]
            if sent:

                @pl.when(self.place == first)
                def _(way=way, sent=sent):
                    for n in pieces or range(self.pieces):
                        for block in sent:
                            self.copy(block, n, way, own=True).start()

    def drain(self, blocks, n):
        for way, first in ((0, 0), (1, self.count - 1)):
            sent = [block for block in blocks if block != first]
            self.drained.update((first, block, n) for block in sent)
            if sent:

                @pl.when(self.place == first)
                def _(way=way, sent=sent):
                    for block in sent:
                        self.copy(block, n, way).wait_send()

    def pass_piece(self, block, n, way):
        self.copy(block, n, way).wait_recv()
        there = self.piece(self.arrived, block + 1 - way, n)
        mine = self.piece(self.parts, block, n)
        there[...] = (there[...].astype(jnp.float32) + mine[...].astype(jnp.float32)).astype(
            there.dtype
        )
        self.copy(block, n, way).start()

    def hops(self, place, way):
        return place if way == 0 else self.count - 1 - place

    def forward(self, turn, blocks):
        for place in range(1, self.count - 1):
            passed = []
            for block in blocks:
                way = 0 if place < block else 1
                n = turn - self.hops(place, way) + 1
                if place != block and 0 <= n < self.pieces:
                    passed.append((self.hops(place, way), block, n, way))
            if passed:

                @pl.when(self.place == place)
                def _(passed=passed):
                    for _, block, n, way in sorted(passed, key=lambda item: -item[0]):
                        self.pass_piece(block, n, way)

    def forward_all(self, block):
        for turn in range(self.pieces + self.count - 3):
            self.forward(turn, (block,))

    def collect(self, total, n):
        place = self.place
        rows = slice(n * self.rows, (n + 1) * self.rows)
        total[rows, :] = self.parts[place, rows, :].astype(jnp.float32)
        for way in (0, 1):

            @pl.when(place > 0 if way == 0 else place < self.count - 1)
            def _(way=way):
                self.copy(place, n, way).wait_recv()
                total[rows, :] += self.arrived[place + 1 - way, rows, :].astype(jnp.float32)

    def finish(self):
        for place in range(self.count):
            left = [
                (block, n)
                for block in range(self.count)
                for n in range(self.pieces)
                if block != place and (place, block, n) not in self.drained
            ]
            if left:

                @pl.when(self.place == place)
                def _(place=place, left=left):
                    for block, n in left:
                        self.copy(block, n, 0 if place < block else 1).wait_send()


class Halving:
    def __init__(self, source, kept, first, stages, sems, dp, dp_bits, splits):
        self.source, self.kept, self.first, self.stages = source, kept, first, stages
        self.first_send, self.first_recv, self.local, self.send, self.recv = sems
        self.dp, self.bits, self.splits = dp, dp_bits, splits
        self.core = bit_of(dp, 0)
        upper = list(range(dp_bits - 1))
        self.orders = (upper, upper[1:] + upper[:1])

    def first_copy(self, e):
        return pltpu.make_async_remote_copy(
            src_ref=self.source.at[e, 1 - self.core],
            dst_ref=self.first.at[e],
            send_sem=self.first_send.at[e],
            recv_sem=self.first_recv.at[e],
            device_id={"dp": flipped(self.dp, 0)},
            device_id_type=MESH,
        )

    def local_copy(self, e):
        return pltpu.make_async_copy(
            self.source.at[e, self.core], self.kept.at[e], self.local.at[e]
        )

    def blocks(self, part, stage, k, mine):
        order = self.orders[part]
        index = 0
        for done in order[:stage]:
            index = index + (1 << done) * bit_of(self.dp, done + 1)
        here = bit_of(self.dp, order[stage] + 1)
        index = index + (1 << order[stage]) * (here if mine else 1 - here)
        for n, free in enumerate(order[stage + 1 :]):
            index = index + (1 << free) * (k // (1 << n) % 2)
        return index

    def width(self, part):
        return pl.ds(*self.splits[part])

    def stage_copy(self, e, part, stage, k):
        start, size = self.splits[part]
        return pltpu.make_async_remote_copy(
            src_ref=self.kept.at[e, self.blocks(part, stage, k, False), :, pl.ds(start, size)],
            dst_ref=self.stages[stage].at[e, k, :, pl.ds(start, size)],
            send_sem=self.send[stage].at[e, part, k],
            recv_sem=self.recv[stage].at[e, part, k],
            device_id={"dp": flipped(self.dp, self.orders[part][stage] + 1)},
            device_id_type=MESH,
        )

    def number(self, stage):
        return 1 << (self.bits - 2 - stage)

    def start(self, e):
        self.first_copy(e).start()
        self.local_copy(e).start()

    def send_stage(self, e, stage):
        for k in range(self.number(stage)):
            for part in (0, 1):
                self.stage_copy(e, part, stage, k).start()

    def add_rows(self, target, addend):
        rows = target.shape[0]
        step = 32 if rows % 32 == 0 else rows

        def body(n, _):
            at = pl.ds(pl.multiple_of(n * step, step), step)
            target[at, :] = (
                target[at, :].astype(jnp.float32) + addend[at, :].astype(jnp.float32)
            ).astype(target.dtype)
            return 0

        lax.fori_loop(0, rows // step, body, 0)

    def open(self, e):
        self.first_copy(e).wait_recv()
        self.local_copy(e).wait()
        for block in range(self.kept.shape[1]):
            self.add_rows(self.kept.at[e, block], self.first.at[e, block])
        self.send_stage(e, 0)

    def advance(self, e, stage, arrived=False):
        for k in range(self.number(stage)):
            for part in (0, 1):
                if not arrived:
                    self.stage_copy(e, part, stage, k).wait_recv()
                block = self.blocks(part, stage, k, True)
                self.add_rows(
                    self.kept.at[e, block, :, self.width(part)],
                    self.stages[stage].at[e, k, :, self.width(part)],
                )
        self.send_stage(e, stage + 1)

    def close(self, e, out):
        stage = self.bits - 2
        for part in (0, 1):
            self.stage_copy(e, part, stage, 0).wait_recv()
            block = self.blocks(part, stage, 0, True)
            columns = self.width(part)
            out[:, columns] = self.kept[e, block, :, columns].astype(jnp.float32) + self.stages[
                stage
            ][e, 0, :, columns].astype(jnp.float32)

    def finish(self, e):
        self.first_copy(e).wait_send()
        for stage in range(self.bits - 1):
            for k in range(self.number(stage)):
                for part in (0, 1):
                    self.stage_copy(e, part, stage, k).wait_send()


class LateHalving(Halving):
    def item_copy(self, e):
        return pltpu.make_async_copy(self.source[0].at[e], self.kept.at[e], self.local.at[e])

    def stage_item(self, e):
        return pltpu.make_async_copy(
            self.source[1].at[e], self.stages[0].at[e], self.first_recv.at[e]
        )

    def begin(self, early, count):
        for e in range(count):
            self.item_copy(e).start()
            if e < early:
                self.stage_item(e).start()

    def open(self, e, early):
        self.item_copy(e).wait()
        if e < early:
            self.stage_item(e).wait()
            self.advance(e, 0, arrived=True)
        else:
            self.send_stage(e, 0)

    def finish(self, e, early):
        for stage in range(self.bits - 1):
            if stage > 0 or e >= early:
                for k in range(self.number(stage)):
                    for part in (0, 1):
                        self.stage_copy(e, part, stage, k).wait_send()


class Exchange:
    def __init__(self, totals, arrived, sends, recvs, axes):
        self.totals, self.arrived, self.sends, self.recvs, self.axes = (
            totals,
            arrived,
            sends,
            recvs,
            axes,
        )

    def copy(self, turn, step):
        axis, index, count = self.axes[turn]
        return pltpu.make_async_remote_copy(
            src_ref=self.totals.at[turn],
            dst_ref=self.arrived[turn].at[step],
            send_sem=self.sends[turn].at[step],
            recv_sem=self.recvs[turn].at[step],
            device_id={axis: (index + step + 1) % count},
            device_id_type=MESH,
        )

    def start(self, turn):
        def body(step, _):
            self.copy(turn, step).start()
            return 0

        lax.fori_loop(0, self.axes[turn][2] - 1, body, 0)

    def take(self, turn):
        self.totals[turn + 1] = self.totals[turn]

        def body(step, _):
            self.copy(turn, step).wait()
            self.totals[turn + 1] += self.arrived[turn][step]
            return 0

        lax.fori_loop(0, self.axes[turn][2] - 1, body, 0)


def reduced_inside(step):
    return step % 32 == 0


class Nothing:
    def __getattr__(self, name):
        return lambda *arguments: None


def select_lanes(rows, columns, source):
    row = lax.broadcasted_iota(jnp.int32, (rows, columns), 0)
    column = lax.broadcasted_iota(jnp.int32, (rows, columns), 1)
    return jnp.where(row == source(column), 1.0, 0.0).astype(jnp.bfloat16)


def forward_kernel(
    n_t,
    input_ref,
    attn_gain_ref,
    moe_gain_ref,
    q_w_ref,
    k_w_ref,
    v_w_ref,
    out_w_ref,
    grad_ref,
    cos_ref,
    sin_ref,
    *rest,
):
    stored, rest = rest[:7], rest[7:]
    (
        moe_out,
        grad_out,
        hidden_out,
        lse_out,
        q_out,
        k_out,
        v_out,
        o_out,
        rows_out,
        qkv_out,
        double_out,
        store_sem,
        weights,
        part,
        arrived,
        acc,
        rows_send,
        rows_recv,
        grad_send,
        grad_recv,
        moe_send,
        moe_recv,
        line_send,
        line_recv,
    ) = rest
    held = (q_out, k_out, v_out, o_out, rows_out, qkv_out, double_out)
    place = lax.axis_index("tensor")
    heads = q_out.shape[0]
    local, width = input_ref.shape
    barrier = pltpu.get_barrier_semaphore()
    for step in range(1, n_t):
        pl.semaphore_signal(
            barrier,
            inc=1,
            device_id={"tensor": (place + step) % n_t},
            device_id_type=MESH,
        )
    wide = input_ref[...].astype(jnp.float32)
    scale = lax.rsqrt(jnp.mean(wide * wide, axis=1, keepdims=True) + EPSILON)
    rows_out[place] = (wide * scale * attn_gain_ref[...].reshape(1, width)).astype(jnp.bfloat16)
    grad_out[place] = grad_ref[...]
    pl.semaphore_wait(barrier, n_t - 1)

    rows_gather = LineGather(rows_out, rows_send, rows_recv, place)
    grad_gather = LineGather(grad_out, grad_send, grad_recv, place, GRAD_PIECES)
    moe_gather = LineGather(moe_out, moe_send, moe_recv, place, PIECES)
    line = LineScatter(part, arrived, line_send, line_recv, place, PIECES)
    rows_gather.start()

    columns = heads * HD
    twice = select_lanes(columns, heads * 128, lambda c: c // 128 * HD + c % HD)
    swapped = select_lanes(
        columns,
        heads * 128,
        lambda c: c // 128 * HD + (c % HD + c % 128 // HD * (HD // 2)) % HD,
    )
    for n, (ref, lanes) in enumerate(
        ((q_w_ref, swapped), (k_w_ref, swapped), (v_w_ref, twice))
    ):
        weights[n * heads * 128 : (n + 1) * heads * 128, :] = dot_tn(lanes, ref[...]).astype(
            jnp.bfloat16
        )
    for n, ref in enumerate((q_w_ref, k_w_ref, v_w_ref)):
        qkv_out[n * columns : (n + 1) * columns, :] = ref[...]
    qkv_out[3 * columns :, :] = jnp.zeros(
        (qkv_out.shape[0] - 3 * columns, width), jnp.bfloat16
    )
    double_out[...] = dot_tn(twice, out_w_ref[...]).astype(jnp.bfloat16)

    def project(block):
        at = pl.ds(pl.multiple_of(block * local, local), local)
        product = dot_nt(rows_out[block], weights[...])
        cosine, sine = cos_ref[at, :], sin_ref[at, :]
        for n, target in enumerate((q_out, k_out, v_out)):
            for h in range(heads):
                start = (n * heads + h) * 128
                piece = product[:, start : start + 128]
                if n < 2:
                    piece = piece * cosine + pltpu.roll(piece, 64, 1) * sine
                target[h, at, :] = piece.astype(jnp.bfloat16)

    def arrive(distance, _):
        @pl.when(distance > 0)
        def _():
            rows_gather.step(distance)

        def side(way, _):
            block = place + (2 * way - 1) * distance

            @pl.when((block >= 0) & (block < n_t) & ((distance > 0) | (way == 0)))
            def _():
                project(block)

            return 0

        lax.fori_loop(0, 2, side, 0)
        return 0

    lax.fori_loop(0, n_t, arrive, 0)
    grad_gather.start()

    factor = 0.5 * HD ** (-0.5)

    lse_out[...] = jnp.zeros_like(lse_out)

    def attend(block):
        at = slice(block * local, (block + 1) * local)
        seen = (block + 1) * local
        mixed = []
        for h in range(heads):
            scores = dot_nt(q_out[h, at, :], k_out[h, 0:seen, :]) * factor
            top = jnp.max(scores, axis=1, keepdims=True)
            exps = jnp.exp(scores - top)
            total = jnp.sum(exps, axis=1, keepdims=True)
            probs = (exps / total).astype(jnp.bfloat16)
            out = dot(probs, v_out[h, 0:seen, :]).astype(jnp.bfloat16)
            o_out[h, at, :] = out
            mixed.append(out)
            log_total = jnp.broadcast_to(top + jnp.log(total), (local, 128))
            lse_out[h : h + 1, at] = log_total.T[0:1, :]
        mixed = jnp.concatenate(mixed, axis=1)
        part[block] = (0.5 * dot(mixed, double_out[...])).astype(jnp.bfloat16)

    for block in range(n_t):
        attend(block)
    ends_first = (n_t - 1, 0, *range(n_t - 2, 0, -1))
    line.originate(ends_first, (0,))
    stores = [
        pltpu.make_async_copy(source, target, store_sem.at[n])
        for n, (source, target) in enumerate(zip(held, stored))
    ]
    for store in stores:
        store.start()
    lag = n_t - 2
    for turn in range(PIECES + lag + n_t - 1):
        line.forward(turn, ends_first)
        if turn + 1 < PIECES:
            line.drain(ends_first, turn)
            line.originate(ends_first, (turn + 1,))
        if 0 <= turn - lag < PIECES:
            n = turn - lag
            line.collect(acc, n)
            at = slice(n * (local // PIECES), (n + 1) * (local // PIECES))
            hidden = input_ref[at, :].astype(jnp.float32) + acc[at, :]
            hidden_out[at, :] = hidden
            scale = lax.rsqrt(jnp.mean(hidden * hidden, axis=1, keepdims=True) + EPSILON)
            moe_out[place, at, :] = (hidden * scale * moe_gain_ref[...].reshape(1, width)).astype(jnp.bfloat16)
            moe_gather.start(n)
        for step in range(1, n_t):
            if 0 <= turn - lag - step < PIECES:
                moe_gather.step(step, turn - lag - step)
        if turn % 2 == 0 and turn // 2 + 1 < n_t:
            grad_gather.step(turn // 2 + 1)
    for exchange in (rows_gather, moe_gather, line):
        exchange.finish()
    grad_gather.finish((0,))
    for store in stores:
        store.wait()


def forward(n_t, layer_input, attn_gain, moe_gain, q_w, k_w, v_w, out_w, grad_out, cosine, sine):
    local, width = layer_input.shape
    group = local * n_t
    heads = q_w.shape[0] // HD
    bf, f32 = jnp.bfloat16, jnp.float32
    dma = pltpu.SemaphoreType.DMA
    vmem = pl.BlockSpec(memory_space=pltpu.VMEM)
    blocks = (n_t, local, width)
    qkv_width = -(-3 * heads * HD // 128) * 128
    stored = (
        *[jax.ShapeDtypeStruct((heads, group, 128), bf)] * 4,
        jax.ShapeDtypeStruct(blocks, bf),
        jax.ShapeDtypeStruct((qkv_width, width), bf),
        jax.ShapeDtypeStruct((heads * 128, width), bf),
    )
    outs = (
        *stored,
        *[jax.ShapeDtypeStruct(blocks, bf)] * 2,
        jax.ShapeDtypeStruct((local, width), f32),
        jax.ShapeDtypeStruct((8, group), f32),
    )
    return pl.pallas_call(
        functools.partial(forward_kernel, n_t),
        out_shape=outs,
        in_specs=[vmem] * 10,
        out_specs=(*[pl.BlockSpec(memory_space=pl.ANY)] * len(stored), *[vmem] * 4),
        scratch_shapes=[
            *[pltpu.VMEM(a.shape, a.dtype) for a in stored],
            dma((len(stored),)),
            pltpu.VMEM((3 * heads * 128, width), bf),
            pltpu.VMEM(blocks, bf),
            pltpu.VMEM((n_t + 1, local, width), bf),
            pltpu.VMEM((local, width), f32),
            *[s for n in (1, GRAD_PIECES, PIECES) for s in (dma((2, n_t, n)), dma((n_t, n)))],
            dma((2, n_t, PIECES)),
            dma((2, n_t, PIECES)),
        ],
        compiler_params=pltpu.CompilerParams(
            collective_id=2, has_side_effects=True, vmem_limit_bytes=56 << 20
        ),
        name="forward",
    )(layer_input, attn_gain, moe_gain, q_w, k_w, v_w, out_w, grad_out, cosine, sine)


def expert_kernel(
    sizes,
    moe_ref,
    half_ref,
    grad_ref,
    routes_ref,
    residual_ref,
    router_ref,
    gate_ref,
    up_ref,
    down_ref,
    back_ref,
    sum_ref,
    chosen_ref,
    *rest,
):
    n_dp, n_t, ffn_count, route_count, inside = sizes
    weight_outs = rest[: 2 if inside else 1]
    (
        probs_s,
        rank_s,
        router_s,
        hit_s,
        turned_s,
        slot_s,
        rows_s,
        gate_s,
        up_s,
        active_s,
        out_s,
        grad_s,
        part_s,
        arrived_s,
        acc,
        weight_s,
        grad_send,
        grad_recv,
        half_sem,
        line_send,
        line_recv,
        own_sem,
        *paired,
    ) = rest[2 if inside else 1 :]
    turn = pl.program_id(0)
    expert = turn % ffn_count
    slot = turn % 2
    dp = lax.axis_index("dp")
    place = lax.axis_index("tensor")
    local, width = grad_ref.shape
    rows = n_t * local
    hidden = gate_ref.shape[2]
    step = width // n_dp
    grad_rows = local // GRAD_PIECES
    gather = LineGather(grad_s, grad_send, grad_recv, place, GRAD_PIECES)
    line = LineScatter(part_s, arrived_s, line_send, line_recv, place, SUM_PIECES)
    blocks = tuple(range(n_t))
    ends_first = (n_t - 1, 0, *range(n_t - 2, 0, -1))

    def line_turn(n):
        line.forward(n, ends_first)
        if n + 1 < SUM_PIECES:
            line.drain(ends_first, n)
            line.originate(ends_first, (n + 1,))

    def half_copy(block):
        return pltpu.make_async_copy(
            half_ref.at[block, pl.ds(0, grad_rows)],
            grad_s.at[block, pl.ds(0, grad_rows)],
            half_sem.at[block],
        )

    early = min(EARLY, ffn_count)
    core = bit_of(dp, 0)
    if inside:
        pair_s, pair_send, pair_recv, stage_send, stage_recv = paired
        splits = ((0, 3 * hidden // 2), (3 * hidden // 2, 3 * hidden // 2))
        sems = (None, None, None, [stage_send], [stage_recv])
        halving = Halving(
            None, pair_s, None, [weight_outs[1]], sems, dp, log2_of(n_dp), splits
        )

    def own_copy(e, at):
        return pltpu.make_async_copy(
            pair_s.at[e] if inside else weight_s.at[at], weight_outs[0].at[e], own_sem.at[e]
        )

    def pair_copy(e, at):
        return pltpu.make_async_remote_copy(
            src_ref=weight_s.at[at, 1 - core],
            dst_ref=pair_s.at[e],
            send_sem=pair_send.at[e],
            recv_sem=pair_recv.at[e],
            device_id={"dp": flipped(dp, 0)},
            device_id_type=MESH,
        )

    def left(e, at):
        if inside:
            pair_copy(e, at).wait_send()
        else:
            own_copy(e, at).wait()

    def settle(e, at):
        pair_copy(e, at).wait_recv()
        for block in range(n_dp // 2):
            halving.add_rows(pair_s.at[e, block], weight_s.at[at, core, block])
        own_copy(e, at).start()

        @pl.when(e < early)
        def _():
            halving.send_stage(e, 0)

    def combine(block):
        at = slice(block * local, (block + 1) * local)
        out = out_s[...].reshape(ffn_count * CAP, width)
        return dot(turned_s[at, :], out).astype(jnp.bfloat16)

    @pl.when(turn == 0)
    def _():
        for block in blocks:
            half_copy(block).start()
        grad_s[place, grad_rows:, :] = grad_ref[grad_rows:, :]
        greet((("tensor", place, n_t), ("dp", dp, n_dp)))
        gather.start(1)
        router_s[...] = jnp.zeros_like(router_s)
        router_s[0:route_count, :] = router_ref[...]
        parts = three_parts(router_s[...])
        logits = jnp.concatenate(
            [residual_ref[...], jnp.zeros((EXP_PAD - route_count, rows), jnp.float32)], axis=0
        )
        moe = moe_ref[...].reshape(rows, width)
        for part in parts:
            logits = logits + dot_nt(part, moe)
        index = lax.broadcasted_iota(jnp.int32, (EXP_PAD, rows), 0)
        logits = jnp.where(index < route_count, logits, MASKED)
        top = jnp.max(logits, axis=0, keepdims=True)
        exps = jnp.exp(logits - top)
        probs_s[...] = exps / jnp.sum(exps, axis=0, keepdims=True)
        named = (routes_ref[0:1, :] == index) | (routes_ref[1:2, :] == index)
        named = jnp.where(named, 1.0, 0.0)
        before = lax.broadcasted_iota(jnp.int32, (256, 256), 0)
        after = lax.broadcasted_iota(jnp.int32, (256, 256), 1)
        earlier = jnp.where(before < after, 1.0, 0.0).astype(jnp.bfloat16)
        total = jnp.zeros((EXP_PAD, 1), jnp.float32)
        for start in range(0, rows, 256):
            block = named[:, start : start + 256]
            rank = dot(block.astype(jnp.bfloat16), earlier) + total
            rank_s[:, start : start + 256] = jnp.where(block > 0.5, rank, -1.0)
            total = total + jnp.sum(block, axis=1, keepdims=True)

    @pl.when(turn < ffn_count)
    def _():
        place_in = lax.broadcasted_iota(jnp.int32, (CAP, rows), 0).astype(jnp.float32)
        hit = rank_s[pl.ds(expert, 1), :] == place_in
        slot_weight = jnp.sum(
            jnp.where(hit, probs_s[pl.ds(expert, 1), :], 0.0), axis=1, keepdims=True
        )
        slot_s[expert] = slot_weight
        dispatch = jnp.where(hit, 1.0, 0.0).astype(jnp.bfloat16)
        hit_s[expert] = dispatch
        turned_s[:, pl.ds(pl.multiple_of(expert * CAP, CAP), CAP)] = dispatch.T
        rows_in = dot(dispatch, moe_ref[...].reshape(rows, width)).astype(jnp.bfloat16)
        rows_s[expert] = rows_in
        gate_pre = dot(rows_in, gate_ref[0])
        up_pre = dot(rows_in, up_ref[0])
        sigmoid = 1.0 / (1.0 + jnp.exp(-gate_pre))
        silu = gate_pre * sigmoid
        active = (silu * up_pre).astype(jnp.bfloat16)
        active_s[expert] = active
        gate_s[expert] = up_pre * (sigmoid + silu * (1.0 - sigmoid))
        up_s[expert] = silu
        out_s[expert] = (dot(active, down_ref[0]) * slot_weight).astype(jnp.bfloat16)
        for distance in range(1, n_t - 1):

            @pl.when(turn == 3 * distance - 2)
            def _(distance=distance):
                gather.step(distance, 1)

    @pl.when(turn == ffn_count)
    def _():
        for block in blocks:
            part_s[block] = combine(block)
            half_copy(block).wait()
        line.originate(ends_first, (0,))
        gather.step(n_t - 1, 1)

    @pl.when(turn >= ffn_count)
    def _():
        active = active_s[expert]
        rows_grad = dot(hit_s[expert], grad_s[...].reshape(rows, width))
        low = rows_grad.astype(jnp.bfloat16)
        grad_active = dot_nt(low, down_ref[0])
        slot_weight = slot_s[expert]
        inner = jnp.sum(grad_active * active.astype(jnp.float32), axis=1, keepdims=True)
        lane = lax.broadcasted_iota(jnp.int32, (CAP, 128), 1)
        inner_parts = jnp.zeros((CAP, 128), jnp.float32)
        for n, inner_part in enumerate(three_parts(inner)):
            inner_parts = jnp.where(lane == n, inner_part.astype(jnp.float32), inner_parts)
        chosen_rows = dot_tn(inner_parts.astype(jnp.bfloat16), hit_s[expert])
        chosen_row = chosen_rows[0:1] + chosen_rows[1:2] + chosen_rows[2:3]
        for n in blocks:
            chosen_ref[n, pl.ds(expert, 1), :] = chosen_row[:, n * local : (n + 1) * local]
        grad_low = (rows_grad * slot_weight).astype(jnp.bfloat16)
        grad_active = grad_active * slot_weight
        grad_gate = (grad_active * gate_s[expert]).astype(jnp.bfloat16)
        grad_up = (grad_active * up_s[expert]).astype(jnp.bfloat16)
        out_s[expert] = (dot_nt(grad_gate, gate_ref[0]) + dot_nt(grad_up, up_ref[0])).astype(
            jnp.bfloat16
        )

        @pl.when(expert >= 2)
        def _():
            left(expert - 2, slot)

        rows_in = rows_s[expert]
        for n, (one, other) in enumerate(
            ((rows_in, grad_gate), (rows_in, grad_up), (grad_low, active))
        ):
            product = dot_tn(one, other).astype(jnp.bfloat16)
            for d in range(n_dp):
                weight_s[slot, d % 2, d // 2, :, n * hidden : (n + 1) * hidden] = product[
                    d * step : (d + 1) * step
                ]
        if inside:
            pair_copy(expert, slot).start()

            @pl.when(expert >= 1)
            def _():
                settle(expert - 1, 1 - slot)

        else:
            own_copy(expert, slot).start()
        for n, at in enumerate(LINE_TURNS):

            @pl.when(expert == at)
            def _(n=n):
                line_turn(n)

    @pl.when(turn == 2 * ffn_count - 1)
    def _():
        for block in blocks:
            back_ref[block] = combine(block)
        if inside:
            settle(ffn_count - 1, (ffn_count - 1) % 2)
        for e in range(ffn_count - 2, ffn_count):
            left(e, e % 2)
        for n in range(len(LINE_TURNS), SUM_PIECES + n_t - 3):
            line_turn(n)
        for n in range(SUM_PIECES):
            line.collect(acc, n)
        sum_ref[...] = acc[...]
        line.finish()
        gather.finish((1,))
        if inside:
            for e in range(ffn_count):
                own_copy(e, e % 2).wait()
            for e in range(early):
                for k in range(halving.number(0)):
                    for part in (0, 1):
                        halving.stage_copy(e, part, 0, k).wait()


def experts(n_dp, n_t, moe_rows, grad_half, grad_out, routes_t, residual_t, router_t, gate_w, up_w, down_w):
    _, local, width = moe_rows.shape
    rows = n_t * local
    route_count = router_t.shape[0]
    ffn_count, _, hidden = gate_w.shape
    step = width // n_dp
    half = n_dp // 2
    inside = reduced_inside(step)
    bf, f32 = jnp.bfloat16, jnp.float32
    dma = pltpu.SemaphoreType.DMA

    def whole(shape):
        return pl.BlockSpec(shape, lambda s: (0,) * len(shape), pipeline_mode=pl.Buffered(1))

    any_space = pl.BlockSpec(memory_space=pl.ANY)
    item = (half, step, 3 * hidden)
    weights = (
        [
            jax.ShapeDtypeStruct((ffn_count, *item), bf),
            jax.ShapeDtypeStruct((min(EARLY, ffn_count), half // 2, *item[1:]), bf),
        ]
        if inside
        else [jax.ShapeDtypeStruct((ffn_count, 2, *item), bf)]
    )
    paired = []
    if inside:
        stage = dma((min(EARLY, ffn_count), 2, half // 2))
        paired = [pltpu.VMEM((ffn_count, *item), bf), dma((ffn_count,)), dma((ffn_count,)), stage, stage]
    blocks = (n_t, local, width)
    return pl.pallas_call(
        functools.partial(expert_kernel, (n_dp, n_t, ffn_count, route_count, inside)),
        grid=(2 * ffn_count,),
        out_shape=(
            jax.ShapeDtypeStruct(blocks, bf),
            jax.ShapeDtypeStruct((local, width), f32),
            jax.ShapeDtypeStruct((n_t, ffn_count, local), f32),
            *weights,
        ),
        in_specs=[
            whole(blocks),
            any_space,
            whole((local, width)),
            whole((2, rows)),
            whole((route_count, rows)),
            whole((route_count, width)),
            pl.BlockSpec((1, width, hidden), lambda s: (s % ffn_count, 0, 0)),
            pl.BlockSpec((1, width, hidden), lambda s: (s % ffn_count, 0, 0)),
            pl.BlockSpec((1, hidden, width), lambda s: (s % ffn_count, 0, 0)),
        ],
        out_specs=(
            whole(blocks),
            whole((local, width)),
            whole((n_t, ffn_count, local)),
            *[any_space for _ in weights],
        ),
        scratch_shapes=[
            pltpu.VMEM((EXP_PAD, rows), f32),
            pltpu.VMEM((EXP_PAD, rows), f32),
            pltpu.VMEM((EXP_PAD, width), f32),
            pltpu.VMEM((ffn_count, CAP, rows), bf),
            pltpu.VMEM((rows, ffn_count * CAP), bf),
            pltpu.VMEM((ffn_count, CAP, 1), f32),
            pltpu.VMEM((ffn_count, CAP, width), bf),
            pltpu.VMEM((ffn_count, CAP, hidden), f32),
            pltpu.VMEM((ffn_count, CAP, hidden), f32),
            pltpu.VMEM((ffn_count, CAP, hidden), bf),
            pltpu.VMEM((ffn_count, CAP, width), bf),
            pltpu.VMEM(blocks, bf),
            pltpu.VMEM(blocks, bf),
            pltpu.VMEM((n_t + 1, local, width), bf),
            pltpu.VMEM((local, width), f32),
            pltpu.VMEM((2, 2, *item), bf),
            dma((2, n_t, GRAD_PIECES)),
            dma((n_t, GRAD_PIECES)),
            dma((n_t,)),
            dma((2, n_t, SUM_PIECES)),
            dma((2, n_t, SUM_PIECES)),
            dma((ffn_count,)),
            *paired,
        ],
        compiler_params=pltpu.CompilerParams(
            dimension_semantics=("arbitrary",),
            collective_id=3,
            has_side_effects=True,
            vmem_limit_bytes=62 << 20,
        ),
        name="experts",
    )(moe_rows, grad_half, grad_out, routes_t, residual_t, router_t, gate_w, up_w, down_w)


def side_forward(norm, named, residual, weight_parts, const_value, route_count, ffn_count):
    lane = lax.broadcasted_iota(jnp.int32, named.shape, 1)
    low = norm.astype(jnp.bfloat16)
    both = sum(dot_nt(low, part) for part in weight_parts)
    logits = jnp.where(lane < route_count, both + residual, MASKED)
    exps = jnp.exp(logits - jnp.max(logits, axis=1, keepdims=True))
    probs = exps / jnp.sum(exps, axis=1, keepdims=True)
    chosen = probs * named
    shares, keeps, rests = [], chosen[:, ffn_count + 1 : ffn_count + 2], []
    for c in range(2):
        at = route_count + 2 * c
        share = 1.0 / (1.0 + jnp.exp(both[:, at + 1 : at + 2] - both[:, at : at + 1]))
        weight = chosen[:, ffn_count + 2 + c : ffn_count + 3 + c]
        shares.append(share)
        keeps = keeps + weight * share
        rests.append(weight * (1.0 - share))
    special = keeps * norm + rests[0] * const_value[0:1] + rests[1] * const_value[1:2]
    return probs, chosen, shares, keeps, rests, special


def side_backward(
    norm, grad, named, forward, chosen_back, weight_parts, const_value, route_count, ffn_count
):
    probs, chosen, shares, keeps, rests, _ = forward
    lane = lax.broadcasted_iota(jnp.int32, named.shape, 1)
    self_dot = jnp.sum(grad * norm, axis=1, keepdims=True)
    value_dots = [
        jnp.sum(grad * const_value[c : c + 1], axis=1, keepdims=True) for c in range(2)
    ]
    d_probs = jnp.where(lane < ffn_count, chosen_back, 0.0)
    d_probs = jnp.where(lane == ffn_count + 1, self_dot, d_probs)
    for c in range(2):
        mixed = shares[c] * self_dot + (1.0 - shares[c]) * value_dots[c]
        d_probs = jnp.where(lane == ffn_count + 2 + c, mixed, d_probs)
    d_probs = d_probs * named
    d_both = probs * (d_probs - jnp.sum(probs * d_probs, axis=1, keepdims=True))
    d_both = jnp.where(lane < route_count, d_both, 0.0)
    for c in range(2):
        weight = chosen[:, ffn_count + 2 + c : ffn_count + 3 + c]
        d_share = shares[c] * (1.0 - shares[c]) * weight * (self_dot - value_dots[c])
        d_both = jnp.where(lane == route_count + 2 * c, d_share, d_both)
        d_both = jnp.where(lane == route_count + 2 * c + 1, -d_share, d_both)
    d_parts = three_parts(d_both)
    back = keeps * grad
    for m, n in ((0, 0), (0, 1), (1, 0), (1, 1)):
        back = back + dot(d_parts[m], weight_parts[n])
    low = norm.astype(jnp.bfloat16)
    weight_part = dot_tn(d_parts[0], low) + dot_tn(d_parts[1], low) + dot_tn(d_parts[2], low)
    value_part = [jnp.sum(rests[c] * grad, axis=0, keepdims=True) for c in range(2)]
    return back, weight_part, value_part


LATE = 9


def backward_kernel(
    sizes,
    sum_ref,
    back_ref,
    chosen_ref,
    hidden_ref,
    moe_ref,
    grad_ref,
    input_ref,
    routes_ref,
    residual_ref,
    router_ref,
    gates_ref,
    value_ref,
    moe_gain_ref,
    attn_gain_ref,
    *rest,
):
    dp_bits, n_t, ffn_count, route_count, attn_split, inside = sizes
    stage_count = dp_bits - 1 if inside else 0
    late_refs, rest = rest[:LATE], rest[LATE:]
    expert_refs = rest[: 2 if inside else 0]
    rest = rest[2 if inside else 0 :]
    (
        output_ref,
        input_grad_ref,
        expert_out,
        attn_out,
        small_out,
        gain_out,
        chosen_in,
        pair_buf,
        line_back,
        staged,
        both_s,
        turned_s,
        grad_rows,
        attn_part,
        acc,
        hidden_grad,
        double_grad,
        delta,
        dq,
        dk,
        dv,
        packed,
    ) = rest[:22]
    loaded, rest = rest[22 : 22 + LATE], rest[22 + LATE :]
    q_ref, k_ref, v_ref, o_ref, lse_ref, rows_ref, qkv_ref, out_w_ref, table_ref = loaded
    if inside:
        attn_pairs, kept = rest[:2]
        stages = rest[2 : 2 + stage_count]
        rest = rest[2 + stage_count :]
        a_kept, a_first = rest[:2]
        a_stages = rest[2 : 2 + stage_count]
        rest = rest[2 + stage_count :]
    else:
        attn_pairs = attn_out
    smalls, small_dp, small_tensor, gains, gain_dp, gain_tensor, side_back = rest[:7]
    rest = list(rest[7:])

    def sems(count):
        taken = rest[:count]
        del rest[:count]
        return taken

    (chosen_send, chosen_recv, gather_send, gather_recv) = sems(4)
    line_sems = [sems(2) for _ in range(2)]
    if inside:
        e_sems = [None] + sems(2) + [sems(stage_count), sems(stage_count)]
        a_sems = sems(3) + [sems(stage_count), sems(stage_count)]
    small_sems = [sems(2), sems(2)]
    gain_sems = [sems(2), sems(2)]
    staged_sem, load_sem = sems(2)
    loads = [
        pltpu.make_async_copy(source, target, load_sem.at[n])
        for n, (source, target) in enumerate(zip(late_refs, loaded))
    ]
    for load in loads:
        load.start()

    dp = lax.axis_index("dp")
    place = lax.axis_index("tensor")
    local = hidden_ref.shape[0]
    width = hidden_ref.shape[1]
    hidden_units = expert_out.shape[-1]
    heads = q_ref.shape[0]
    greet((("dp", dp, 1 << dp_bits), ("tensor", place, n_t)))

    back_line = LineScatter(back_ref, line_back, *line_sems[0], place, PIECES)
    attn_line = LineScatter(attn_part, line_back, *line_sems[1], place, PIECES)
    gather = LineGather(grad_rows, gather_send, gather_recv, place, PIECES)
    half = hidden_units // 2
    attn_width = attn_pairs.shape[-1]
    expert = attn = Nothing()
    if inside:
        splits = ((0, half), (half, half))
        expert = LateHalving(expert_refs, kept, None, stages, e_sems, dp, dp_bits, splits)
        splits = ((0, attn_split), (attn_split, attn_width - attn_split))
        attn = Halving(attn_pairs, a_kept, a_first, a_stages, a_sems, dp, dp_bits, splits)
    everyone = (("dp", dp, 1 << dp_bits), ("tensor", place, n_t))
    small = Exchange(smalls, (small_dp, small_tensor), *small_sems, everyone)
    gain = Exchange(gains, (gain_dp, gain_tensor), *gain_sems, everyone)

    def chosen_copy(step):
        there = (place + step) % n_t
        return pltpu.make_async_remote_copy(
            src_ref=chosen_ref.at[there],
            dst_ref=chosen_in.at[step - 1],
            send_sem=chosen_send.at[step - 1],
            recv_sem=chosen_recv.at[step - 1],
            device_id={"tensor": there},
            device_id_type=MESH,
        )

    ends_first = (n_t - 1, 0, *range(n_t - 2, 0, -1))
    for step in range(1, n_t):
        chosen_copy(step).start()
    back_line.originate(ends_first, (0,))

    def over_experts(action):
        def body(e, _):
            action(e)
            return 0

        def run(first, last):
            lax.fori_loop(first, last, body, 0)

        return run

    early = min(EARLY, ffn_count)
    expert.begin(early, ffn_count)

    norm = moe_ref[place].astype(jnp.float32)
    lane = lax.broadcasted_iota(jnp.int32, (local, 128), 1)
    mine = pl.ds(pl.multiple_of(place * local, local), local)
    turned_s[...] = jnp.zeros_like(turned_s)
    turned_s[0:route_count, :] = residual_ref[:, mine]
    turned_s[16:18, :] = routes_ref[:, mine].astype(jnp.float32)
    turned = turned_s[...].T
    residual = turned
    kind = lane.astype(jnp.float32)
    named = jnp.where((turned[:, 16:17] == kind) | (turned[:, 17:18] == kind), 1.0, 0.0)
    both_s[...] = jnp.zeros_like(both_s)
    both_s[0:route_count, :] = router_ref[...]
    for c in range(2):
        both_s[route_count + 2 * c : route_count + 2 * c + 2, :] = gates_ref[c]
    weight_parts = three_parts(both_s[...])
    const_value = value_ref[...]
    grad = grad_ref[...].astype(jnp.float32)
    forward = side_forward(
        norm, named, residual, weight_parts, const_value, route_count, ffn_count
    )
    pair_buf[...] = hidden_ref[...] + forward[-1]
    chosen_total = chosen_ref[place]
    for step in range(1, n_t):
        chosen_copy(step).wait_recv()
        chosen_total = chosen_total + chosen_in[step - 1]
    chosen_back = jnp.concatenate(
        [chosen_total, jnp.zeros((128 - ffn_count, local), jnp.float32)], axis=0
    ).T
    back, weight_part, value_part = side_backward(
        norm, grad, named, forward, chosen_back, weight_parts, const_value, route_count, ffn_count
    )
    side_back[...] = back
    smalls[0, 1:2, :] = value_part[0]
    smalls[0, 2:3, :] = value_part[1]
    smalls[0, 3:8, :] = jnp.zeros((5, width), jnp.float32)
    smalls[0, 8:24, :] = weight_part[0:16]

    opening = -(-ffn_count // PIECES)
    moe_gain_total = jnp.zeros((1, width), jnp.float32)
    lag = n_t - 2
    for turn in range(PIECES + lag + n_t - 1):
        back_line.forward(turn, ends_first)
        if turn + 1 < PIECES:
            back_line.drain(ends_first, turn)
            back_line.originate(ends_first, (turn + 1,))
        for e in range(turn * opening, min((turn + 1) * opening, ffn_count)):
            expert.open(e, early)
        if 0 <= turn - lag < PIECES:
            n = turn - lag
            at = slice(n * (local // PIECES), (n + 1) * (local // PIECES))
            back_line.collect(acc, n)
            norm_grad = acc[at, :] + side_back[at, :]
            hidden = hidden_ref[at, :]
            scale = lax.rsqrt(jnp.mean(hidden * hidden, axis=1, keepdims=True) + EPSILON)
            u = norm_grad * moe_gain_ref[...].reshape(1, width)
            moe_gain_total = moe_gain_total + jnp.sum(
                norm_grad * hidden * scale, axis=0, keepdims=True
            )
            hidden_grad[at, :] = (
                grad_ref[at, :].astype(jnp.float32)
                + scale * u
                - hidden
                * (scale * scale * scale)
                * jnp.mean(u * hidden, axis=1, keepdims=True)
            )
            grad_rows[place, at, :] = hidden_grad[at, :].astype(jnp.bfloat16)
            if n == PIECES - 1:
                back_line.finish()
            gather.start(n)
        for step in range(1, n_t):
            if 0 <= turn - lag - step < PIECES:
                gather.step(step, turn - lag - step)
    smalls[0, 0:1, :] = moe_gain_total
    small.start(0)
    output_ref[...] = (pair_buf[...] + sum_ref[...]).astype(output_ref.dtype)
    advance = over_experts(lambda e: expert.advance(e, 0))

    for load in loads:
        load.wait()
    rows = local

    def row_block(n):
        return pl.ds(pl.multiple_of(n * rows, rows), rows)

    count = n_t
    head_lane = lax.broadcasted_iota(jnp.int32, (rows, 128), 1)
    low_half = head_lane < 64
    for block in range(count):
        at = pl.ds(block * rows, rows)
        product = dot_nt(grad_rows[block], out_w_ref[...])
        for h in range(heads):
            piece = product[:, h * 128 : (h + 1) * 128].astype(jnp.bfloat16)
            double_grad[h, at, :] = piece
            both = piece.astype(jnp.float32) * o_ref[h, at, :].astype(jnp.float32)
            delta[h : h + 1, at] = 0.5 * jnp.sum(both.T, axis=0, keepdims=True)
    out_pack = []
    for h in range(0, heads, 2):
        o_a = o_ref[h]
        o_b = o_ref[h + 1] if h + 1 < heads else jnp.zeros_like(o_a)
        lanes = lax.broadcasted_iota(jnp.int32, o_a.shape, 1)
        out_pack.append(jnp.where(lanes < 64, o_a, o_b))
    n_half = attn_pairs.shape[2]
    step_rows = attn_pairs.shape[3]
    qkv_width = packed.shape[1]

    def spread(product, start, stop):
        low = product.astype(jnp.bfloat16)
        for d in range(2 * n_half):
            attn_pairs[0, d % 2, d // 2, :, start:stop] = low[d * step_rows : (d + 1) * step_rows]

    for n, pack in enumerate(out_pack):
        total = jnp.zeros((width, 128), jnp.float32)
        for block in range(count):
            total = total + dot_tn(grad_rows[block], pack[block * rows : (block + 1) * rows])
        spread(total, qkv_width + n * 128, qkv_width + (n + 1) * 128)

    dq[...] = jnp.zeros_like(dq)
    factor = 64 ** (-0.5)
    gain_total = jnp.zeros((1, width), jnp.float32)
    for turn, key_block in enumerate(range(count)):
        keys = pl.ds(key_block * rows, rows)
        dk[...] = jnp.zeros_like(dk)
        dv[...] = jnp.zeros_like(dv)

        def query_step(query_block, _, keys=keys):
            at = row_block(query_block)
            for h in range(heads):
                q, g = q_ref[h, at, :], double_grad[h, at, :]
                k, v = k_ref[h, keys, :], v_ref[h, keys, :]
                scores = dot_nt(k, q) * (0.5 * factor)
                probs = jnp.exp(scores - lse_ref[h : h + 1, at])
                d_probs = dot_nt(v, g) * 0.5
                d_scores = (probs * (d_probs - delta[h : h + 1, at])).astype(jnp.bfloat16)
                dk[h] += dot(d_scores, q)
                dv[h] += dot(probs.astype(jnp.bfloat16), g)
                dq[h, at, :] += dot_tn(d_scores, k)
            return 0

        lax.fori_loop(key_block, count, query_step, 0)
        table = table_ref[keys, :]
        pieces = []
        for source in (dq.at[:, keys, :], dk):
            for h in range(heads):
                turned = source[h] * (table * factor)
                pieces.append(turned + pltpu.roll(turned, 64, 1))
        for h in range(heads):
            pieces.append(dv[h])
        if len(pieces) % 2:
            pieces.append(jnp.zeros((rows, 128), jnp.float32))
        for n in range(0, len(pieces), 2):
            packed[keys, n * 64 : n * 64 + 128] = jnp.where(
                low_half, pieces[n], pieces[n + 1]
            ).astype(jnp.bfloat16)
        back_rows = dot(packed[keys, :], qkv_ref[...])
        gain_total = gain_total + jnp.sum(
            back_rows * rows_ref[key_block].astype(jnp.float32), axis=0, keepdims=True
        )
        attn_part[key_block] = back_rows.astype(jnp.bfloat16)
        attn_line.originate((key_block,))
        if turn > 0:
            attn_line.forward_all(key_block - 1)
        if turn == 0:
            advance(early, ffn_count)
        if turn == 1:
            small.take(0)
            small.start(1)

    gains[0] = gain_total / attn_gain_ref[...].reshape(1, width)
    gain.start(0)
    for n in range(qkv_width // 128):
        total = jnp.zeros((width, 128), jnp.float32)
        for block in range(count):
            total = total + dot_tn(
                rows_ref[block], packed[pl.ds(block * rows, rows), n * 128 : (n + 1) * 128]
            )
        spread(total, n * 128, (n + 1) * 128)
    attn.start(0)
    attn_line.forward_all(count - 1)
    gain.take(0)
    gain.start(1)
    attn.open(0)
    for stage in range(1, stage_count - 1):
        over_experts(lambda e, stage=stage: expert.advance(e, stage))(0, ffn_count)
    small.take(1)
    small_out[...] = smalls[2]
    for stage in range(stage_count - 1):
        attn.advance(0, stage)
    gain.take(1)
    gain_out[...] = jnp.broadcast_to(gains[2], gain_out.shape)
    for n in range(PIECES):
        attn_line.collect(acc, n)
    wide = input_ref[...].astype(jnp.float32)
    scale = lax.rsqrt(jnp.mean(wide * wide, axis=1, keepdims=True) + EPSILON)
    w = acc[...] * attn_gain_ref[...].reshape(1, width)
    input_grad_ref[...] = (
        hidden_grad[...]
        + scale * w
        - wide * (scale * scale * scale) * jnp.mean(w * wide, axis=1, keepdims=True)
    ).astype(input_grad_ref.dtype)
    def stored(e):
        return pltpu.make_async_copy(staged.at[e % 2], expert_out.at[e], staged_sem.at[e])

    for e in range(ffn_count if inside else 0):
        if e > 1:
            stored(e - 2).wait()
        expert.close(e, staged.at[e % 2])
        stored(e).start()
    attn.close(0, attn_out)

    attn_line.finish()
    for step in range(1, n_t):
        chosen_copy(step).wait_send()
    gather.finish()

    for e in range(ffn_count):
        expert.finish(e, early)
    attn.finish(0)
    for e in range(ffn_count - 2, ffn_count if inside else 0):
        stored(e).wait()


def backward(dp_count, n_t, ffn_sum, ffn_back, chosen, weight_pairs, hidden, moe_rows, grad_out,
             layer_input, routes, residual, router, gates, const_value, moe_gain, attn_gain,
             q2, k2, v2, o2, lse, attn_rows, qkv_weight, out_double, table):
    late = (q2, k2, v2, o2, lse, attn_rows, qkv_weight, out_double, table)
    local, width = hidden.shape
    group = local * n_t
    ffn_count = weight_pairs[0].shape[0]
    units = weight_pairs[0].shape[-1]
    step = width // dp_count
    half = dp_count // 2
    dp_bits = log2_of(dp_count)
    inside = reduced_inside(step)
    stage_count = dp_bits - 1 if inside else 0
    heads = q2.shape[0]
    qkv_width = qkv_weight.shape[0]
    attn_width = qkv_width + -(-heads // 2) * 128
    attn_split = attn_width // 2 // 128 * 128
    bf, f32 = jnp.bfloat16, jnp.float32
    dma = pltpu.SemaphoreType.DMA

    def numbers(stage):
        return half >> (stage + 1)

    def line(rows_shape):
        return pltpu.VMEM((n_t + 1, *rows_shape[1:]), bf)

    block_shape = (n_t, local, width)
    reduction = []
    if inside:
        reduction = [
            pltpu.VMEM((1, 2, half, step, attn_width), bf),
            pltpu.VMEM((ffn_count, half, step, units), bf),
            *[pltpu.VMEM((ffn_count, numbers(s), step, units), bf) for s in range(stage_count)],
            pltpu.VMEM((1, half, step, attn_width), bf),
            pltpu.VMEM((1, half, step, attn_width), bf),
            *[pltpu.VMEM((1, numbers(s), step, attn_width), bf) for s in range(stage_count)],
        ]
    scratch = [
        pltpu.VMEM((n_t - 1, ffn_count, local), f32),
        pltpu.VMEM((local, width), f32),
        line(block_shape),
        pltpu.VMEM((2, step, units), f32),
        pltpu.VMEM((128, width), f32),
        pltpu.VMEM((128, local), f32),
        pltpu.VMEM(block_shape, bf),
        pltpu.VMEM(block_shape, bf),
        pltpu.VMEM((local, width), f32),
        pltpu.VMEM((local, width), f32),
        pltpu.VMEM((heads, group, 128), bf),
        pltpu.VMEM((8, group), f32),
        pltpu.VMEM((heads, group, 128), f32),
        pltpu.VMEM((heads, local, 128), f32),
        pltpu.VMEM((heads, local, 128), f32),
        pltpu.VMEM((group, qkv_width), bf),
        *[pltpu.VMEM(a.shape, a.dtype) for a in late],
        *reduction,
        pltpu.VMEM((3, 24, width), f32),
        pltpu.VMEM((dp_count - 1, 24, width), f32),
        pltpu.VMEM((n_t - 1, 24, width), f32),
        pltpu.VMEM((3, 1, width), f32),
        pltpu.VMEM((dp_count - 1, 1, width), f32),
        pltpu.VMEM((n_t - 1, 1, width), f32),
        pltpu.VMEM((local, width), f32),
        dma((n_t - 1,)),
        dma((n_t - 1,)),
        dma((2, n_t, PIECES)),
        dma((n_t, PIECES)),
        dma((2, n_t, PIECES)),
        dma((2, n_t, PIECES)),
        dma((2, n_t, PIECES)),
        dma((2, n_t, PIECES)),
        *[
            s
            for n in ((ffn_count, 1) if inside else ())
            for s in (
                *[dma((n,)) for _ in range(2 if n == ffn_count else 3)],
                *[dma((n, 2, numbers(s))) for s in range(stage_count)],
                *[dma((n, 2, numbers(s))) for s in range(stage_count)],
            )
        ],
        *[dma((n - 1,)) for _ in range(4) for n in (dp_count, n_t)],
        dma((ffn_count,)),
        dma((LATE,)),
    ]
    vmem = pl.BlockSpec(memory_space=pltpu.VMEM)
    operands = (ffn_sum, ffn_back, chosen, hidden, moe_rows, grad_out, layer_input, routes, residual,
                router, gates, const_value, moe_gain, attn_gain, *late)
    specs = [vmem] * (len(operands) - LATE) + [pl.BlockSpec(memory_space=pl.ANY)] * LATE
    if inside:
        operands = (*operands, *weight_pairs)
        specs += [pl.BlockSpec(memory_space=pl.ANY)] * 2
    return pl.pallas_call(
        functools.partial(
            backward_kernel, (dp_bits, n_t, ffn_count, residual.shape[0], attn_split, inside)
        ),
        out_shape=(
            jax.ShapeDtypeStruct((local, width), bf),
            jax.ShapeDtypeStruct((local, width), bf),
            jax.ShapeDtypeStruct((ffn_count, step, units) if inside else (8, 128), f32),
            jax.ShapeDtypeStruct((step, attn_width), f32)
            if inside
            else jax.ShapeDtypeStruct((1, 2, half, step, attn_width), bf),
            jax.ShapeDtypeStruct((24, width), f32),
            jax.ShapeDtypeStruct((8, width), f32),
        ),
        in_specs=specs,
        out_specs=(vmem, vmem, pl.BlockSpec(memory_space=pl.ANY), vmem, vmem, vmem),
        scratch_shapes=scratch,
        compiler_params=pltpu.CompilerParams(
            collective_id=1, has_side_effects=True, vmem_limit_bytes=62 << 20
        ),
        name="backward",
    )(*operands)


def rope_lanes(length, head_width):
    position = np.arange(length, dtype=np.float64)[:, None]
    inverse = np.exp(np.arange(head_width // 2) * (-2.0 * math.log(10000.0) / head_width))
    angle = position * inverse[None, :]
    c, s = np.cos(angle), np.sin(angle)
    cosine = np.concatenate([c, c, c, c], axis=1).astype(np.float32)
    sine = np.concatenate([-s, s, s, -s], axis=1).astype(np.float32)
    return cosine, sine


def tidy_kernel(
    wide, route_count, gate_ref, up_ref, down_ref, attn_ref, small_ref, gain_ref, output_ref, grad_ref, *outs
):
    (output, grad, attn_gain, q_out, k_out, v_out, out_out, moe_gain, router, gates, value) = outs[:11]
    for source, target in zip((gate_ref, up_ref, down_ref), outs[11:]):
        target[...] = source[...]

    @pl.when(pl.program_id(0) == 0)
    def _():
        output[...] = output_ref[...]
        grad[...] = grad_ref[...]
        attn_gain[...] = gain_ref[0, :]
        moe_gain[...] = small_ref[0, :]
        value[...] = small_ref[1:3, :]
        router[...] = small_ref[8 : 8 + route_count, :]
        for c in range(2):
            at = 8 + route_count + 2 * c
            gates[c] = small_ref[at : at + 2, :]
        for n, ref in enumerate((q_out, k_out, v_out)):
            ref[...] = attn_ref[:, n * wide : (n + 1) * wide]
        at = -(-3 * wide // 128) * 128
        out_out[...] = attn_ref[:, at : at + -(-wide // 128) * 128].T[0:wide, :]


def tidy(wide, route_count, expert_sum, attn_sum, small, gain, output, input_grad):
    count, step, units = expert_sum.shape
    units = units // 3
    width = small.shape[1]
    f32 = jnp.float32
    group = 4 if count % 4 == 0 else 1

    def whole(shape):
        return pl.BlockSpec(shape, lambda e: (0,) * len(shape), pipeline_mode=pl.Buffered(1))

    small_shapes = (
        (width,),
        (step, wide),
        (step, wide),
        (step, wide),
        (wide, step),
        (width,),
        (route_count, width),
        (2, 2, width),
        (2, width),
    )
    shapes = [output, input_grad]
    shapes += [jax.ShapeDtypeStruct(shape, f32) for shape in small_shapes]
    shapes += [jax.ShapeDtypeStruct((count, step, units), f32)] * 3
    piece = [
        pl.BlockSpec((group, step, units), lambda e, n=n: (e, 0, n)) for n in (0, 1, 2, 0, 0, 0)
    ]
    rest = (attn_sum, small, gain, output, input_grad)
    return pl.pallas_call(
        functools.partial(tidy_kernel, wide, route_count),
        grid=(count // group,),
        out_shape=tuple(jax.ShapeDtypeStruct(s.shape, s.dtype) for s in shapes),
        in_specs=[*piece[:3], *[whole(a.shape) for a in rest]],
        out_specs=(*[whole(s.shape) for s in shapes[:11]], *piece[3:]),
        compiler_params=pltpu.CompilerParams(
            dimension_semantics=("arbitrary",), vmem_limit_bytes=62 << 20
        ),
        name="tidy",
    )(expert_sum, expert_sum, expert_sum, *rest)


def on_device(
    layer_input,
    attn_gain,
    query_weight,
    key_weight,
    value_weight,
    out_weight,
    moe_gain,
    router_weight,
    gate_residual,
    const_gate,
    const_value,
    gate_weight,
    up_weight,
    down_weight,
    routes,
    grad_out,
):
    local_rows, model_width = layer_input.shape
    tensor_size = lax.axis_size("tensor")
    head_count = query_weight.shape[1] // HD
    ffn_count = gate_weight.shape[0]
    route_count = router_weight.shape[1]
    cosine, sine = rope_lanes(LENGTH, HD)
    q2, k2, v2, o2, attn_rows, qkv_weight, out_double, moe_rows, grad_half, hidden, lse = forward(
        tensor_size,
        layer_input,
        attn_gain,
        moe_gain,
        query_weight.T,
        key_weight.T,
        value_weight.T,
        out_weight,
        grad_out,
        jnp.asarray(cosine),
        jnp.asarray(sine),
    )
    n_dp = lax.axis_size("dp")
    ffn_back, ffn_sum, chosen_t, *weight_pairs = experts(
        n_dp,
        tensor_size,
        moe_rows,
        grad_half,
        grad_out,
        routes.T,
        gate_residual.T,
        router_weight.T,
        gate_weight,
        up_weight,
        down_weight,
    )
    output, input_grad, expert_sum, attn_sum_rows, small, gain = backward(
        n_dp,
        tensor_size,
        ffn_sum,
        ffn_back,
        chosen_t,
        weight_pairs,
        hidden,
        moe_rows,
        grad_out,
        layer_input,
        routes.T,
        gate_residual.T,
        router_weight.T,
        jnp.transpose(const_gate, (0, 2, 1)),
        const_value,
        moe_gain,
        attn_gain,
        q2,
        k2,
        v2,
        o2,
        lse,
        attn_rows,
        qkv_weight,
        out_double,
        jnp.asarray(np.concatenate([cosine[:, :HD], sine[:, HD:]], axis=1)),
    )
    if not reduced_inside(model_width // n_dp):

        def scattered(pairs):
            pairs = jnp.transpose(pairs, (2, 1, 3, 0, 4)).reshape(model_width, -1)
            return lax.psum_scatter(pairs, "dp", scatter_dimension=0, tiled=True).astype(
                jnp.float32
            )

        attn_sum_rows = scattered(attn_sum_rows)
        expert_sum = scattered(weight_pairs[0]).reshape(
            model_width // n_dp, ffn_count, weight_pairs[0].shape[-1]
        )
        expert_sum = jnp.transpose(expert_sum, (1, 0, 2))
    outs = list(
        tidy(
            head_count * HD, route_count, expert_sum, attn_sum_rows, small, gain, output, input_grad
        )
    )
    outs[8] = outs[8].T
    outs[9] = jnp.transpose(outs[9], (0, 2, 1))
    outs[13] = jnp.transpose(outs[13], (0, 2, 1))
    return tuple(outs)


def solution(mesh):
    in_specs = (
        P(("dp", "tensor"), None),
        P(),
        P(None, "tensor"),
        P(None, "tensor"),
        P(None, "tensor"),
        P("tensor", None),
        P(),
        P(),
        P("dp", None),
        P(),
        P(),
        P(None, None, "tensor"),
        P(None, None, "tensor"),
        P(None, "tensor", None),
        P("dp", None),
        P(("dp", "tensor"), None),
    )
    out_specs = (
        P(("dp", "tensor"), None),
        P(("dp", "tensor"), None),
        P(),
        P("dp", "tensor"),
        P("dp", "tensor"),
        P("dp", "tensor"),
        P("tensor", "dp"),
        P(),
        P(),
        P(),
        P(),
        P(None, "dp", "tensor"),
        P(None, "dp", "tensor"),
        P(None, "tensor", "dp"),
    )
    return jax.shard_map(
        on_device, mesh=mesh, in_specs=in_specs, out_specs=out_specs, check_vma=False
    )
```
